32 devices in a mesh: rows: 4 (over x, core), filt: 8 (over z, y).
Axes of the slice: x: 2, y: 2, z: 4, core: 2. Of those that a mesh axis runs over, the one named last changes fastest.
Arguments:
- inputs: bfloat16 [1024, 16, 512], P('filt', 'rows'), may hold values from -6 to 6
- filters: float32 [24, 1024], replicated, may hold values from -0.1875 to 0.1875
- gain_in: float32 [512], replicated, may hold values from 0.5 to 1.5
- mixing: bfloat16 [48, 512, 512], P('filt'), may hold values from -0.0390625 to 0.0390625
- regression: bfloat16 [3, 512, 512], replicated, may hold values from -0.15625 to 0.15625
- gain_mid: float32 [512], replicated, may hold values from 0.5 to 1.5
- w_gate: bfloat16 [512, 2048], P(None, 'filt'), may hold values from -0.25 to 0.25
- w_up: bfloat16 [512, 2048], P(None, 'filt'), may hold values from -0.25 to 0.25
- w_down: bfloat16 [2048, 512], P('filt'), may hold values from -0.1875 to 0.1875
- out_grad: bfloat16 [1024, 16, 512], P('filt', 'rows'), may hold values from -6 to 6
Outputs:
- block_out: bfloat16 [1024, 16, 512], P('filt', 'rows')
- input_grad: float32 [1024, 16, 512], P('filt', 'rows')
- mixing_grad: float32 [48, 512, 512], P('filt')
- regression_grad: float32 [3, 512, 512], replicated
- gain_in_grad: float32 [512], replicated
- gain_mid_grad: float32 [512], replicated
- w_gate_grad: float32 [512, 2048], P(None, 'filt')
- w_up_grad: float32 [512, 2048], P(None, 'filt')
- w_down_grad: float32 [2048, 512], P('filt')
The draws below stay inside these ranges and needn't reach their ends.
All inputs are finite; a program needn't handle non-finite values.
Results may differ from the reference program's by a relative error of at most 0.013.
Values may be sent and summed in bfloat16 or wider, within the bound.
No kernel may reach another device: no remote copies, remote signals or barrier semaphores. Data moves between devices by JAX's collectives and lax.ppermute only.
A program may use at most 256 MiB of HBM per device.

```python
import jax
import jax.numpy as jnp
from jax import lax

D = 512
FF = 2048
K = 24
ORDER = 3
SEQ_LEN = 1024
SEQS = 16


def block_levels(own_key, extent, pieces, smallest, high):
    def one(axis_at, shards_of):
        heights = jax.random.uniform(jax.random.fold_in(jax.random.fold_in(own_key, 6), axis_at), (shards_of,), jnp.float32, smallest / len(pieces), high / len(pieces))
        return jnp.repeat(jnp.exp(heights), extent[axis_at] // shards_of).reshape((-1,) + (1,) * (len(extent) - axis_at - 1))

    level = one(*pieces[0])
    for cut in pieces[1:]:
        level = level * one(*cut)
    return level


def bell_draw(stream_key, shape, deviation, reach, pieces=(), held_as=jnp.bfloat16):
    loudness = block_levels(stream_key, shape, pieces, -0.22, 0.18) if pieces else 1.0
    drawn = jax.random.normal(stream_key, shape, jnp.float32) * deviation * loudness
    return jnp.minimum(jnp.maximum(drawn, -reach), reach).astype(held_as)


def setup_inputs(seed: int = 0) -> dict:
    key_list = jax.random.split(jax.random.key(seed), 11)
    inputs = bell_draw(key_list[0], (SEQ_LEN, SEQS, D), 1.0, 6.0, ((0, 8), (1, 4)))
    filters = bell_draw(key_list[1], (K, SEQ_LEN), SEQ_LEN ** -0.5, 0.1875, (), jnp.float32)
    gain_in = jnp.clip(1.0 + 0.1 * jax.random.normal(key_list[2], (D,), jnp.float32), 0.5, 1.5)
    mixing = bell_draw(key_list[3], (2 * K, D, D), (2 * K * D) ** -0.5, 0.0390625, ((0, 8),))
    regression = bell_draw(key_list[4], (ORDER, D, D), (ORDER * D) ** -0.5, 0.15625)
    gain_mid = jnp.clip(1.0 + 0.1 * jax.random.normal(key_list[5], (D,), jnp.float32), 0.5, 1.5)
    w_gate = bell_draw(key_list[6], (D, FF), D ** -0.5, 0.25, ((1, 8),))
    w_up = bell_draw(key_list[7], (D, FF), D ** -0.5, 0.25, ((1, 8),))
    w_down = bell_draw(key_list[8], (FF, D), (FF // 2) ** -0.5, 0.1875, ((0, 8),))
    out_grad = bell_draw(key_list[9], (SEQ_LEN, SEQS, D), 1.0, 6.0, ((0, 8), (1, 4)))
    return {"inputs": inputs, "filters": filters, "gain_in": gain_in, "mixing": mixing, "regression": regression, "gain_mid": gain_mid, "w_gate": w_gate, "w_up": w_up, "w_down": w_down, "out_grad": out_grad}


@jax.custom_vjp
def low(v):
    return lax.optimization_barrier(v.astype(jnp.bfloat16)).astype(jnp.float32)

@jax.custom_vjp
def low_back(v):
    return v

def low_keep(v):
    return (low(v), None)

def low_pass(kept, grad):
    return (grad,)

def back_keep(v):
    return (v, None)

def back_low(kept, grad):
    return (low(grad),)
low.defvjp(low_keep, low_pass)
low_back.defvjp(back_keep, back_low)
epsilon = 1e-05
highest = lax.Precision.HIGHEST

def branch_kernels(filters):
    seq_length = filters.shape[1]
    alternate = jnp.where(jnp.arange(seq_length) % 2 == 0, 1.0, -1.0).astype(filters.dtype)
    paired = jnp.stack([filters, filters * alternate], axis=1)
    return paired.reshape(2 * filters.shape[0], seq_length)

def causal_mix(projected, kernels):
    seq_length = projected.shape[1]
    fft_size = 2 * seq_length
    proj_spec = jnp.fft.rfft(projected, n=fft_size, axis=1)
    kernel_spec = jnp.fft.rfft(kernels, n=fft_size, axis=1)
    total = lax.optimization_barrier(jnp.sum(kernel_spec[:, :, None] * proj_spec, axis=0))
    return jnp.fft.irfft(total, n=fft_size, axis=0)[:seq_length, :]

def normalize(values, gain):
    normed = values * lax.rsqrt(lax.optimization_barrier(jnp.mean(values * values, axis=-1, keepdims=True)) + epsilon)
    return normed * gain

def one_sequence(seq_in, kernels, gain_in, mixing, regression, gain_mid, w_gate, w_up, w_down):
    states = low(normalize(seq_in, gain_in))
    projected = low(low_back(jnp.einsum('ld,bde->ble', states, mixing, precision=highest)))
    spectral = causal_mix(projected, kernels)
    regress = jnp.zeros_like(spectral)
    seq_length = states.shape[0]
    for lag_index in range(regression.shape[0]):
        lagged = jnp.concatenate([jnp.zeros((lag_index, states.shape[1]), states.dtype), states[:seq_length - lag_index]], axis=0)
        regress = regress + jnp.dot(lagged, regression[lag_index], precision=highest)
    middle = seq_in + low_back(spectral + regress)
    scaled = low(normalize(middle, gain_mid))
    gate_pre = low_back(jnp.dot(scaled, w_gate, precision=highest))
    up_values = low_back(jnp.dot(scaled, w_up, precision=highest))
    hidden = low(jax.nn.silu(gate_pre) * up_values)
    return middle + jnp.dot(hidden, w_down, precision=highest)

def reference(inputs, filters, gain_in, mixing, regression, gain_mid, w_gate, w_up, w_down, out_grad):
    kernels = low(branch_kernels(filters))

    def forward(seq_major, gain_in, mixing, regression, gain_mid, w_gate, w_up, w_down):

        def step(carry, seq_in):
            result = jax.checkpoint(one_sequence)(seq_in, kernels, gain_in, mixing, regression, gain_mid, w_gate, w_up, w_down)
            return (carry, result)
        unused, outputs = lax.scan(step, jnp.zeros((), jnp.float32), seq_major)
        return outputs
    floats = [array_in.astype(jnp.float32) for array_in in (inputs, gain_in, mixing, regression, gain_mid, w_gate, w_up, w_down)]
    floats[0] = jnp.swapaxes(floats[0], 0, 1)
    outputs, pullback = jax.vjp(forward, *floats)
    grads = pullback(jnp.swapaxes(out_grad.astype(jnp.float32), 0, 1))
    block_out = jnp.swapaxes(outputs, 0, 1).astype(jnp.bfloat16)
    input_grad = jnp.swapaxes(grads[0], 0, 1)
    return (block_out, input_grad, grads[2], grads[3], grads[1], grads[4], grads[5], grads[6], grads[7])
```

```python
import functools

import jax
import jax.numpy as jnp
from jax import lax
from jax.experimental import pallas as pl
from jax.experimental.pallas import tpu as pltpu
from jax.sharding import PartitionSpec as P

EPSILON = 1e-05
CHUNKS = 2
F32 = jnp.float32
BF16 = jnp.bfloat16


def dot(left, right):
    return jnp.dot(left, right, preferred_element_type=F32)


def contract_rows(left, right):
    return lax.dot_general(left, right, (((0,), (0,)), ((), ())), preferred_element_type=F32)


def times_transpose(left, right):
    return lax.dot_general(left, right, (((1,), (1,)), ((), ())), preferred_element_type=F32)


def rms_factor(values):
    return lax.rsqrt(jnp.mean(values * values, axis=-1, keepdims=True) + EPSILON)


def norm_backward(grad_out, normed, factor, gain):
    inner = grad_out * gain
    return factor * (inner - normed * jnp.mean(inner * normed, axis=-1, keepdims=True))


class Grid:
    def __init__(self, size):
        self.far = 4 if size % 4 == 0 else 1
        self.near = size // self.far
        self.size = size

    def shift(self, far_step, near_step):
        far, near = self.far, self.near
        return [
            (f, ((f // near + far_step) % far) * near + (f % near + near_step) % near)
            for f in range(self.size)
        ]

    def order(self, index, sign):
        far, near = self.far, self.near
        steps = jnp.arange(self.size, dtype=jnp.int32)
        return (
            lax.rem(index // near + sign * (steps // near) + far, far) * near
            + lax.rem(index % near + sign * (steps % near) + near, near)
        ).astype(jnp.int32)


def spread_pieces(grid, own):
    columns = [own] + [
        lax.ppermute(own, "filt", grid.shift(i, 0)) for i in range(1, grid.far)
    ]
    pieces = []
    for column in columns:
        pieces.append(column)
        for j in range(1, grid.near):
            pieces.append(lax.ppermute(column, "filt", grid.shift(0, j)))
    return pieces


def sum_pieces(grid, pieces):
    columns = []
    for i in range(grid.far):
        total = pieces[i * grid.near].astype(F32)
        for j in range(1, grid.near):
            total = total + lax.ppermute(
                pieces[i * grid.near + j], "filt", grid.shift(0, j)
            ).astype(F32)
        columns.append(total)
    total = columns[0]
    for i in range(1, grid.far):
        total = total + lax.ppermute(
            columns[i].astype(BF16), "filt", grid.shift(i, 0)
        ).astype(F32)
    return total


def swap_rows(values, bit):
    count = lax.axis_size("rows")
    return lax.ppermute(values, "rows", [(r, r ^ bit) for r in range(count)])


def row_bits():
    count = lax.axis_size("rows")
    return [1 << n for n in range(count.bit_length() - 1)]


def all_reduce_rows(partial):
    index = lax.axis_index("rows")
    kept = partial
    for bit in row_bits():
        parts, height, width = kept.shape
        halves = kept.reshape(parts, 2, height // 2, width)
        high = (index & bit) != 0
        away = jnp.where(high, halves[:, 0], halves[:, 1]).astype(BF16)
        stay = jnp.where(high, halves[:, 1], halves[:, 0])
        kept = stay + swap_rows(away, bit).astype(F32)
    full = kept.astype(BF16)
    for bit in reversed(row_bits()):
        high = (index & bit) != 0
        other = swap_rows(full, bit)
        full = jnp.concatenate(
            [jnp.where(high, other, full), jnp.where(high, full, other)], axis=1
        )
    return full.astype(F32)


def toeplitz_kernel(half, down_ref, up_ref, t00_ref, t10_ref, u00_ref, u10_ref):
    width = down_ref.shape[-1]
    down = jnp.broadcast_to(down_ref[0], (half, width))
    block = pltpu.roll(down, 0, axis=1, stride=1, stride_axis=0)
    t10_ref[0] = block[:, :half].astype(BF16)
    t00_ref[0] = block[:, half : 2 * half].astype(BF16)
    up = jnp.broadcast_to(up_ref[0], (half, width))
    block = pltpu.roll(up, 0, axis=1, stride=1, stride_axis=0)
    u00_ref[0] = block[:, :half].astype(BF16)
    u10_ref[0] = block[:, half : 2 * half].astype(BF16)


def toeplitz_blocks(filters, first, count):
    seq_length = filters.shape[1]
    half = seq_length // 4
    taps = lax.dynamic_slice_in_dim(
        jnp.pad(filters, ((0, 1), (0, 0))), first, count, 0
    ).astype(BF16).astype(F32)
    taps = taps.reshape(count, seq_length // 2, 2)
    even, odd = taps[:, :, 0], taps[:, :, 1]
    late = jnp.concatenate([jnp.zeros_like(odd[:, :1]), odd[:, :-1]], axis=1)
    rows = jnp.stack([jnp.stack([even, late], 1), jnp.stack([even, odd], 1)], 0)
    rows = rows.reshape(4 * count, seq_length // 2)
    zeros = jnp.zeros_like(rows)
    reverse = rows[:, ::-1]
    down = jnp.concatenate(
        [
            reverse[:, half - 1 :],
            zeros[:, : half - 1],
            zeros[:, : half + 1],
            reverse[:, : half - 1],
        ],
        axis=1,
    )
    up = jnp.concatenate([rows, zeros], axis=1)
    total = 4 * count
    by_column = pl.BlockSpec((1, half, half), lambda n: (n // (2 * count), 0, n % (2 * count)))
    by_row = pl.BlockSpec((1, half, half), lambda n: (n // (2 * count), n % (2 * count), 0))
    line = pl.BlockSpec((1, 1, 4 * half), lambda n: (n, 0, 0))
    wide = jax.ShapeDtypeStruct((2, half, 2 * count * half), BF16)
    tall = jax.ShapeDtypeStruct((2, 2 * count * half, half), BF16)
    return pl.pallas_call(
        functools.partial(toeplitz_kernel, half),
        grid=(total,),
        in_specs=[line, line],
        out_specs=[by_column, by_column, by_row, by_row],
        out_shape=[wide, wide, tall, tall],
        name="toeplitz",
    )(down[:, None], up[:, None])


def assemble(order_ref, pieces, whole_ref):
    length = whole_ref.shape[0] // 2
    height = pieces[0].shape[2]
    for n, piece in enumerate(pieces):
        start = order_ref[n] * height
        for parity in range(2):
            place = pl.multiple_of(parity * length + start, height)
            whole_ref[pl.ds(place, height), :] = piece[0, parity]


def scatter(order_ref, whole_ref, pieces):
    length = whole_ref.shape[0] // 2
    height = pieces[0].shape[2]
    for n, piece in enumerate(pieces):
        start = order_ref[n] * height
        for parity in range(2):
            place = pl.multiple_of(parity * length + start, height)
            piece[0, parity] = whole_ref[pl.ds(place, height), :].astype(piece.dtype)


def mix_kernel(parts, from_ref, to_ref, *refs):
    pieces = refs[:parts]
    mix_ref, t00_ref, t10_ref = refs[parts : parts + 3]
    outs = refs[parts + 3 : 2 * parts + 3]
    states_ref, low_ref, high_ref, sum_ref = refs[2 * parts + 3 :]
    half = t00_ref.shape[1]
    branches = mix_ref.shape[0]
    assemble(from_ref, pieces, states_ref)

    for branch in range(branches):
        slot = pl.ds(branch * half, half)
        for quarter in range(4):
            value = dot(
                states_ref[pl.ds(quarter * half, half), :], mix_ref[branch]
            ).astype(BF16)
            target = (quarter // 2) ^ (branch % 2)
            (low_ref, high_ref)[quarter % 2][target, slot, :] = value

    for parity in range(2):
        base = 2 * parity * half
        sum_ref[pl.ds(base, half), :] = dot(t00_ref[parity], low_ref[parity]).astype(
            sum_ref.dtype
        )
        sum_ref[pl.ds(base + half, half), :] = (
            dot(t10_ref[parity], low_ref[parity]) + dot(t00_ref[parity], high_ref[parity])
        ).astype(sum_ref.dtype)
    scatter(to_ref, sum_ref, outs)


def mix_back_kernel(parts, from_ref, to_ref, own_ref, *refs):
    state_pieces = refs[:parts]
    grad_pieces = refs[parts : 2 * parts]
    turned_ref, u00_ref, u10_ref, before_ref, before_lag_ref = refs[2 * parts : 2 * parts + 5]
    outs = refs[2 * parts + 5 : 3 * parts + 5]
    mixing_ref, lag_ref = refs[3 * parts + 5 : 3 * parts + 7]
    states_ref, grad_ref, flip_ref, back_ref, sum_ref = refs[3 * parts + 7 :]
    half = u00_ref.shape[2]
    branches = mixing_ref.shape[0]
    width = grad_ref.shape[1]
    length = states_ref.shape[0] // 2

    @pl.when(pl.program_id(0) == 0)
    def _():
        mixing_ref[...] = before_ref[...]
        lag_ref[...] = before_lag_ref[...]

    assemble(from_ref, state_pieces, states_ref)
    assemble(from_ref, grad_pieces, grad_ref)
    flip_ref[...] = states_ref[...].T

    for parity in range(2):
        base = 2 * parity * half
        low = grad_ref[pl.ds(base, half), :]
        high = grad_ref[pl.ds(base + half, half), :]
        for branch in range(branches):
            rows = pl.ds(branch * half, half)
            columns = pl.ds(branch * width, width)
            target = 2 * half * (parity ^ (branch % 2))
            back_ref[pl.ds(target, half), columns] = (
                dot(u00_ref[parity, rows, :], low) + dot(u10_ref[parity, rows, :], high)
            ).astype(BF16)
            back_ref[pl.ds(target + half, half), columns] = dot(
                u00_ref[parity, rows, :], high
            ).astype(BF16)

    for quarter in range(4):
        rows = pl.ds(quarter * half, half)
        sum_ref[rows, :] = dot(back_ref[rows, :], turned_ref[...]).astype(sum_ref.dtype)
    scatter(to_ref, sum_ref, outs)

    for branch in range(branches):
        columns = pl.ds(branch * width, width)
        mixing_ref[branch] += dot(flip_ref[...], back_ref[:, columns])

    slab = lag_ref.shape[1]
    start = pl.multiple_of(own_ref[0] * slab, slab)
    own = flip_ref[pl.ds(start, slab), :].astype(F32)
    even, odd = own[:, :length], own[:, length:]
    first = lax.broadcasted_iota(jnp.int32, even.shape, 1) == 0
    even_late = jnp.where(first, 0.0, pltpu.roll(even, 1, axis=1))
    odd_late = jnp.where(first, 0.0, pltpu.roll(odd, 1, axis=1))
    for lag, (on_even, on_odd) in enumerate(
        ((even, odd), (odd_late, even), (even_late, odd_late))
    ):
        lag_ref[lag] += dot(on_even.astype(BF16), grad_ref[:length, :]) + dot(
            on_odd.astype(BF16), grad_ref[length:, :]
        )


def resident(shape):
    zeros = (0,) * len(shape)
    return pl.BlockSpec(shape, lambda *_: zeros, pipeline_mode=pl.Buffered(1))


def mix_sequences(pieces, order_from, order_to, pairs, t00, t10):
    parts = len(pieces)
    count, _, height, width = pieces[0].shape
    half = t00.shape[1]
    block = pl.BlockSpec((1, 2, height, width), lambda n, *_: (n, 0, 0, 0))
    rows = t00.shape[2]
    return pl.pallas_call(
        functools.partial(mix_kernel, parts),
        grid_spec=pltpu.PrefetchScalarGridSpec(
            num_scalar_prefetch=2,
            grid=(count,),
            in_specs=[block] * parts
            + [resident(pairs.shape), resident(t00.shape), resident(t10.shape)],
            out_specs=[block] * parts,
            scratch_shapes=[
                pltpu.VMEM((4 * half, width), BF16),
                pltpu.VMEM((2, rows, width), BF16),
                pltpu.VMEM((2, rows, width), BF16),
                pltpu.VMEM((4 * half, width), F32),
            ],
        ),
        out_shape=[jax.ShapeDtypeStruct(pieces[0].shape, BF16)] * parts,
        compiler_params=pltpu.CompilerParams(vmem_limit_bytes=48 << 20),
        cost_estimate=pl.CostEstimate(
            flops=count * (8 * half * width * pairs.shape[0] * width + 12 * half * rows * width),
            bytes_accessed=2 * parts * pieces[0].size * 2 + 2 * pairs.size + 4 * t00.size,
            transcendentals=0,
        ),
        name="mix",
    )(order_from, order_to, *pieces, pairs, t00, t10)


def mix_sequences_back(
    states, grads, order_from, order_to, own, turned, u00, u10, before, before_lag
):
    parts = len(states)
    count, _, height, width = states[0].shape
    half = u00.shape[2]
    block = pl.BlockSpec((1, 2, height, width), lambda n, *_: (n, 0, 0, 0))
    rows = u00.shape[1]
    return pl.pallas_call(
        functools.partial(mix_back_kernel, parts),
        grid_spec=pltpu.PrefetchScalarGridSpec(
            num_scalar_prefetch=3,
            grid=(count,),
            in_specs=[block] * (2 * parts)
            + [resident(a.shape) for a in (turned, u00, u10, before, before_lag)],
            out_specs=[block] * parts + [resident(before.shape), resident(before_lag.shape)],
            scratch_shapes=[
                pltpu.VMEM((4 * half, width), BF16),
                pltpu.VMEM((4 * half, width), BF16),
                pltpu.VMEM((width, 4 * half), BF16),
                pltpu.VMEM((4 * half, turned.shape[0]), BF16),
                pltpu.VMEM((4 * half, width), F32),
            ],
        ),
        out_shape=[jax.ShapeDtypeStruct(states[0].shape, BF16)] * parts
        + [
            jax.ShapeDtypeStruct(before.shape, F32),
            jax.ShapeDtypeStruct(before_lag.shape, F32),
        ],
        compiler_params=pltpu.CompilerParams(vmem_limit_bytes=56 << 20),
        cost_estimate=pl.CostEstimate(
            flops=count * (16 * half * width * turned.shape[0] + 12 * half * rows * width),
            bytes_accessed=3 * parts * states[0].size * 2 + 2 * turned.size + 8 * before.size,
            transcendentals=0,
        ),
        name="mix_back",
    )(order_from, order_to, own, *states, *grads, turned, u00, u10, before, before_lag)


def lagged(values, edge):
    late = jnp.concatenate([edge, values[:, :, :-1]], axis=2)
    return values, jnp.stack([late[:, 1], values[:, 0]], axis=1), late


def leading(values, edge):
    early = jnp.concatenate([values[:, :, 1:], edge], axis=2)
    return values, jnp.stack([values[:, 1], early[:, 0]], axis=1), early


def row_masks():
    masks = [0]
    for bit in reversed(row_bits()):
        masks = masks + [mask ^ bit for mask in masks]
    return masks


def spread_rows(own):
    full = own[None]
    for bit in reversed(row_bits()):
        full = jnp.concatenate([full, swap_rows(full, bit)], axis=0)
    return full


def shards(inputs, filters, gain_in, mixing, regression, gain_mid, w_gate, w_up, w_down, out_grad):
    shard_rows, local_seqs, width = inputs.shape
    grid = Grid(lax.axis_size("filt"))
    row_count = lax.axis_size("rows")
    index = lax.axis_index("filt")
    branches = mixing.shape[0]
    lag_count = regression.shape[0]
    height = shard_rows // 2
    chunks = CHUNKS
    step = local_seqs // chunks

    def inward(values):
        return values.reshape(height, 2, local_seqs, width).transpose(2, 1, 0, 3)

    def outward(values):
        return values.transpose(2, 1, 0, 3).reshape(shard_rows, local_seqs, width)

    def cut(values):
        return [values[c * step : (c + 1) * step] for c in range(chunks)]

    residual = inward(inputs).astype(F32)
    cotangent_low = inward(out_grad)
    factor_in = rms_factor(residual)
    normed_in = residual * factor_in
    states = (normed_in * gain_in).astype(BF16)
    state_pieces = [spread_pieces(grid, part) for part in cut(states)]

    hidden_own = w_down.shape[0]
    share = hidden_own // row_count
    packed = jnp.stack([w_gate.T, w_up.T, w_down]).reshape(3, row_count, share, width)
    own_share = lax.dynamic_index_in_dim(packed, lax.axis_index("rows"), 1, keepdims=False)
    shares = jnp.stack(spread_pieces(grid, own_share), axis=1)
    weights = spread_rows(shares)
    gate_t, up_t, down = (
        weights[:, n].reshape(row_count * grid.size * share, width) for n in range(3)
    )

    slots = (branches + 1) // 2
    first_branch = index * branches
    t00, t10, u00, u10 = toeplitz_blocks(filters, first_branch // 2, slots)
    if branches % 2:
        odd_start = first_branch % 2
        paired = lax.dynamic_update_slice_in_dim(
            jnp.zeros((2 * slots,) + mixing.shape[1:], mixing.dtype), mixing, odd_start, 0
        )
    else:
        paired = mixing
    paired = paired.astype(F32).reshape(slots, 2, width, width)
    pairs = (
        jnp.stack([paired[:, 0] + paired[:, 1], paired[:, 0] - paired[:, 1]], axis=1)
        .astype(BF16)
        .reshape(2 * slots, width, width)
    )
    turned = pairs.transpose(0, 2, 1).reshape(2 * slots * width, width)

    order_from, order_to = grid.order(index, -1), grid.order(index, 1)

    edge = lax.ppermute(
        states[:, :, -1:], "filt", [(f, f + 1) for f in range(grid.size - 1)]
    )
    regress = sum(
        jnp.einsum("spad,de->spae", lag, regression[n], preferred_element_type=F32)
        for n, lag in enumerate(lagged(states, edge))
    )
    cotangent = cotangent_low.astype(F32)

    spectral = []
    for c in range(chunks):
        partial = mix_sequences(state_pieces[c], order_from, order_to, pairs, t00, t10)
        spectral.append(sum_pieces(grid, partial))

    block_out, middle_grad, grad_pieces, kept = [], [], [], []
    gain_mid_part = jnp.zeros((width,), F32)
    for c in range(chunks):
        part = slice(c * step, (c + 1) * step)
        middle = residual[part] + (spectral[c] + regress[part])
        factor_mid = rms_factor(middle)
        normed_mid = middle * factor_mid
        scaled = (normed_mid * gain_mid).astype(BF16).reshape(-1, width)
        cot_low = cotangent_low[part].reshape(-1, width)
        gate_pre = times_transpose(scaled, gate_t)
        up_values = times_transpose(scaled, up_t)
        sigmoid = jax.nn.sigmoid(gate_pre)
        silu = gate_pre * sigmoid
        hidden = (silu * up_values).astype(BF16)
        block_out.append(
            (middle + dot(hidden, down).reshape(middle.shape)).astype(BF16)
        )
        grad_hidden = times_transpose(cot_low, down)
        gate_back = (
            grad_hidden * up_values * (sigmoid * (1.0 + gate_pre * (1.0 - sigmoid)))
        ).astype(BF16)
        up_back = (grad_hidden * silu).astype(BF16)
        mid_back = (dot(gate_back, gate_t) + dot(up_back, up_t)).reshape(middle.shape)
        gain_mid_part = gain_mid_part + jnp.sum(mid_back * normed_mid, axis=(0, 1, 2))
        grad = cotangent[part] + norm_backward(mid_back, normed_mid, factor_mid, gain_mid)
        middle_grad.append(grad)
        grad_pieces.append(spread_pieces(grid, grad.astype(BF16)))
        kept.append((scaled, cot_low, hidden, gate_back, up_back))

    scaled, cot_low, hidden, gate_back, up_back = (
        jnp.concatenate(values, axis=0) for values in zip(*kept, strict=True)
    )
    grads = jnp.stack(
        [
            contract_rows(gate_back, scaled),
            contract_rows(up_back, scaled),
            contract_rows(hidden, cot_low),
        ]
    ).reshape(3, row_count, grid.size, share, width)
    for bit in row_bits():
        half_count = grads.shape[1] // 2
        grads = grads[:, :half_count] + swap_rows(
            grads[:, half_count:].astype(BF16), bit
        ).astype(F32)
    grads = grads[:, 0].astype(BF16)
    returning = []
    for i in range(grid.far):
        for j in range(grid.near):
            n = ((grid.far - i) % grid.far) * grid.near + (grid.near - j) % grid.near
            returning.append(grads[:, n])
    own_grads = sum_pieces(grid, returning).astype(BF16)

    before = jnp.zeros((2 * slots, width, width), F32)
    before_lag = jnp.zeros((lag_count, width // grid.size, width), F32)
    own = jnp.reshape(index, (1,)).astype(jnp.int32)
    state_back = []
    for c in range(chunks):
        *partial, before, before_lag = mix_sequences_back(
            state_pieces[c], grad_pieces[c], order_from, order_to, own, turned, u00, u10,
            before, before_lag,
        )
        state_back.append(sum_pieces(grid, partial))

    doubled = before.reshape(slots, 2, width, width)
    mixing_part = jnp.stack(
        [doubled[:, 0] + doubled[:, 1], doubled[:, 0] - doubled[:, 1]], axis=1
    ).reshape(2 * slots, width, width)
    if branches % 2:
        mixing_part = lax.dynamic_slice_in_dim(mixing_part, odd_start, branches, 0)
    mixing_grad = all_reduce_rows(mixing_part)

    slab = width // grid.size
    own_regression = lax.dynamic_slice_in_dim(regression, index * slab, slab, 1)
    gain_lag = jnp.sum(own_regression.astype(F32) * before_lag, axis=(0, 2))
    gain_in_part = jnp.sum(mixing.astype(F32) * mixing_part, axis=(0, 2))
    gain_in_part = lax.dynamic_update_slice_in_dim(
        gain_in_part,
        lax.dynamic_slice_in_dim(gain_in_part, index * slab, slab, 0) + gain_lag,
        index * slab,
        0,
    ) / gain_in
    gains = jnp.stack([gain_in_part, gain_mid_part])
    small = jnp.concatenate(
        [before_lag.reshape(lag_count * slab, width), jnp.pad(gains, ((0, 6), (0, 0)))], axis=0
    )
    for bit in row_bits():
        rounded = small[:-8].astype(BF16)
        gain_high = small[-8:].astype(BF16)
        gain_low = (small[-8:] - gain_high.astype(F32)).astype(BF16)
        other = swap_rows(jnp.concatenate([rounded, gain_high, gain_low], axis=0), bit).astype(F32)
        small = small + jnp.concatenate([other[:-16], other[-16:-8] + other[-8:]], axis=0)
    gain_high = small[-8:].astype(BF16)
    gain_low = (small[-8:] - gain_high.astype(F32)).astype(BF16)
    small_low = jnp.concatenate([small[:-8].astype(BF16), gain_high, gain_low], axis=0)
    spread = jnp.stack(spread_pieces(grid, small_low))
    gains = jnp.sum(spread[:, -16:-8].astype(F32) + spread[:, -8:].astype(F32), axis=0)
    regression_grad = jnp.zeros((lag_count, grid.size, slab, width), F32)
    for n in range(grid.size):
        piece = spread[n, :-16].astype(F32).reshape(lag_count, 1, slab, width)
        regression_grad = lax.dynamic_update_slice_in_dim(regression_grad, piece, order_from[n], 1)
    regression_grad = regression_grad.reshape(lag_count, width, width)

    mix_back = jnp.concatenate(middle_grad, axis=0).astype(BF16)
    edge = lax.ppermute(
        mix_back[:, :, :1], "filt", [(f + 1, f) for f in range(grid.size - 1)]
    )
    lag_back = sum(
        jnp.einsum("spae,de->spad", lead, regression[n], preferred_element_type=F32)
        for n, lead in enumerate(leading(mix_back, edge))
    )
    input_grad = []
    for c in range(chunks):
        part = slice(c * step, (c + 1) * step)
        back = state_back[c] + lag_back[part]
        input_grad.append(
            middle_grad[c] + norm_backward(back, normed_in[part], factor_in[part], gain_in)
        )

    full = spread_rows(own_grads)
    row_index = lax.axis_index("rows")
    ordered = jnp.zeros((row_count, 3, share, width), BF16)
    for n, mask in enumerate(row_masks()):
        ordered = lax.dynamic_update_slice_in_dim(ordered, full[n][None], row_index ^ mask, 0)
    ordered = ordered.transpose(1, 0, 2, 3).reshape(3, hidden_own, width).astype(F32)
    return (
        outward(jnp.concatenate(block_out, axis=0)),
        outward(jnp.concatenate(input_grad, axis=0)),
        mixing_grad,
        regression_grad,
        gains[0],
        gains[1],
        ordered[0].T,
        ordered[1].T,
        ordered[2],
    )


def solution(mesh):
    placed = (
        P("filt", "rows", None),
        P(),
        P(),
        P("filt", None, None),
        P(),
        P(),
        P(None, "filt"),
        P(None, "filt"),
        P("filt", None),
        P("filt", "rows", None),
    )
    return jax.shard_map(
        shards,
        mesh=mesh,
        in_specs=placed,
        out_specs=(
            P("filt", "rows", None),
            P("filt", "rows", None),
            P("filt", None, None),
            P(),
            P(),
            P(),
            P(None, "filt"),
            P(None, "filt"),
            P("filt", None),
        ),
        check_vma=False,
    )
```

```python
import functools

import jax
import jax.numpy as jnp
from jax import lax
from jax.experimental import pallas as pl
from jax.experimental.pallas import tpu as pltpu
from jax.sharding import PartitionSpec as P

EPSILON = 1e-05
CHUNKS = 2
F32 = jnp.float32
BF16 = jnp.bfloat16


def dot(left, right):
    return jnp.dot(left, right, preferred_element_type=F32)


def contract_rows(left, right):
    return lax.dot_general(left, right, (((0,), (0,)), ((), ())), preferred_element_type=F32)


def times_transpose(left, right):
    return lax.dot_general(left, right, (((1,), (1,)), ((), ())), preferred_element_type=F32)


def rms_factor(values):
    return lax.rsqrt(jnp.mean(values * values, axis=-1, keepdims=True) + EPSILON)


def norm_backward(grad_out, normed, factor, gain):
    inner = grad_out * gain
    return factor * (inner - normed * jnp.mean(inner * normed, axis=-1, keepdims=True))


class Grid:
    def __init__(self, size):
        self.far = 4 if size % 4 == 0 else 1
        self.near = size // self.far
        self.size = size

    def near_shift(self, step):
        near = self.near
        return [(f, f // near * near + (f % near + step) % near) for f in range(self.size)]

    def swap_far(self, values):
        groups = [
            [i * self.near + j for i in range(self.far)] for j in range(self.near)
        ]
        return lax.all_to_all(values, "filt", 0, 0, axis_index_groups=groups, tiled=True)


def tie(value, *others):
    return lax.optimization_barrier((value, *others))[0] if others else value


def tie_all(values, *others):
    count = len(values)
    return list(lax.optimization_barrier((*values, *others))[:count]) if others else list(values)


def near_swaps(grid, values):
    return [
        lax.ppermute(
            values[j] if isinstance(values, list) else values, "filt", grid.near_shift(j)
        )
        for j in range(1, grid.near)
    ]


def total_of(values):
    total = values[0].astype(F32)
    for value in values[1:]:
        total = total + value.astype(F32)
    return total


def swap_rows(values, bit):
    count = lax.axis_size("rows")
    return lax.ppermute(values, "rows", [(r, r ^ bit) for r in range(count)])


def row_bits():
    count = lax.axis_size("rows")
    return [1 << n for n in range(count.bit_length() - 1)]


def all_reduce_rows(partial):
    index = lax.axis_index("rows")
    kept = partial
    for bit in row_bits():
        parts, height, width = kept.shape
        halves = kept.reshape(parts, 2, height // 2, width)
        high = (index & bit) != 0
        away = jnp.where(high, halves[:, 0], halves[:, 1]).astype(BF16)
        stay = jnp.where(high, halves[:, 1], halves[:, 0])
        kept = stay + swap_rows(away, bit).astype(F32)
    full = kept.astype(BF16)
    for bit in reversed(row_bits()):
        high = (index & bit) != 0
        other = swap_rows(full, bit)
        full = jnp.concatenate(
            [jnp.where(high, other, full), jnp.where(high, full, other)], axis=1
        )
    return full.astype(F32)


def toeplitz_kernel(half, down_ref, up_ref, t00_ref, t10_ref, u00_ref, u10_ref):
    width = down_ref.shape[-1]
    down = jnp.broadcast_to(down_ref[0], (half, width))
    block = pltpu.roll(down, 0, axis=1, stride=1, stride_axis=0)
    t10_ref[0] = block[:, :half].astype(BF16)
    t00_ref[0] = block[:, half : 2 * half].astype(BF16)
    up = jnp.broadcast_to(up_ref[0], (half, width))
    block = pltpu.roll(up, 0, axis=1, stride=1, stride_axis=0)
    u00_ref[0] = block[:, :half].astype(BF16)
    u10_ref[0] = block[:, half : 2 * half].astype(BF16)


def toeplitz_blocks(filters, first, count):
    seq_length = filters.shape[1]
    half = seq_length // 4
    taps = lax.dynamic_slice_in_dim(
        jnp.pad(filters, ((0, 1), (0, 0))), first, count, 0
    ).astype(BF16).astype(F32)
    taps = taps.reshape(count, seq_length // 2, 2)
    even, odd = taps[:, :, 0], taps[:, :, 1]
    late = jnp.concatenate([jnp.zeros_like(odd[:, :1]), odd[:, :-1]], axis=1)
    rows = jnp.stack([jnp.stack([even, late], 1), jnp.stack([even, odd], 1)], 0)
    rows = rows.reshape(4 * count, seq_length // 2)
    zeros = jnp.zeros_like(rows)
    reverse = rows[:, ::-1]
    down = jnp.concatenate(
        [
            reverse[:, half - 1 :],
            zeros[:, : half - 1],
            zeros[:, : half + 1],
            reverse[:, : half - 1],
        ],
        axis=1,
    )
    up = jnp.concatenate([rows, zeros], axis=1)
    total = 4 * count
    by_column = pl.BlockSpec((1, half, half), lambda n: (n // (2 * count), 0, n % (2 * count)))
    by_row = pl.BlockSpec((1, half, half), lambda n: (n // (2 * count), n % (2 * count), 0))
    line = pl.BlockSpec((1, 1, 4 * half), lambda n: (n, 0, 0))
    wide = jax.ShapeDtypeStruct((2, half, 2 * count * half), BF16)
    tall = jax.ShapeDtypeStruct((2, 2 * count * half, half), BF16)
    return pl.pallas_call(
        functools.partial(toeplitz_kernel, half),
        grid=(total,),
        in_specs=[line, line],
        out_specs=[by_column, by_column, by_row, by_row],
        out_shape=[wide, wide, tall, tall],
        name="toeplitz",
    )(down[:, None], up[:, None])


def places(near, pieces, whole_ref, sign):
    length = whole_ref.shape[0] // 2
    nears = len(pieces)
    fars, _, _, height, _ = pieces[0].shape
    for j, piece in enumerate(pieces):
        at = lax.rem(near + sign * j + nears, nears)
        for i in range(fars):
            for parity in range(2):
                start = parity * length + (i * nears + at) * height
                yield piece.at[i, 0, parity], pl.ds(pl.multiple_of(start, height), height)


def assemble(near, pieces, whole_ref):
    for piece, rows in places(near, pieces, whole_ref, -1):
        whole_ref[rows, :] = piece[...]


def scatter(near, whole_ref, pieces):
    for piece, rows in places(near, pieces, whole_ref, 1):
        piece[...] = whole_ref[rows, :].astype(piece.dtype)


def mix_kernel(parts, near_ref, *refs):
    pieces = refs[:parts]
    mixes = refs[parts : parts + 2]
    t00_ref, t10_ref = refs[parts + 2 : parts + 4]
    outs = refs[parts + 4 : 2 * parts + 4]
    states_ref, low_ref, high_ref, sum_ref = refs[2 * parts + 4 :]
    half = t00_ref.shape[1]
    branches = 2 * mixes[0].shape[0]
    assemble(near_ref[0], pieces, states_ref)

    for branch in range(branches):
        slot = pl.ds(branch * half, half)
        for quarter in range(4):
            value = dot(
                states_ref[pl.ds(quarter * half, half), :], mixes[branch % 2][branch // 2]
            ).astype(BF16)
            target = (quarter // 2) ^ (branch % 2)
            (low_ref, high_ref)[quarter % 2][target, slot, :] = value

    for parity in range(2):
        base = 2 * parity * half
        sum_ref[pl.ds(base, half), :] = dot(t00_ref[parity], low_ref[parity]).astype(
            sum_ref.dtype
        )
        sum_ref[pl.ds(base + half, half), :] = (
            dot(t10_ref[parity], low_ref[parity]) + dot(t00_ref[parity], high_ref[parity])
        ).astype(sum_ref.dtype)
    scatter(near_ref[0], sum_ref, outs)


def mix_back_kernel(parts, near_ref, own_ref, *refs):
    state_pieces = refs[:parts]
    grad_pieces = refs[parts : 2 * parts]
    turned = refs[2 * parts : 2 * parts + 2]
    u00_ref, u10_ref = refs[2 * parts + 2 : 2 * parts + 4]
    before = refs[2 * parts + 4 : -parts - 7]
    outs = refs[-parts - 7 : -7]
    mixing_ref, lag_ref = refs[-7:-5]
    states_ref, grad_ref, flip_ref, back_ref, sum_ref = refs[-5:]
    half = u00_ref.shape[2]
    branches = mixing_ref.shape[0]
    slots = branches // 2
    width = grad_ref.shape[1]
    length = states_ref.shape[0] // 2

    @pl.when(pl.program_id(0) == 0)
    def _():
        if before:
            mixing_ref[...] = before[0][...]
            lag_ref[...] = before[1][...]
        else:
            mixing_ref[...] = jnp.zeros_like(mixing_ref)
            lag_ref[...] = jnp.zeros_like(lag_ref)

    assemble(near_ref[0], state_pieces, states_ref)
    assemble(near_ref[0], grad_pieces, grad_ref)
    flip_ref[...] = states_ref[...].T

    for parity in range(2):
        base = 2 * parity * half
        low = grad_ref[pl.ds(base, half), :]
        high = grad_ref[pl.ds(base + half, half), :]
        for branch in range(branches):
            rows = pl.ds(branch * half, half)
            columns = pl.ds((branch % 2 * slots + branch // 2) * width, width)
            target = 2 * half * (parity ^ (branch % 2))
            back_ref[pl.ds(target, half), columns] = (
                dot(u00_ref[parity, rows, :], low) + dot(u10_ref[parity, rows, :], high)
            ).astype(BF16)
            back_ref[pl.ds(target + half, half), columns] = dot(
                u00_ref[parity, rows, :], high
            ).astype(BF16)

    for quarter in range(4):
        rows = pl.ds(quarter * half, half)
        sum_ref[rows, :] = dot(back_ref[rows, : slots * width], turned[0][...]) + dot(
            back_ref[rows, slots * width :], turned[1][...]
        )
    scatter(near_ref[0], sum_ref, outs)

    for branch in range(branches):
        columns = pl.ds((branch % 2 * slots + branch // 2) * width, width)
        mixing_ref[branch] += dot(flip_ref[...], back_ref[:, columns])

    slab = lag_ref.shape[1]
    start = pl.multiple_of(own_ref[0] * slab, slab)
    own = flip_ref[pl.ds(start, slab), :].astype(F32)
    even, odd = own[:, :length], own[:, length:]
    first = lax.broadcasted_iota(jnp.int32, even.shape, 1) == 0
    even_late = jnp.where(first, 0.0, pltpu.roll(even, 1, axis=1))
    odd_late = jnp.where(first, 0.0, pltpu.roll(odd, 1, axis=1))
    for lag, (on_even, on_odd) in enumerate(
        ((even, odd), (odd_late, even), (even_late, odd_late))
    ):
        lag_ref[lag] += dot(on_even.astype(BF16), grad_ref[:length, :]) + dot(
            on_odd.astype(BF16), grad_ref[length:, :]
        )


def resident(shape):
    zeros = (0,) * len(shape)
    return pl.BlockSpec(shape, lambda *_: zeros, pipeline_mode=pl.Buffered(1))


def mix_sequences(pieces, near, pairs, t00, t10):
    parts = len(pieces)
    fars, count, _, height, width = pieces[0].shape
    half = t00.shape[1]
    block = pl.BlockSpec((fars, 1, 2, height, width), lambda n, *_: (0, n, 0, 0, 0))
    rows = t00.shape[2]
    return pl.pallas_call(
        functools.partial(mix_kernel, parts),
        grid_spec=pltpu.PrefetchScalarGridSpec(
            num_scalar_prefetch=1,
            grid=(count,),
            in_specs=[block] * parts
            + [resident(a.shape) for a in (*pairs, t00, t10)],
            out_specs=[block] * parts,
            scratch_shapes=[
                pltpu.VMEM((4 * half, width), BF16),
                pltpu.VMEM((2, rows, width), BF16),
                pltpu.VMEM((2, rows, width), BF16),
                pltpu.VMEM((4 * half, width), F32),
            ],
        ),
        out_shape=[jax.ShapeDtypeStruct(pieces[0].shape, BF16)] * parts,
        compiler_params=pltpu.CompilerParams(vmem_limit_bytes=48 << 20),
        cost_estimate=pl.CostEstimate(
            flops=count * (16 * half * pairs[0].size + 12 * half * rows * width),
            bytes_accessed=4 * parts * pieces[0].size + 4 * pairs[0].size + 4 * t00.size,
            transcendentals=0,
        ),
        name="mix",
    )(near, *pieces, *pairs, t00, t10)


def mix_sequences_back(
    states, grads, near, own, turned, u00, u10, lag_count, before
):
    parts = len(states)
    fars, count, _, height, width = states[0].shape
    half = u00.shape[2]
    block = pl.BlockSpec((fars, 1, 2, height, width), lambda n, *_: (0, n, 0, 0, 0))
    rows = u00.shape[1]
    mixing_shape = (2 * turned[0].shape[0] // width, width, width)
    lag_shape = (lag_count, width // (parts * fars), width)
    return pl.pallas_call(
        functools.partial(mix_back_kernel, parts),
        grid_spec=pltpu.PrefetchScalarGridSpec(
            num_scalar_prefetch=2,
            grid=(count,),
            in_specs=[block] * (2 * parts)
            + [resident(a.shape) for a in (*turned, u00, u10, *before)],
            out_specs=[block] * parts + [resident(mixing_shape), resident(lag_shape)],
            scratch_shapes=[
                pltpu.VMEM((4 * half, width), BF16),
                pltpu.VMEM((4 * half, width), BF16),
                pltpu.VMEM((width, 4 * half), BF16),
                pltpu.VMEM((4 * half, 2 * turned[0].shape[0]), BF16),
                pltpu.VMEM((4 * half, width), F32),
            ],
        ),
        out_shape=[jax.ShapeDtypeStruct(states[0].shape, BF16)] * parts
        + [
            jax.ShapeDtypeStruct(mixing_shape, F32),
            jax.ShapeDtypeStruct(lag_shape, F32),
        ],
        compiler_params=pltpu.CompilerParams(vmem_limit_bytes=56 << 20),
        cost_estimate=pl.CostEstimate(
            flops=count * (32 * half * turned[0].size + 12 * half * rows * width),
            bytes_accessed=3 * parts * states[0].size * 2 + 20 * turned[0].size,
            transcendentals=0,
        ),
        name="mix_back",
    )(near, own, *states, *grads, *turned, u00, u10, *before)


def lagged(values, edge):
    late = jnp.concatenate([edge, values[:, :, :-1]], axis=2)
    return values, jnp.stack([late[:, 1], values[:, 0]], axis=1), late


def leading(values, edge):
    early = jnp.concatenate([values[:, :, 1:], edge], axis=2)
    return values, jnp.stack([values[:, 1], early[:, 0]], axis=1), early


def row_masks():
    masks = [0]
    for bit in reversed(row_bits()):
        masks = masks + [mask ^ bit for mask in masks]
    return masks


def spread_rows(own):
    full = own[None]
    for bit in reversed(row_bits()):
        full = jnp.concatenate([full, swap_rows(full, bit)], axis=0)
    return full


def shards(inputs, filters, gain_in, mixing, regression, gain_mid, w_gate, w_up, w_down, out_grad):
    shard_rows, local_seqs, width = inputs.shape
    grid = Grid(lax.axis_size("filt"))
    row_count = lax.axis_size("rows")
    index = lax.axis_index("filt")
    branches = mixing.shape[0]
    lag_count = regression.shape[0]
    height = shard_rows // 2
    chunks = CHUNKS
    step = local_seqs // chunks

    def inward(values):
        return values.reshape(height, 2, local_seqs, width).transpose(2, 1, 0, 3)

    def outward(values):
        return values.transpose(2, 1, 0, 3).reshape(shard_rows, local_seqs, width)

    def cut(values):
        return [values[c * step : (c + 1) * step] for c in range(chunks)]

    residual = inward(inputs).astype(F32)
    cotangent_low = inward(out_grad)
    factor_in = rms_factor(residual)
    normed_in = residual * factor_in
    states = (normed_in * gain_in).astype(BF16)
    state_far = []
    for c, part in enumerate(cut(states)):
        if c:
            part = tie(part, state_far[-1])
        state_far.append(grid.swap_far(jnp.stack([part] * grid.far)))

    hidden_own = w_down.shape[0]
    share = hidden_own // row_count
    packed = jnp.stack([w_gate.T, w_up.T, w_down]).reshape(3, row_count, share, width)
    own_share = lax.dynamic_index_in_dim(packed, lax.axis_index("rows"), 1, keepdims=False)
    shares = lax.all_gather(tie(own_share, state_far[0]), "filt", axis=1)
    slots = (branches + 1) // 2
    first_branch = index * branches
    t00, t10, u00, u10 = toeplitz_blocks(filters, first_branch // 2, slots)
    if branches % 2:
        odd_start = first_branch % 2
        paired = lax.dynamic_update_slice_in_dim(
            jnp.zeros((2 * slots,) + mixing.shape[1:], mixing.dtype), mixing, odd_start, 0
        )
    else:
        paired = mixing
    first, second = (paired[n::2].astype(F32) for n in range(2))
    pairs = ((first + second).astype(BF16), (first - second).astype(BF16))

    near = jnp.reshape(index % grid.near, (1,)).astype(jnp.int32)

    edge = lax.ppermute(
        states[:, :, -1:], "filt", [(f, f + 1) for f in range(grid.size - 1)]
    )
    regress = sum(
        jnp.einsum("spad,de->spae", lag, regression[n], preferred_element_type=F32)
        for n, lag in enumerate(lagged(states, edge))
    )
    cotangent = cotangent_low.astype(F32)

    state_pieces, partials = [], []
    for c in range(chunks):
        received = near_swaps(grid, state_far[c])
        if c:
            received = tie_all(received, partials[-1][0])
        pieces = [state_far[c], *received]
        state_pieces.append(pieces)
        ahead = [] if c else [regress]
        if c + 1 < chunks:
            ahead.append(state_far[c + 1])
        pieces = [tie(pieces[0], *ahead), *pieces[1:]]
        partials.append(list(mix_sequences(pieces, near, pairs, t00, t10)))
    near_received = [near_swaps(grid, partial) for partial in partials]
    for c in range(chunks - 1):
        near_received[c] = tie_all(near_received[c], partials[c + 1][0])
    arrivals = near_received[0] or partials[-1][:1]
    shares = tie(shares, partials[0][0])
    full_shares = shares[None]
    for n, bit in enumerate(reversed(row_bits())):
        received = swap_rows(full_shares, bit)
        if n == 0:
            received = tie(received, *arrivals)
        full_shares = jnp.concatenate([full_shares, received], axis=0)
    gate_t, up_t, down = (
        full_shares[:, n].reshape(row_count * grid.size * share, width) for n in range(3)
    )
    late_pairs = tie_all(pairs, *arrivals)
    turned = [value.transpose(0, 2, 1).reshape(slots * width, width) for value in late_pairs]

    spectral = []
    for c in range(chunks):
        spectral.append(
            grid.swap_far(total_of([partials[c][0], *near_received[c]]).astype(BF16))
        )

    block_out, middle_grad, grad_far, kept = [], [], [], []
    gain_mid_part = jnp.zeros((width,), F32)
    for c in range(chunks):
        part = slice(c * step, (c + 1) * step)
        arrived = spectral[c]
        if c:
            arrived = tie(arrived, middle_grad[-1])
        if c + 1 < chunks:
            arrived = tie(arrived, *near_received[c + 1], *turned)
        middle = residual[part] + (total_of(arrived) + regress[part])
        factor_mid = rms_factor(middle)
        normed_mid = middle * factor_mid
        scaled = (normed_mid * gain_mid).astype(BF16).reshape(-1, width)
        cot_low = cotangent_low[part].reshape(-1, width)
        gate_pre = times_transpose(scaled, gate_t)
        up_values = times_transpose(scaled, up_t)
        sigmoid = jax.nn.sigmoid(gate_pre)
        silu = gate_pre * sigmoid
        hidden = (silu * up_values).astype(BF16)
        block_out.append(
            (middle + dot(hidden, down).reshape(middle.shape)).astype(BF16)
        )
        grad_hidden = times_transpose(cot_low, down)
        gate_back = (
            grad_hidden * up_values * (sigmoid * (1.0 + gate_pre * (1.0 - sigmoid)))
        ).astype(BF16)
        up_back = (grad_hidden * silu).astype(BF16)
        mid_back = (dot(gate_back, gate_t) + dot(up_back, up_t)).reshape(middle.shape)
        gain_mid_part = gain_mid_part + jnp.sum(mid_back * normed_mid, axis=(0, 1, 2))
        grad = cotangent[part] + norm_backward(mid_back, normed_mid, factor_mid, gain_mid)
        middle_grad.append(grad)
        own_grad = grad.astype(BF16)
        grad_far.append(grid.swap_far(jnp.stack([own_grad] * grid.far)))
        kept.append((scaled, cot_low, hidden, gate_back, up_back))

    scaled, cot_low, hidden, gate_back, up_back = (
        jnp.concatenate(values, axis=0) for values in zip(*kept, strict=True)
    )
    sources = ((gate_back, scaled), (up_back, scaled), (hidden, cot_low))
    middle_unit = hidden.shape[1] // 2
    grads = [
        [contract_rows(left[:, n * middle_unit : (n + 1) * middle_unit], right) for left, right in sources]
        for n in range(2)
    ]
    bits = row_bits()
    kept_grads = [
        stay + swap_rows(away.astype(BF16), bits[0]).astype(F32)
        for stay, away in zip(*grads, strict=True)
    ]

    own = jnp.reshape(index, (1,)).astype(jnp.int32)
    before = ()
    back_partials = []
    ahead = list(kept_grads)
    for c in range(chunks):
        received = near_swaps(grid, grad_far[c])
        if c:
            received = tie_all(received, back_partials[-1][0])
        if c + 1 < chunks:
            ahead.append(grad_far[c + 1])
        pieces = [tie(grad_far[c], *ahead), *received]
        *partial, mixing_sum, lag_sum = mix_sequences_back(
            state_pieces[c], pieces, near, own, turned, u00, u10, lag_count, before
        )
        before = (mixing_sum, lag_sum)
        back_partials.append(partial)
        ahead = []
        if c == 0:
            for n, bit in enumerate(bits[1:]):
                half_count = kept_grads[0].shape[0] // 2
                received = [swap_rows(g[half_count:].astype(BF16), bit) for g in kept_grads]
                if n == 0:
                    received = tie_all(received, partial[0])
                kept_grads = [
                    g[:half_count] + value.astype(F32)
                    for g, value in zip(kept_grads, received, strict=True)
                ]
            filt_grads = jnp.stack(
                [g.astype(BF16).reshape(grid.size, share, width) for g in kept_grads], axis=1
            )
            ahead = [filt_grads]
    near_received = [near_swaps(grid, partial) for partial in back_partials]
    for c in range(chunks - 1):
        near_received[c] = tie_all(near_received[c], back_partials[c + 1][0])
    arrivals = near_received[0] or back_partials[-1][:1]
    filt_grads = tie(
        lax.all_to_all(filt_grads, "filt", 0, 0, tiled=True), back_partials[-1][0]
    )
    mixing_sum, lag_sum = tie_all([mixing_sum, lag_sum], *arrivals)
    near_received[0] = tie_all(near_received[0], filt_grads)
    state_back = []
    for c in range(chunks):
        state_back.append(
            total_of(
                grid.swap_far(total_of([back_partials[c][0], *near_received[c]]).astype(BF16))
            )
        )
    own_grads = jnp.sum(filt_grads.astype(F32), axis=0).astype(BF16)

    doubled = mixing_sum.reshape(slots, 2, width, width)
    mixing_part = jnp.stack(
        [doubled[:, 0] + doubled[:, 1], doubled[:, 0] - doubled[:, 1]], axis=1
    ).reshape(2 * slots, width, width)
    if branches % 2:
        mixing_part = lax.dynamic_slice_in_dim(mixing_part, odd_start, branches, 0)
    mixing_grad = all_reduce_rows(mixing_part)

    slab = width // grid.size
    own_regression = lax.dynamic_slice_in_dim(regression, index * slab, slab, 1)
    gain_lag = jnp.sum(own_regression.astype(F32) * lag_sum, axis=(0, 2))
    gain_in_part = jnp.sum(mixing.astype(F32) * mixing_part, axis=(0, 2))
    gain_in_part = lax.dynamic_update_slice_in_dim(
        gain_in_part,
        lax.dynamic_slice_in_dim(gain_in_part, index * slab, slab, 0) + gain_lag,
        index * slab,
        0,
    ) / gain_in
    gains = jnp.stack([gain_in_part, gain_mid_part])
    small = jnp.concatenate(
        [lag_sum.reshape(lag_count * slab, width), jnp.pad(gains, ((0, 6), (0, 0)))], axis=0
    )
    for bit in row_bits():
        rounded = small[:-8].astype(BF16)
        gain_high = small[-8:].astype(BF16)
        gain_low = (small[-8:] - gain_high.astype(F32)).astype(BF16)
        other = swap_rows(jnp.concatenate([rounded, gain_high, gain_low], axis=0), bit).astype(F32)
        small = small + jnp.concatenate([other[:-16], other[-16:-8] + other[-8:]], axis=0)
    gain_high = small[-8:].astype(BF16)
    gain_low = (small[-8:] - gain_high.astype(F32)).astype(BF16)
    small_low = jnp.concatenate([small[:-8].astype(BF16), gain_high, gain_low], axis=0)
    spread = lax.all_gather(small_low, "filt", axis=0)
    gains = jnp.sum(spread[:, -16:-8].astype(F32) + spread[:, -8:].astype(F32), axis=0)
    regression_grad = (
        spread[:, :-16]
        .reshape(grid.size, lag_count, slab, width)
        .transpose(1, 0, 2, 3)
        .reshape(lag_count, width, width)
        .astype(F32)
    )

    mix_back = jnp.concatenate(middle_grad, axis=0).astype(BF16)
    edge = lax.ppermute(
        mix_back[:, :, :1], "filt", [(f + 1, f) for f in range(grid.size - 1)]
    )
    lag_back = sum(
        jnp.einsum("spae,de->spad", lead, regression[n], preferred_element_type=F32)
        for n, lead in enumerate(leading(mix_back, edge))
    )
    input_grad = []
    for c in range(chunks):
        part = slice(c * step, (c + 1) * step)
        back = state_back[c] + lag_back[part]
        input_grad.append(
            middle_grad[c] + norm_backward(back, normed_in[part], factor_in[part], gain_in)
        )

    full = spread_rows(own_grads)
    row_index = lax.axis_index("rows")
    ordered = jnp.zeros((row_count, 3, share, width), BF16)
    for n, mask in enumerate(row_masks()):
        ordered = lax.dynamic_update_slice_in_dim(ordered, full[n][None], row_index ^ mask, 0)
    ordered = ordered.transpose(1, 0, 2, 3).reshape(3, hidden_own, width).astype(F32)
    return (
        outward(jnp.concatenate(block_out, axis=0)),
        outward(jnp.concatenate(input_grad, axis=0)),
        mixing_grad,
        regression_grad,
        gains[0],
        gains[1],
        ordered[0].T,
        ordered[1].T,
        ordered[2],
    )


def solution(mesh):
    placed = (
        P("filt", "rows", None),
        P(),
        P(),
        P("filt", None, None),
        P(),
        P(),
        P(None, "filt"),
        P(None, "filt"),
        P("filt", None),
        P("filt", "rows", None),
    )
    return jax.shard_map(
        shards,
        mesh=mesh,
        in_specs=placed,
        out_specs=(
            P("filt", "rows", None),
            P("filt", "rows", None),
            P("filt", None, None),
            P(),
            P(),
            P(),
            P(None, "filt"),
            P(None, "filt"),
            P("filt", None),
        ),
        check_vma=False,
    )
```

```python
import functools

import jax
import jax.numpy as jnp
from jax import lax
from jax.experimental import pallas as pl
from jax.experimental.pallas import tpu as pltpu
from jax.sharding import PartitionSpec as P

EPSILON = 1e-05
CHUNKS = 2
F32 = jnp.float32
BF16 = jnp.bfloat16


def dot(left, right):
    return jnp.dot(left, right, preferred_element_type=F32)


def contract_rows(left, right):
    return lax.dot_general(left, right, (((0,), (0,)), ((), ())), preferred_element_type=F32)


def times_transpose(left, right):
    return lax.dot_general(left, right, (((1,), (1,)), ((), ())), preferred_element_type=F32)


def rms_factor(values):
    return lax.rsqrt(jnp.mean(values * values, axis=-1, keepdims=True) + EPSILON)


def norm_backward(grad_out, normed, factor, gain):
    inner = grad_out * gain
    return factor * (inner - normed * jnp.mean(inner * normed, axis=-1, keepdims=True))


class Grid:
    def __init__(self, size):
        self.far = 4 if size % 4 == 0 else 1
        self.near = size // self.far
        self.size = size

    def near_shift(self, step):
        near = self.near
        return [(f, f // near * near + (f % near + step) % near) for f in range(self.size)]

    def swap_far(self, values):
        groups = [
            [i * self.near + j for i in range(self.far)] for j in range(self.near)
        ]
        return lax.all_to_all(values, "filt", 0, 0, axis_index_groups=groups, tiled=True)


def tie(value, *others):
    return lax.optimization_barrier((value, *others))[0] if others else value


def tied(*values):
    return list(lax.optimization_barrier(values))


def copies(grid, own):
    return jnp.broadcast_to(own[None], (grid.far, *own.shape))


def tie_all(values, *others):
    count = len(values)
    return list(lax.optimization_barrier((*values, *others))[:count]) if others else list(values)


def near_swaps(grid, values):
    return [
        lax.ppermute(
            values[j] if isinstance(values, list) else values, "filt", grid.near_shift(j)
        )
        for j in range(1, grid.near)
    ]


def total_of(values):
    total = values[0].astype(F32)
    for value in values[1:]:
        total = total + value.astype(F32)
    return total


def swap_rows(values, bit):
    count = lax.axis_size("rows")
    return lax.ppermute(values, "rows", [(r, r ^ bit) for r in range(count)])


def row_bits():
    count = lax.axis_size("rows")
    return [1 << n for n in range(count.bit_length() - 1)]


def row_step(values, bit):
    parts, height, width = values.shape
    halves = values.reshape(parts, 2, height // 2, width)
    high = (lax.axis_index("rows") & bit) != 0
    away = jnp.where(high, halves[:, 0], halves[:, 1]).astype(BF16)
    return jnp.where(high, halves[:, 1], halves[:, 0]), swap_rows(away, bit)


def gather_rows(full):
    index = lax.axis_index("rows")
    for bit in reversed(row_bits()):
        high = (index & bit) != 0
        other = swap_rows(full, bit)
        full = jnp.concatenate(
            [jnp.where(high, other, full), jnp.where(high, full, other)], axis=1
        )
    return full


def gather_near(grid, own):
    at = lax.axis_index("filt") % grid.near
    whole = jnp.zeros((grid.near, *own.shape), own.dtype)
    for j, value in enumerate([own, *near_swaps(grid, own)]):
        place = lax.rem(at - j + grid.near, grid.near)
        whole = lax.dynamic_update_slice_in_dim(whole, value[None], place, 0)
    return whole


def all_sum(values):
    for axis in ("filt", "rows"):
        count = lax.axis_size(axis)
        for bit in (1 << n for n in range(count.bit_length() - 1)):
            values = values + lax.ppermute(values, axis, [(r, r ^ bit) for r in range(count)])
    return values


def toeplitz_kernel(half, count, up_ref, t00_ref, t10_ref, u00_ref, u10_ref):
    width = up_ref.shape[-1]
    step = pl.program_id(0)
    up = up_ref[0]
    first = lax.broadcasted_iota(jnp.int32, up.shape, 1) == 0
    late = jnp.where(first, 0.0, pltpu.roll(up, 1, axis=1))
    up = jnp.where((step < 2 * count) & (step % 2 == 1), late, up)
    block = pltpu.roll(
        jnp.broadcast_to(up, (half, width)), 0, axis=1, stride=1, stride_axis=0
    )
    u00, u10 = block[:, :half], block[:, half : 2 * half]
    u00_ref[0] = u00.astype(BF16)
    u10_ref[0] = u10.astype(BF16)
    t00_ref[0] = u00.T.astype(BF16)
    t10_ref[0] = u10.T.astype(BF16)


def toeplitz_blocks(filters, first, count):
    length = filters.shape[1] // 2
    half = length // 2
    taps = lax.dynamic_slice_in_dim(filters, first, count, 0).astype(BF16).astype(F32)
    taps = taps.reshape(count, length, 2).transpose(0, 2, 1).reshape(2 * count, 1, length)
    up = jnp.pad(taps, ((0, 0), (0, 0), (0, length)))
    by_column = pl.BlockSpec((1, half, half), lambda n: (n // (2 * count), 0, n % (2 * count)))
    by_row = pl.BlockSpec((1, half, half), lambda n: (n // (2 * count), n % (2 * count), 0))
    line = pl.BlockSpec((1, 1, 2 * length), lambda n: (n % (2 * count), 0, 0))
    wide = jax.ShapeDtypeStruct((2, half, 2 * count * half), BF16)
    tall = jax.ShapeDtypeStruct((2, 2 * count * half, half), BF16)
    return pl.pallas_call(
        functools.partial(toeplitz_kernel, half, count),
        grid=(4 * count,),
        in_specs=[line],
        out_specs=[by_column, by_column, by_row, by_row],
        out_shape=[wide, wide, tall, tall],
        name="toeplitz",
    )(up)


def places(near, pieces, whole_ref, sign):
    length = whole_ref.shape[0] // 2
    nears = len(pieces)
    fars, _, _, height, _ = pieces[0].shape
    for j, piece in enumerate(pieces):
        at = lax.rem(near + sign * j + nears, nears)
        for i in range(fars):
            for parity in range(2):
                start = parity * length + (i * nears + at) * height
                yield piece.at[i, 0, parity], pl.ds(pl.multiple_of(start, height), height)


def assemble(near, pieces, whole_ref):
    for piece, rows in places(near, pieces, whole_ref, -1):
        whole_ref[rows, :] = piece[...]


def scatter(near, whole_ref, pieces):
    for piece, rows in places(near, pieces, whole_ref, 1):
        piece[...] = whole_ref[rows, :].astype(piece.dtype)


def mix_kernel(parts, near_ref, *refs):
    pieces = refs[:parts]
    mixes = refs[parts : parts + 2]
    t00_ref, t10_ref = refs[parts + 2 : parts + 4]
    outs = refs[-parts - 5 : -5]
    flip_ref, states_ref, low_ref, high_ref, sum_ref = refs[-5:]
    half = t00_ref.shape[1]
    branches = 2 * mixes[0].shape[0]
    assemble(near_ref[0], pieces, states_ref)

    for branch in range(branches):
        slot = pl.ds(branch * half, half)
        for quarter in range(4):
            value = dot(
                states_ref[pl.ds(quarter * half, half), :], mixes[branch % 2][branch // 2]
            ).astype(BF16)
            target = (quarter // 2) ^ (branch % 2)
            (low_ref, high_ref)[quarter % 2][target, slot, :] = value

    for parity in range(2):
        base = 2 * parity * half
        sum_ref[pl.ds(base, half), :] = dot(t00_ref[parity], low_ref[parity]).astype(
            sum_ref.dtype
        )
        sum_ref[pl.ds(base + half, half), :] = (
            dot(t10_ref[parity], low_ref[parity]) + dot(t00_ref[parity], high_ref[parity])
        ).astype(sum_ref.dtype)
    scatter(near_ref[0], sum_ref, outs)
    flip_ref[0] = states_ref[...].T


def mix_back_kernel(parts, near_ref, own_ref, *refs):
    pieces = refs[:parts]
    turned = refs[parts : parts + 2]
    u00_ref, u10_ref, slab_ref = refs[parts + 2 : parts + 5]
    before = refs[parts + 5 : -parts - 4]
    outs = refs[-parts - 4 : -4]
    back_ref, lag_ref, grad_ref, sum_ref = refs[-4:]
    half = u00_ref.shape[2]
    width = grad_ref.shape[1]
    length = grad_ref.shape[0] // 2
    branches = back_ref.shape[2] // width
    slots = branches // 2

    @pl.when(pl.program_id(0) == 0)
    def _():
        lag_ref[...] = before[1][...] if before else jnp.zeros_like(lag_ref)

    assemble(near_ref[0], pieces, grad_ref)

    for parity in range(2):
        base = 2 * parity * half
        low = grad_ref[pl.ds(base, half), :]
        high = grad_ref[pl.ds(base + half, half), :]
        for branch in range(branches):
            rows = pl.ds(branch * half, half)
            columns = pl.ds((branch % 2 * slots + branch // 2) * width, width)
            target = 2 * half * (parity ^ (branch % 2))
            back_ref[0, pl.ds(target, half), columns] = (
                dot(u00_ref[parity, rows, :], low) + dot(u10_ref[parity, rows, :], high)
            ).astype(BF16)
            back_ref[0, pl.ds(target + half, half), columns] = dot(
                u00_ref[parity, rows, :], high
            ).astype(BF16)

    for quarter in range(4):
        rows = pl.ds(quarter * half, half)
        sum_ref[rows, :] = dot(back_ref[0, rows, : slots * width], turned[0][...]) + dot(
            back_ref[0, rows, slots * width :], turned[1][...]
        )
    scatter(near_ref[0], sum_ref, outs)

    own = slab_ref[0].astype(F32)
    even, odd = own[:, :length], own[:, length:]
    first = lax.broadcasted_iota(jnp.int32, even.shape, 1) == 0
    even_late = jnp.where(first, 0.0, pltpu.roll(even, 1, axis=1))
    odd_late = jnp.where(first, 0.0, pltpu.roll(odd, 1, axis=1))
    for lag, (on_even, on_odd) in enumerate(
        ((even, odd), (odd_late, even), (even_late, odd_late))
    ):
        lag_ref[lag] += dot(on_even.astype(BF16), grad_ref[:length, :]) + dot(
            on_odd.astype(BF16), grad_ref[length:, :]
        )


def feed_forward_kernel(
    shares, earlier, last, arrived, inputs, states, late, lag_ref, gain_ref, cot_ref, *refs
):
    weights = refs[:shares]
    saved = refs[shares : shares + 5 * earlier]
    block, grad, low, gain_out, *rest = refs[shares + 5 * earlier :]
    if last:
        stay_ref, away_ref = rest
    else:
        scaled_ref, hidden_ref, gate_ref, up_ref = rest
    width = gain_ref.shape[1]
    shape = inputs.shape
    flat = (shape[0] * shape[1] * shape[2], width)

    spectral = arrived[0].astype(F32)
    for i in range(1, arrived.shape[0]):
        spectral = spectral + arrived[i].astype(F32)
    lags = (
        states[...],
        jnp.stack([late[:, 1], states[:, 0]], axis=1),
        late[...],
    )
    regress = sum(dot(lag.reshape(flat), lag_ref[n]) for n, lag in enumerate(lags))
    middle = (inputs[...].astype(F32) + spectral).reshape(flat) + regress
    factor = rms_factor(middle)
    normed = middle * factor
    gain = gain_ref[...]
    scaled = (normed * gain).astype(BF16)
    if not last:
        scaled_ref[...] = scaled
    cot = cot_ref[...].reshape(flat)
    value = middle
    mid_back = jnp.zeros(flat, F32)
    for n, weight in enumerate(weights):
        units = weight.shape[0] * weight.shape[2]
        columns = pl.ds(n * units, units)
        gate_t, up_t, down = (weight[:, m].reshape(units, width) for m in range(3))
        gate_pre = times_transpose(scaled, gate_t)
        up_values = times_transpose(scaled, up_t)
        grad_hidden = times_transpose(cot, down)
        sigmoid = 1.0 / (1.0 + jnp.exp(-gate_pre))
        silu = gate_pre * sigmoid
        hidden = (silu * up_values).astype(BF16)
        gate_back = (
            grad_hidden * up_values * (sigmoid * (1.0 + gate_pre * (1.0 - sigmoid)))
        ).astype(BF16)
        up_back = (grad_hidden * silu).astype(BF16)
        if last:
            sums = [
                contract_rows(gate_back, scaled),
                contract_rows(up_back, scaled),
                contract_rows(hidden, cot),
            ]
            for e in range(earlier):
                *parts, right, right_cot = saved[5 * e : 5 * e + 5]
                right_cot = right_cot[...].reshape(-1, width)
                for m, part in enumerate(parts):
                    sums[m] += contract_rows(
                        part[:, columns], right_cot if m == 2 else right[...]
                    )
            for m in range(3):
                split = (weight.shape[0], weight.shape[2], width)
                if n < shares // 2 or shares == 1:
                    stay_ref[n, :, m] = sums[m].reshape(split)
                else:
                    away_ref[n - shares // 2, :, m] = sums[m].astype(BF16).reshape(split)
        else:
            hidden_ref[:, columns] = hidden
            gate_ref[:, columns] = gate_back
            up_ref[:, columns] = up_back
        value = value + dot(hidden, down)
        mid_back = mid_back + (dot(gate_back, gate_t) + dot(up_back, up_t))
    block[...] = value.astype(BF16).reshape(shape)
    gain_out[...] = jnp.sum(mid_back * normed, axis=0, keepdims=True)
    total = cot.astype(F32) + norm_backward(mid_back, normed, factor, gain)
    grad[...] = total.reshape(shape)
    rounded = total.astype(BF16).reshape(shape)
    for i in range(low.shape[0]):
        low[i] = rounded


def mixing_kernel(
    bit_ref, flip_ref, plus_ref, minus_ref, sum_ref, rest_ref, stay_ref, away_ref, gain_ref
):
    rows = stay_ref.shape[1]

    @pl.when(pl.program_id(0) == 0)
    def _():
        gain_ref[...] = jnp.zeros_like(gain_ref)

    for n, out_ref in enumerate((stay_ref, away_ref)):
        here = pl.ds(pl.multiple_of((bit_ref[0] ^ n) * rows, rows), rows)
        plus, minus = (
            sum(dot(flip_ref[s, here, :], ref[s]) for s in range(flip_ref.shape[0]))
            for ref in (plus_ref, minus_ref)
        )
        out_ref[0] = (plus + minus).astype(out_ref.dtype)
        out_ref[1] = (plus - minus).astype(out_ref.dtype)
        gain_ref[here, :] += jnp.sum(
            plus * sum_ref[0, here, :].astype(F32) + minus * rest_ref[0, here, :].astype(F32),
            axis=1,
            keepdims=True,
        )


def resident(shape):
    zeros = (0,) * len(shape)
    return pl.BlockSpec(shape, lambda *_: zeros, pipeline_mode=pl.Buffered(1))


def mix_sequences(pieces, near, pairs, t00, t10, start, total, flips):
    parts = len(pieces)
    fars, count, _, height, width = pieces[0].shape
    half = t00.shape[1]
    block = pl.BlockSpec((fars, 1, 2, height, width), lambda n, *_: (0, n, 0, 0, 0))
    rows = t00.shape[2]
    flip = pl.BlockSpec((1, width, 4 * half), lambda n, *_: (start + n, 0, 0))
    return pl.pallas_call(
        functools.partial(mix_kernel, parts),
        grid_spec=pltpu.PrefetchScalarGridSpec(
            num_scalar_prefetch=1,
            grid=(count,),
            in_specs=[block] * parts
            + [resident(a.shape) for a in (*pairs, t00, t10)]
            + [pl.BlockSpec(memory_space=pl.ANY)] * len(flips),
            out_specs=[block] * parts + [flip],
            scratch_shapes=[
                pltpu.VMEM((4 * half, width), BF16),
                pltpu.VMEM((2, rows, width), BF16),
                pltpu.VMEM((2, rows, width), BF16),
                pltpu.VMEM((4 * half, width), F32),
            ],
        ),
        out_shape=[jax.ShapeDtypeStruct(pieces[0].shape, BF16)] * parts
        + [jax.ShapeDtypeStruct((total, width, 4 * half), BF16)],
        input_output_aliases={parts + 5: parts} if flips else {},
        compiler_params=pltpu.CompilerParams(vmem_limit_bytes=48 << 20),
        cost_estimate=pl.CostEstimate(
            flops=count * (16 * half * pairs[0].size + 12 * half * rows * width),
            bytes_accessed=4 * parts * pieces[0].size + 4 * pairs[0].size + 4 * t00.size,
            transcendentals=0,
        ),
        name="mix",
    )(near, *pieces, *pairs, t00, t10, *flips)


def mix_sequences_back(pieces, near, own, turned, u00, u10, lag_count, start, flips, before):
    parts = len(pieces)
    fars, count, _, height, width = pieces[0].shape
    half = u00.shape[2]
    block = pl.BlockSpec((fars, 1, 2, height, width), lambda n, *_: (0, n, 0, 0, 0))
    rows = u00.shape[1]
    slab = width // (parts * fars)
    lag_shape = (lag_count, slab, width)
    back_shape = (flips.shape[0], 4 * half, 2 * turned[0].shape[0])
    back = pl.BlockSpec((1, *back_shape[1:]), lambda n, *_: (start + n, 0, 0))
    slab_spec = pl.BlockSpec((1, slab, 4 * half), lambda n, _, own: (start + n, own[0], 0))
    return pl.pallas_call(
        functools.partial(mix_back_kernel, parts),
        grid_spec=pltpu.PrefetchScalarGridSpec(
            num_scalar_prefetch=2,
            grid=(count,),
            in_specs=[block] * parts
            + [resident(a.shape) for a in (*turned, u00, u10)]
            + [slab_spec]
            + ([pl.BlockSpec(memory_space=pl.ANY), resident(lag_shape)] if before else []),
            out_specs=[block] * parts + [back, resident(lag_shape)],
            scratch_shapes=[
                pltpu.VMEM((4 * half, width), BF16),
                pltpu.VMEM((4 * half, width), F32),
            ],
        ),
        out_shape=[jax.ShapeDtypeStruct(pieces[0].shape, BF16)] * parts
        + [
            jax.ShapeDtypeStruct(back_shape, BF16),
            jax.ShapeDtypeStruct(lag_shape, F32),
        ],
        input_output_aliases={parts + 7: parts} if before else {},
        compiler_params=pltpu.CompilerParams(vmem_limit_bytes=56 << 20),
        cost_estimate=pl.CostEstimate(
            flops=count * (16 * half * turned[0].size + 12 * half * rows * width),
            bytes_accessed=4 * parts * pieces[0].size + 8 * turned[0].size,
            transcendentals=0,
        ),
        name="mix_back",
    )(near, own, *pieces, *turned, u00, u10, flips, *before)


def mixing_products(flips, backs, pairs, bit):
    count, width, length = flips.shape
    slots = pairs[0].shape[0]
    plus = pl.BlockSpec((count, length, width), lambda k, _: (0, 0, k))
    minus = pl.BlockSpec((count, length, width), lambda k, _: (0, 0, slots + k))
    pair = pl.BlockSpec((1, width, width), lambda k, _: (k, 0, 0))
    half = pl.BlockSpec((2, width // 2, width), lambda k, _: (k, 0, 0))
    return pl.pallas_call(
        mixing_kernel,
        grid_spec=pltpu.PrefetchScalarGridSpec(
            num_scalar_prefetch=1,
            grid=(slots,),
            in_specs=[resident(flips.shape), plus, minus, pair, pair],
            out_specs=[half, half, resident((width, 1))],
        ),
        out_shape=[
            jax.ShapeDtypeStruct((2 * slots, width // 2, width), F32),
            jax.ShapeDtypeStruct((2 * slots, width // 2, width), BF16),
            jax.ShapeDtypeStruct((width, 1), F32),
        ],
        compiler_params=pltpu.CompilerParams(vmem_limit_bytes=56 << 20),
        cost_estimate=pl.CostEstimate(
            flops=2 * backs.size * width,
            bytes_accessed=2 * (flips.size + backs.size) + 8 * slots * width * width,
            transcendentals=0,
        ),
        name="mixing_products",
    )(bit, flips, backs, backs, *pairs)


def feed_forward(arrived, inputs, states, late, lag, gain, cot, weights, saved, last):
    rows, width = inputs.size // inputs.shape[-1], inputs.shape[-1]
    shares = len(weights)
    units = weights[0].shape[0] * weights[0].shape[2]
    flat_saved = [value for values in saved for value in values] if last else []
    operands = (arrived, inputs, states, late, lag, gain, cot, *weights, *flat_saved)
    whole = pl.BlockSpec(memory_space=pltpu.VMEM)
    kept = max(shares // 2, 1)
    if last:
        extra = [
            jax.ShapeDtypeStruct((kept, *weights[0].shape), F32),
            jax.ShapeDtypeStruct((kept, *weights[0].shape), BF16),
        ]
    else:
        extra = [jax.ShapeDtypeStruct((rows, width), BF16)] + [
            jax.ShapeDtypeStruct((rows, shares * units), BF16)
        ] * 3
    return pl.pallas_call(
        functools.partial(feed_forward_kernel, shares, len(flat_saved) // 5, last),
        in_specs=[whole] * len(operands),
        out_specs=[whole] * (4 + len(extra)),
        out_shape=[
            jax.ShapeDtypeStruct(inputs.shape, BF16),
            jax.ShapeDtypeStruct(inputs.shape, F32),
            jax.ShapeDtypeStruct(arrived.shape, BF16),
            jax.ShapeDtypeStruct((1, width), F32),
            *extra,
        ],
        compiler_params=pltpu.CompilerParams(vmem_limit_bytes=56 << 20),
        cost_estimate=pl.CostEstimate(
            flops=(24 if last else 12) * rows * width * shares * units,
            bytes_accessed=6 * shares * units * width + 40 * rows * width,
            transcendentals=rows * shares * units,
        ),
        name="feed_forward",
    )(*operands)


def leading(values, edge):
    early = jnp.concatenate([values[:, :, 1:], edge], axis=2)
    return values, jnp.stack([values[:, 1], early[:, 0]], axis=1), early


def row_masks():
    masks = [0]
    for bit in reversed(row_bits()):
        masks = masks + [mask ^ bit for mask in masks]
    return masks


def spread_rows(own):
    full = own[None]
    for bit in reversed(row_bits()):
        full = jnp.concatenate([full, swap_rows(full, bit)], axis=0)
    return full


def shards(inputs, filters, gain_in, mixing, regression, gain_mid, w_gate, w_up, w_down, out_grad):
    shard_rows, local_seqs, width = inputs.shape
    grid = Grid(lax.axis_size("filt"))
    row_count = lax.axis_size("rows")
    index = lax.axis_index("filt")
    branches = mixing.shape[0]
    lag_count = regression.shape[0]
    height = shard_rows // 2
    chunks = CHUNKS
    step = local_seqs // chunks

    def inward(values):
        return values.reshape(height, 2, local_seqs, width).transpose(2, 1, 0, 3)

    def outward(values):
        return values.transpose(2, 1, 0, 3).reshape(shard_rows, local_seqs, width)

    def cut(values):
        return [values[c * step : (c + 1) * step] for c in range(chunks)]

    inputs_low = inward(inputs)
    residual = inputs_low.astype(F32)
    cotangent_low = inward(out_grad)
    factor_in = rms_factor(residual)
    normed_in = residual * factor_in
    states = (normed_in * gain_in).astype(BF16)
    hidden_own = w_down.shape[0]
    share = hidden_own // row_count
    packed = jnp.stack([w_gate.T, w_up.T, w_down]).reshape(3, row_count, share, width)
    own_share = lax.dynamic_index_in_dim(packed, lax.axis_index("rows"), 1, keepdims=False)
    near_shares = gather_near(grid, own_share)

    slots = (branches + 1) // 2
    first_branch = index * branches
    t00, t10, u00, u10 = toeplitz_blocks(filters, first_branch // 2, slots)
    if branches % 2:
        odd_start = first_branch % 2
        paired = lax.dynamic_update_slice_in_dim(
            jnp.zeros((2 * slots,) + mixing.shape[1:], mixing.dtype), mixing, odd_start, 0
        )
    else:
        paired = mixing
    first, second = (paired[n::2].astype(F32) for n in range(2))
    pairs = ((first + second).astype(BF16), (first - second).astype(BF16))

    near = jnp.reshape(index % grid.near, (1,)).astype(jnp.int32)

    edge = lax.ppermute(
        states[:, :, -1:], "filt", [(f, f + 1) for f in range(grid.size - 1)]
    )
    late = jnp.concatenate([edge, states[:, :, :-1]], axis=2)
    partials, flips = [], []
    ready = [late, inputs_low, cotangent_low, t00, t10, u00, u10, *pairs, copies(grid, near_shares)]
    state_far = []
    for c, part in enumerate(cut(states)):
        if c:
            part = tie(part, state_far[-1])
        state_far.append(grid.swap_far(copies(grid, part)))
        if c == 0:
            state_far[0], *ready = tied(state_far[0], *ready)
    late, inputs_low, cotangent_low, t00, t10, u00, u10, *pairs, shares = ready
    state_far[-1], shares = tied(state_far[-1], shares)
    shares = grid.swap_far(shares)
    state_near = [near_swaps(grid, values) for values in state_far]
    for c in range(chunks):
        pieces = [state_far[c], *state_near[c]]
        ahead = [] if c else state_far[1:]
        pieces = [tie(pieces[0], *ahead), *pieces[1:]]
        *partial, flip = mix_sequences(
            pieces, near, pairs, t00, t10, c * step, local_seqs, flips
        )
        if c + 1 < chunks:
            state_near[c + 1] = tie_all(state_near[c + 1], partial[0])
            partial = tie_all(partial, *state_near[c + 1])
        partials.append(partial)
        flips = [flip]
    near_received = [near_swaps(grid, partial) for partial in partials]
    for c in range(chunks - 1):
        near_received[c] = tie_all(near_received[c], partials[c + 1][0])
    weights = [tie(shares, partials[0][0]).reshape(grid.size, 3, share, width)]
    for n, bit in enumerate(reversed(row_bits())):
        received = [swap_rows(weight, bit) for weight in weights]
        if n == 0:
            received = tie_all(received, *(near_received[-1] or partials[-1][:1]))
        weights = weights + received

    spectral = []
    for c in range(chunks):
        spectral.append(
            grid.swap_far(total_of([partials[c][0], *near_received[c]]).astype(BF16))
        )

    block_out, middle_grad, lows, grad_far, kept = [], [], [], [], []
    gain_mid_part = jnp.zeros((1, width), F32)
    for c in range(chunks):
        part = slice(c * step, (c + 1) * step)
        arrived = spectral[c]
        if c:
            arrived = tie(arrived, middle_grad[-1])
        if c + 1 < chunks:
            arrived = tie(arrived, *near_received[c + 1])
        if c == chunks - 1:
            turned = [
                value.transpose(0, 2, 1).reshape(slots * width, width)
                for value in (tie_all(pairs, middle_grad[-1]) if c else pairs)
            ]
            arrived = tie(arrived, *turned)
        cot = cotangent_low[part]
        value, grad, low, gain_part, *rest = feed_forward(
            arrived, inputs_low[part], states[part], late[part], regression, gain_mid[None], cot,
            weights, kept, c + 1 == chunks,
        )
        block_out.append(value)
        middle_grad.append(grad)
        lows.append(low[0])
        gain_mid_part = gain_mid_part + gain_part
        grad_far.append(grid.swap_far(low))
        if c + 1 < chunks:
            scaled, hidden, gate_back, up_back = rest
            kept.append((gate_back, up_back, hidden, scaled, cot))
    gain_mid_part = gain_mid_part[0]

    bits = row_bits()
    stay, away = tie_all(rest, grad_far[0]) if chunks > 1 else rest
    grad_near = [near_swaps(grid, values) for values in grad_far]
    if bits:
        value = swap_rows(away, bits[0])
        value, *grad_near[0] = tied(value, *grad_near[0])
        stay = stay + value.astype(F32)

    own = jnp.reshape(index, (1,)).astype(jnp.int32)
    before = ()
    back_partials = []
    mix_back = jnp.concatenate(lows, axis=0)
    next_edge = lax.ppermute(
        mix_back[:, :, :1], "filt", [(f + 1, f) for f in range(grid.size - 1)]
    )
    grad_far[0], stay, next_edge = tied(grad_far[0], stay, next_edge)
    ahead = []
    for c in range(chunks):
        received = grad_near[c]
        if c + 1 < chunks:
            ahead.append(grad_far[c + 1])
        pieces = [tie(grad_far[c], *ahead), *received]
        *partial, backs, lag_sum = mix_sequences_back(
            pieces, near, own, turned, u00, u10, lag_count, c * step, flip, before
        )
        before = (backs, lag_sum)
        if c + 1 < chunks:
            grad_near[c + 1] = tie_all(grad_near[c + 1], partial[0])
            partial = tie_all(partial, *grad_near[c + 1])
        back_partials.append(partial)
        ahead = []
    near_received = [near_swaps(grid, partial) for partial in back_partials]
    near_received[0] = tie_all(near_received[0], back_partials[-1][0])
    columns = [total_of([back_partials[0][0], *near_received[0]]).astype(BF16)]
    later = bits[1:2]
    half_count = stay.shape[0] // 2
    from_rows = [swap_rows(stay[half_count:].astype(BF16), bit) for bit in later]
    kept, value = row_step(tie(lag_sum, columns[0]), bits[0])
    lag_share = kept + value.astype(F32)
    core_bit = jnp.reshape(lax.axis_index("rows") & 1, (1,)).astype(jnp.int32)
    mixing_stay, mixing_away, gain_column = mixing_products(
        flip, tie(backs, columns[0], *from_rows, lag_share), pairs, core_bit
    )
    for bit in later:
        kept, value = row_step(lag_share, bit)
        lag_share = kept + tie(value, gain_column).astype(F32)
    for c in range(1, chunks):
        received = tie_all(near_received[c], gain_column)
        columns.append(total_of([back_partials[c][0], *received]).astype(BF16))
    arrived = [grid.swap_far(column) for column in columns]
    arrived[0], mixing_stay, mixing_away = tie_all(
        [arrived[0], mixing_stay, mixing_away], *columns[1:]
    )
    state_back = [total_of(values) for values in arrived]

    mixing_share = mixing_stay + swap_rows(mixing_away, bits[0]).astype(F32)
    mixing_share, stay = tied(mixing_share, stay)
    value = mixing_away
    for bit in bits[1:]:
        kept, value = row_step(mixing_share, bit)
        mixing_share = kept + value.astype(F32)
    row_done = value
    mixing_low, gain_column, gain_mid_part, lag_sum, lag_share, mix_back, next_edge, *block_out = (
        tied(
            mixing_share.astype(BF16), gain_column, gain_mid_part, lag_sum, lag_share, mix_back,
            next_edge, *block_out,
        )
    )
    mixing_grad = gather_rows(mixing_low).astype(F32)
    if branches % 2:
        mixing_grad = lax.dynamic_slice_in_dim(mixing_grad, odd_start, branches, 0)

    slab = width // grid.size
    own_regression = lax.dynamic_slice_in_dim(regression, index * slab, slab, 1)
    gain_lag = jnp.sum(own_regression.astype(F32) * lag_sum, axis=(0, 2))
    gain_in_part = gain_column[:, 0]
    gain_in_part = lax.dynamic_update_slice_in_dim(
        gain_in_part,
        lax.dynamic_slice_in_dim(gain_in_part, index * slab, slab, 0) + gain_lag,
        index * slab,
        0,
    ) / gain_in
    gains = all_sum(jnp.pad(jnp.stack([gain_in_part, gain_mid_part]), ((0, 6), (0, 0))))

    for value in from_rows:
        stay = stay[:half_count] + value.astype(F32)
    for bit in bits[2:]:
        half_count = stay.shape[0] // 2
        value = swap_rows(stay[half_count:].astype(BF16), bit)
        stay = stay[:half_count] + value.astype(F32)
        kept, value = row_step(lag_share, bit)
        lag_share = kept + value.astype(F32)
    by_filt = stay[0].reshape(grid.far, grid.near, 3, share, width)
    at = index % grid.near
    away = [
        lax.dynamic_index_in_dim(by_filt, lax.rem(at + j, grid.near), 1, keepdims=False)
        for j in range(grid.near)
    ]
    returned = near_swaps(grid, [part.astype(BF16) for part in away])
    far_grads = total_of([away[0], *tie_all(returned, row_done)]).astype(BF16)
    far_grads = grid.swap_far(tie(far_grads, arrived[-1]))
    own_grads = total_of(far_grads).astype(BF16)

    lag_share = copies(grid, gather_near(grid, lag_share.astype(BF16)))
    spread = grid.swap_far(tie(lag_share, far_grads))
    spread = gather_rows(spread.reshape(grid.size * lag_count, -1, width))
    regression_grad = (
        spread.reshape(grid.size, lag_count, slab, width)
        .transpose(1, 0, 2, 3)
        .reshape(lag_count, width, width)
        .astype(F32)
    )

    lag_back = sum(
        jnp.einsum("spae,de->spad", lead, regression[n], preferred_element_type=F32)
        for n, lead in enumerate(leading(mix_back, next_edge))
    )
    input_grad = []
    for c in range(chunks):
        part = slice(c * step, (c + 1) * step)
        back = state_back[c] + lag_back[part]
        input_grad.append(
            middle_grad[c] + norm_backward(back, normed_in[part], factor_in[part], gain_in)
        )

    full = spread_rows(own_grads)
    row_index = lax.axis_index("rows")
    ordered = jnp.zeros((row_count, 3, share, width), BF16)
    for n, mask in enumerate(row_masks()):
        ordered = lax.dynamic_update_slice_in_dim(ordered, full[n][None], row_index ^ mask, 0)
    ordered = ordered.transpose(1, 0, 2, 3).reshape(3, hidden_own, width).astype(F32)
    return (
        outward(jnp.concatenate(block_out, axis=0)),
        outward(jnp.concatenate(input_grad, axis=0)),
        mixing_grad,
        regression_grad,
        gains[0],
        gains[1],
        ordered[0].T,
        ordered[1].T,
        ordered[2],
    )


def solution(mesh):
    placed = (
        P("filt", "rows", None),
        P(),
        P(),
        P("filt", None, None),
        P(),
        P(),
        P(None, "filt"),
        P(None, "filt"),
        P("filt", None),
        P("filt", "rows", None),
    )
    return jax.shard_map(
        shards,
        mesh=mesh,
        in_specs=placed,
        out_specs=(
            P("filt", "rows", None),
            P("filt", "rows", None),
            P("filt", None, None),
            P(),
            P(),
            P(),
            P(None, "filt"),
            P(None, "filt"),
            P("filt", None),
        ),
        check_vma=False,
    )
```

```python
import functools

import jax
import jax.numpy as jnp
from jax import lax
from jax.experimental import pallas as pl
from jax.experimental.pallas import tpu as pltpu
from jax.sharding import PartitionSpec as P

EPSILON = 1e-05
CHUNKS = 2
F32 = jnp.float32
BF16 = jnp.bfloat16


def dot(left, right):
    return jnp.dot(left, right, preferred_element_type=F32)


def contract_rows(left, right):
    return lax.dot_general(left, right, (((0,), (0,)), ((), ())), preferred_element_type=F32)


def times_transpose(left, right):
    return lax.dot_general(left, right, (((1,), (1,)), ((), ())), preferred_element_type=F32)


def rms_factor(values):
    return lax.rsqrt(jnp.mean(values * values, axis=-1, keepdims=True) + EPSILON)


def norm_backward(grad_out, normed, factor, gain):
    inner = grad_out * gain
    return factor * (inner - normed * jnp.mean(inner * normed, axis=-1, keepdims=True))


class Grid:
    def __init__(self, size):
        self.size = size
        self.near = size // 4
        self.mate = self.near
        self.far = 2 * self.near

    def near_bits(self):
        return [1 << n for n in range(self.near.bit_length() - 1)]

    def near_shift(self, step):
        near = self.near
        return [(f, f // near * near + (f % near + step) % near) for f in range(self.size)]

    def flag(self, bit):
        return (lax.axis_index("filt") & bit) != 0

    def swap(self, values, bit):
        return lax.ppermute(values, "filt", [(f, f ^ bit) for f in range(self.size)])

    def split(self, halves, bit):
        flag = self.flag(bit)
        return jnp.where(flag, halves[1], halves[0]), jnp.where(flag, halves[0], halves[1])

    def join(self, own, other, bit):
        return jnp.where(self.flag(bit), jnp.stack([other, own]), jnp.stack([own, other]))

    def spread_bits(self):
        return [self.far, self.mate, *self.near_bits()]


def gather_filt(grid, values):
    for bit in grid.spread_bits():
        values = grid.join(values, grid.swap(values, bit), bit)
    return values


def reduce_filt(grid, values, bits):
    for bit in bits:
        own, away = grid.split(values, bit)
        values = own.astype(F32) + grid.swap(away.astype(BF16), bit).astype(F32)
    return values


def tie(value, *others):
    return lax.optimization_barrier((value, *others))[0] if others else value


def tied(*values):
    return list(lax.optimization_barrier(values))


def tie_all(values, *others):
    count = len(values)
    return list(lax.optimization_barrier((*values, *others))[:count]) if others else list(values)


def near_swaps(grid, values):
    return [
        lax.ppermute(
            values[j] if isinstance(values, list) else values, "filt", grid.near_shift(j)
        )
        for j in range(1, grid.near)
    ]


def total_of(values):
    total = values[0].astype(F32)
    for value in values[1:]:
        total = total + value.astype(F32)
    return total


def swap_rows(values, bit):
    count = lax.axis_size("rows")
    return lax.ppermute(values, "rows", [(r, r ^ bit) for r in range(count)])


def row_bits():
    count = lax.axis_size("rows")
    return [1 << n for n in range(count.bit_length() - 1)]


def row_halves(values, bit):
    parts, height, width = values.shape
    halves = values.reshape(parts, 2, height // 2, width)
    high = (lax.axis_index("rows") & bit) != 0
    away = jnp.where(high, halves[:, 0], halves[:, 1]).astype(BF16)
    return jnp.where(high, halves[:, 1], halves[:, 0]), away


def row_step(values, bit):
    kept, away = row_halves(values, bit)
    return kept, swap_rows(away, bit)


def gather_rows(full, after=()):
    index = lax.axis_index("rows")
    for n, bit in enumerate(reversed(row_bits())):
        high = (index & bit) != 0
        other = swap_rows(full, bit)
        if n == 0:
            other = tie(other, *after)
        full = jnp.concatenate(
            [jnp.where(high, other, full), jnp.where(high, full, other)], axis=1
        )
    return full


def all_sum(values):
    for axis in ("filt", "rows"):
        count = lax.axis_size(axis)
        for bit in (1 << n for n in range(count.bit_length() - 1)):
            values = values + lax.ppermute(values, axis, [(r, r ^ bit) for r in range(count)])
    return values


def toeplitz_kernel(half, count, up_ref, t00_ref, t10_ref, u00_ref, u10_ref):
    width = up_ref.shape[-1]
    step = pl.program_id(0)
    up = up_ref[0]
    first = lax.broadcasted_iota(jnp.int32, up.shape, 1) == 0
    late = jnp.where(first, 0.0, pltpu.roll(up, 1, axis=1))
    up = jnp.where((step < 2 * count) & (step % 2 == 1), late, up)
    block = pltpu.roll(
        jnp.broadcast_to(up, (half, width)), 0, axis=1, stride=1, stride_axis=0
    )
    u00, u10 = block[:, :half], block[:, half : 2 * half]
    u00_ref[0] = u00.astype(BF16)
    u10_ref[0] = u10.astype(BF16)
    t00_ref[0] = u00.T.astype(BF16)
    t10_ref[0] = u10.T.astype(BF16)


def toeplitz_blocks(filters, firsts, each):
    count = each * len(firsts)
    length = filters.shape[1] // 2
    half = length // 2
    taps = jnp.concatenate(
        [lax.dynamic_slice_in_dim(filters, first, each, 0) for first in firsts], axis=0
    ).astype(BF16).astype(F32)
    taps = taps.reshape(count, length, 2).transpose(0, 2, 1).reshape(2 * count, 1, length)
    up = jnp.pad(taps, ((0, 0), (0, 0), (0, length)))
    by_column = pl.BlockSpec((1, half, half), lambda n: (n // (2 * count), 0, n % (2 * count)))
    by_row = pl.BlockSpec((1, half, half), lambda n: (n // (2 * count), n % (2 * count), 0))
    line = pl.BlockSpec((1, 1, 2 * length), lambda n: (n % (2 * count), 0, 0))
    wide = jax.ShapeDtypeStruct((2, half, 2 * count * half), BF16)
    tall = jax.ShapeDtypeStruct((2, 2 * count * half, half), BF16)
    return pl.pallas_call(
        functools.partial(toeplitz_kernel, half, count),
        grid=(4 * count,),
        in_specs=[line],
        out_specs=[by_column, by_column, by_row, by_row],
        out_shape=[wide, wide, tall, tall],
        cost_estimate=pl.CostEstimate(
            flops=0, bytes_accessed=64 * count * half * half * 4, transcendentals=0
        ),
        name="toeplitz",
    )(up)


def places(near, pieces, whole_ref, sign):
    length = whole_ref.shape[0] // 2
    nears = len(pieces)
    fars, _, _, height, _ = pieces[0].shape
    for j, piece in enumerate(pieces):
        at = lax.rem(near + sign * j + nears, nears)
        for i in range(fars):
            for parity in range(2):
                start = parity * length + (i * nears + at) * height
                yield piece.at[i, 0, parity], pl.ds(pl.multiple_of(start, height), height)


def assemble(near, pieces, whole_ref):
    for piece, rows in places(near, pieces, whole_ref, -1):
        whole_ref[rows, :] = piece[...]


def scatter(near, whole_ref, pieces):
    for piece, rows in places(near, pieces, whole_ref, 1):
        piece[...] = whole_ref[rows, :].astype(piece.dtype)


def mix_kernel(parts, near_ref, *refs):
    pieces = refs[:parts]
    mixes = refs[parts : parts + 2]
    t00_ref, t10_ref = refs[parts + 2 : parts + 4]
    outs = refs[-parts - 5 : -5]
    flip_ref, states_ref, low_ref, high_ref, sum_ref = refs[-5:]
    half = t00_ref.shape[1]
    branches = 2 * mixes[0].shape[0]
    slots = branches // 4
    assemble(near_ref[0], pieces, states_ref)

    for branch in range(branches):
        slot = pl.ds(branch * half, half)
        for quarter in range(4):
            value = dot(
                states_ref[pl.ds(quarter * half, half), :],
                mixes[branch // 2 // slots][branch % 2 * slots + branch // 2 % slots],
            ).astype(BF16)
            target = (quarter // 2) ^ (branch % 2)
            (low_ref, high_ref)[quarter % 2][target, slot, :] = value

    for parity in range(2):
        base = 2 * parity * half
        sum_ref[pl.ds(base, half), :] = dot(t00_ref[parity], low_ref[parity]).astype(
            sum_ref.dtype
        )
        sum_ref[pl.ds(base + half, half), :] = (
            dot(t10_ref[parity], low_ref[parity]) + dot(t00_ref[parity], high_ref[parity])
        ).astype(sum_ref.dtype)
    scatter(near_ref[0], sum_ref, outs)
    flip_ref[0] = states_ref[...].T


def mix_back_kernel(parts, near_ref, own_ref, *refs):
    pieces = refs[:parts]
    turned = refs[parts : parts + 2]
    u00_ref, u10_ref, slab_ref = refs[parts + 2 : parts + 5]
    before = refs[parts + 5 : -parts - 4]
    outs = refs[-parts - 4 : -4]
    back_ref, lag_ref, grad_ref, sum_ref = refs[-4:]
    half = u00_ref.shape[2]
    width = grad_ref.shape[1]
    length = grad_ref.shape[0] // 2
    branches = back_ref.shape[2] // width
    slots = branches // 4

    @pl.when(pl.program_id(0) == 0)
    def _():
        lag_ref[...] = before[1][...] if before else jnp.zeros_like(lag_ref)

    assemble(near_ref[0], pieces, grad_ref)

    for parity in range(2):
        base = 2 * parity * half
        low = grad_ref[pl.ds(base, half), :]
        high = grad_ref[pl.ds(base + half, half), :]
        for branch in range(branches):
            rows = pl.ds(branch * half, half)
            set_of, slot = branch // 2 // slots, branch // 2 % slots
            columns = pl.ds(((2 * set_of + branch % 2) * slots + slot) * width, width)
            target = 2 * half * (parity ^ (branch % 2))
            back_ref[0, pl.ds(target, half), columns] = (
                dot(u00_ref[parity, rows, :], low) + dot(u10_ref[parity, rows, :], high)
            ).astype(BF16)
            back_ref[0, pl.ds(target + half, half), columns] = dot(
                u00_ref[parity, rows, :], high
            ).astype(BF16)

    for quarter in range(4):
        rows = pl.ds(quarter * half, half)
        sum_ref[rows, :] = dot(back_ref[0, rows, : 2 * slots * width], turned[0][...]) + dot(
            back_ref[0, rows, 2 * slots * width :], turned[1][...]
        )
    scatter(near_ref[0], sum_ref, outs)

    own = slab_ref[0].astype(F32)
    even, odd = own[:, :length], own[:, length:]
    first = lax.broadcasted_iota(jnp.int32, even.shape, 1) == 0
    even_late = jnp.where(first, 0.0, pltpu.roll(even, 1, axis=1))
    odd_late = jnp.where(first, 0.0, pltpu.roll(odd, 1, axis=1))
    for lag, (on_even, on_odd) in enumerate(
        ((even, odd), (odd_late, even), (even_late, odd_late))
    ):
        lag_ref[lag] += dot(on_even.astype(BF16), grad_ref[:length, :]) + dot(
            on_odd.astype(BF16), grad_ref[length:, :]
        )


def feed_forward_kernel(
    shares, earlier, last, arrived, inputs, states, late, lag_ref, gain_ref, cot_ref, *refs
):
    weights = refs[:shares]
    saved = refs[shares : shares + 5 * earlier]
    block, grad, low, gain_out, *rest = refs[shares + 5 * earlier :]
    if last:
        sum_refs = rest
    else:
        scaled_ref, hidden_ref, gate_ref, up_ref = rest
    width = gain_ref.shape[1]
    shape = inputs.shape
    flat = (shape[0] * shape[1] * shape[2], width)

    spectral = arrived[0].astype(F32)
    for i in range(1, arrived.shape[0]):
        spectral = spectral + arrived[i].astype(F32)
    lags = (
        states[...],
        jnp.stack([late[:, 1], states[:, 0]], axis=1),
        late[...],
    )
    regress = sum(dot(lag.reshape(flat), lag_ref[n]) for n, lag in enumerate(lags))
    middle = (inputs[...].astype(F32) + spectral).reshape(flat) + regress
    factor = rms_factor(middle)
    normed = middle * factor
    gain = gain_ref[...]
    scaled = (normed * gain).astype(BF16)
    if not last:
        scaled_ref[...] = scaled
    cot = cot_ref[...].reshape(flat)
    value = middle
    mid_back = jnp.zeros(flat, F32)
    for n, weight in enumerate(weights):
        units = weight.shape[0] * weight.shape[2]
        columns = pl.ds(n * units, units)
        gate_t, up_t, down = (weight[:, m].reshape(units, width) for m in range(3))
        gate_pre = times_transpose(scaled, gate_t)
        up_values = times_transpose(scaled, up_t)
        grad_hidden = times_transpose(cot, down)
        sigmoid = 1.0 / (1.0 + jnp.exp(-gate_pre))
        silu = gate_pre * sigmoid
        hidden = (silu * up_values).astype(BF16)
        gate_back = (
            grad_hidden * up_values * (sigmoid * (1.0 + gate_pre * (1.0 - sigmoid)))
        ).astype(BF16)
        up_back = (grad_hidden * silu).astype(BF16)
        if last:
            sums = [
                contract_rows(gate_back, scaled),
                contract_rows(up_back, scaled),
                contract_rows(hidden, cot),
            ]
            for e in range(earlier):
                *parts, right, right_cot = saved[5 * e : 5 * e + 5]
                right_cot = right_cot[...].reshape(-1, width)
                for m, part in enumerate(parts):
                    sums[m] += contract_rows(
                        part[:, columns], right_cot if m == 2 else right[...]
                    )
            for m in range(3):
                split = (weight.shape[0], weight.shape[2], width)
                sum_refs[n][:, m] = sums[m].astype(sum_refs[n].dtype).reshape(split)
        else:
            hidden_ref[:, columns] = hidden
            gate_ref[:, columns] = gate_back
            up_ref[:, columns] = up_back
        value = value + dot(hidden, down)
        mid_back = mid_back + (dot(gate_back, gate_t) + dot(up_back, up_t))
    block[...] = value.astype(BF16).reshape(shape)
    gain_out[...] = jnp.sum(mid_back * normed, axis=0, keepdims=True)
    total = cot.astype(F32) + norm_backward(mid_back, normed, factor, gain)
    grad[...] = total.reshape(shape)
    rounded = total.astype(BF16).reshape(shape)
    for i in range(low.shape[0]):
        low[i] = rounded


def mixing_kernel(
    bit_ref, flip_ref, plus_ref, minus_ref, sum_ref, rest_ref, stay_ref, away_ref, gain_ref
):
    rows = stay_ref.shape[1]

    @pl.when(pl.program_id(0) == 0)
    def _():
        gain_ref[...] = jnp.zeros_like(gain_ref)

    for n, out_ref in enumerate((stay_ref, away_ref)):
        here = pl.ds(pl.multiple_of((bit_ref[0] ^ n) * rows, rows), rows)
        plus, minus = (
            sum(dot(flip_ref[s, here, :], ref[s]) for s in range(flip_ref.shape[0]))
            for ref in (plus_ref, minus_ref)
        )
        out_ref[0] = (plus + minus).astype(out_ref.dtype)
        out_ref[1] = (plus - minus).astype(out_ref.dtype)
        gain_ref[here, :] += jnp.sum(
            plus * sum_ref[0, here, :].astype(F32) + minus * rest_ref[0, here, :].astype(F32),
            axis=1,
            keepdims=True,
        )


def resident(shape):
    zeros = (0,) * len(shape)
    return pl.BlockSpec(shape, lambda *_: zeros, pipeline_mode=pl.Buffered(1))


def mix_sequences(pieces, near, pairs, t00, t10, start, total, flips):
    parts = len(pieces)
    fars, count, _, height, width = pieces[0].shape
    half = t00.shape[1]
    block = pl.BlockSpec((fars, 1, 2, height, width), lambda n, *_: (0, n, 0, 0, 0))
    rows = t00.shape[2]
    flip = pl.BlockSpec((1, width, 4 * half), lambda n, *_: (start + n, 0, 0))
    return pl.pallas_call(
        functools.partial(mix_kernel, parts),
        grid_spec=pltpu.PrefetchScalarGridSpec(
            num_scalar_prefetch=1,
            grid=(count,),
            in_specs=[block] * parts
            + [resident(a.shape) for a in (*pairs, t00, t10)]
            + [pl.BlockSpec(memory_space=pl.ANY)] * len(flips),
            out_specs=[block] * parts + [flip],
            scratch_shapes=[
                pltpu.VMEM((4 * half, width), BF16),
                pltpu.VMEM((2, rows, width), BF16),
                pltpu.VMEM((2, rows, width), BF16),
                pltpu.VMEM((4 * half, width), F32),
            ],
        ),
        out_shape=[jax.ShapeDtypeStruct(pieces[0].shape, BF16)] * parts
        + [jax.ShapeDtypeStruct((total, width, 4 * half), BF16)],
        input_output_aliases={parts + 5: parts} if flips else {},
        compiler_params=pltpu.CompilerParams(vmem_limit_bytes=48 << 20),
        cost_estimate=pl.CostEstimate(
            flops=count * (16 * half * pairs[0].size + 12 * half * rows * width),
            bytes_accessed=4 * parts * pieces[0].size + 4 * pairs[0].size + 4 * t00.size,
            transcendentals=0,
        ),
        name="mix",
    )(near, *pieces, *pairs, t00, t10, *flips)


def mix_sequences_back(pieces, near, own, turned, u00, u10, lag_count, start, flips, before):
    parts = len(pieces)
    fars, count, _, height, width = pieces[0].shape
    half = u00.shape[2]
    block = pl.BlockSpec((fars, 1, 2, height, width), lambda n, *_: (0, n, 0, 0, 0))
    rows = u00.shape[1]
    slab = 2 * width // (parts * fars)
    lag_shape = (lag_count, slab, width)
    back_shape = (flips.shape[0], 4 * half, 2 * turned[0].shape[0])
    back = pl.BlockSpec((1, *back_shape[1:]), lambda n, *_: (start + n, 0, 0))
    slab_spec = pl.BlockSpec((1, slab, 4 * half), lambda n, _, own: (start + n, own[0], 0))
    return pl.pallas_call(
        functools.partial(mix_back_kernel, parts),
        grid_spec=pltpu.PrefetchScalarGridSpec(
            num_scalar_prefetch=2,
            grid=(count,),
            in_specs=[block] * parts
            + [resident(a.shape) for a in (*turned, u00, u10)]
            + [slab_spec]
            + ([pl.BlockSpec(memory_space=pl.ANY), resident(lag_shape)] if before else []),
            out_specs=[block] * parts + [back, resident(lag_shape)],
            scratch_shapes=[
                pltpu.VMEM((4 * half, width), BF16),
                pltpu.VMEM((4 * half, width), F32),
            ],
        ),
        out_shape=[jax.ShapeDtypeStruct(pieces[0].shape, BF16)] * parts
        + [
            jax.ShapeDtypeStruct(back_shape, BF16),
            jax.ShapeDtypeStruct(lag_shape, F32),
        ],
        input_output_aliases={parts + 7: parts} if before else {},
        compiler_params=pltpu.CompilerParams(vmem_limit_bytes=56 << 20),
        cost_estimate=pl.CostEstimate(
            flops=count * (16 * half * turned[0].size + 12 * half * rows * width),
            bytes_accessed=4 * parts * pieces[0].size + 8 * turned[0].size,
            transcendentals=0,
        ),
        name="mix_back",
    )(near, own, *pieces, *turned, u00, u10, flips, *before)


def mixing_products(flips, backs, pairs, bit, set_of):
    count, width, length = flips.shape
    slots = pairs.shape[0] // 2
    plus = pl.BlockSpec((count, length, width), lambda k, _: (0, 0, 2 * set_of * slots + k))
    minus = pl.BlockSpec(
        (count, length, width), lambda k, _: (0, 0, (2 * set_of + 1) * slots + k)
    )
    pair = pl.BlockSpec((1, width, width), lambda k, _: (k, 0, 0))
    rest = pl.BlockSpec((1, width, width), lambda k, _: (slots + k, 0, 0))
    half = pl.BlockSpec((2, width // 2, width), lambda k, _: (k, 0, 0))
    return pl.pallas_call(
        mixing_kernel,
        grid_spec=pltpu.PrefetchScalarGridSpec(
            num_scalar_prefetch=1,
            grid=(slots,),
            in_specs=[resident(flips.shape), plus, minus, pair, rest],
            out_specs=[half, half, resident((width, 1))],
        ),
        out_shape=[
            jax.ShapeDtypeStruct((2 * slots, width // 2, width), F32),
            jax.ShapeDtypeStruct((2 * slots, width // 2, width), BF16),
            jax.ShapeDtypeStruct((width, 1), F32),
        ],
        compiler_params=pltpu.CompilerParams(vmem_limit_bytes=56 << 20),
        cost_estimate=pl.CostEstimate(
            flops=backs.size * width,
            bytes_accessed=2 * flips.size + backs.size + 8 * slots * width * width,
            transcendentals=0,
        ),
        name="mixing_products",
    )(bit, flips, backs, backs, pairs, pairs)


def feed_forward(arrived, inputs, states, late, lag, gain, cot, weights, saved, last):
    rows, width = inputs.size // inputs.shape[-1], inputs.shape[-1]
    shares = len(weights)
    units = weights[0].shape[0] * weights[0].shape[2]
    flat_saved = [value for values in saved for value in values] if last else []
    operands = (arrived, inputs, states, late, lag, gain, cot, *weights, *flat_saved)
    whole = pl.BlockSpec(memory_space=pltpu.VMEM)
    if last:
        extra = [
            jax.ShapeDtypeStruct(weights[0].shape, F32 if n < shares // 2 else BF16)
            for n in range(shares)
        ]
    else:
        extra = [jax.ShapeDtypeStruct((rows, width), BF16)] + [
            jax.ShapeDtypeStruct((rows, shares * units), BF16)
        ] * 3
    return pl.pallas_call(
        functools.partial(feed_forward_kernel, shares, len(flat_saved) // 5, last),
        in_specs=[whole] * len(operands),
        out_specs=[whole] * (4 + len(extra)),
        out_shape=[
            jax.ShapeDtypeStruct(inputs.shape, BF16),
            jax.ShapeDtypeStruct(inputs.shape, F32),
            jax.ShapeDtypeStruct(arrived.shape, BF16),
            jax.ShapeDtypeStruct((1, width), F32),
            *extra,
        ],
        compiler_params=pltpu.CompilerParams(vmem_limit_bytes=56 << 20),
        cost_estimate=pl.CostEstimate(
            flops=(24 if last else 12) * rows * width * shares * units,
            bytes_accessed=6 * shares * units * width + 40 * rows * width,
            transcendentals=rows * shares * units,
        ),
        name="feed_forward",
    )(*operands)


def leading(values, edge):
    early = jnp.concatenate([values[:, :, 1:], edge], axis=2)
    return values, jnp.stack([values[:, 1], early[:, 0]], axis=1), early


def row_masks():
    masks = [0]
    for bit in reversed(row_bits()):
        masks = masks + [mask ^ bit for mask in masks]
    return masks


def spread_rows(own):
    full = own[None]
    for bit in reversed(row_bits()):
        full = jnp.concatenate([full, swap_rows(full, bit)], axis=0)
    return full


def shards(inputs, filters, gain_in, mixing, regression, gain_mid, w_gate, w_up, w_down, out_grad):
    shard_rows, local_seqs, width = inputs.shape
    grid = Grid(lax.axis_size("filt"))
    row_count = lax.axis_size("rows")
    row_index = lax.axis_index("rows")
    bits = row_bits()
    index = lax.axis_index("filt")
    branches = mixing.shape[0]
    lag_count = regression.shape[0]
    height = shard_rows // 2
    chunks = CHUNKS
    step = local_seqs // chunks
    own_seqs = step // 2
    block = (own_seqs, 2, height, width)

    def inward(values):
        return values.reshape(height, 2, local_seqs, width).transpose(2, 1, 0, 3)

    def outward(values):
        return values.transpose(2, 1, 0, 3).reshape(shard_rows, local_seqs, width)

    def cut(values):
        return [values[c * step : (c + 1) * step] for c in range(chunks)]

    def to_mate(part):
        keep, away = grid.split(part.reshape(2, *block), grid.mate)
        return keep, grid.swap(away, grid.mate)

    def to_far(keep, received):
        pair = grid.join(keep, received, grid.mate)
        return pair, grid.swap(pair, grid.far)

    def to_near(pair, received):
        quad = grid.join(pair, received, grid.far).reshape(4, *block)
        return quad, near_swaps(grid, quad)

    def from_near(partial, received):
        total = total_of([partial[0], *received]).reshape(2, 2, *block)
        keep, away = grid.split(total, grid.far)
        return keep, away.astype(BF16)

    def from_far(keep, received):
        return grid.split((keep + received.astype(F32)).astype(BF16), grid.mate)

    def from_mate(keep, received):
        return grid.join(keep, received, grid.mate).reshape(step, 2, height, width)

    inputs_low = inward(inputs)
    residual = inputs_low.astype(F32)
    factor_in = rms_factor(residual)
    normed_in = residual * factor_in
    states = (normed_in * gain_in).astype(BF16)
    mates = [to_mate(part) for part in cut(states)]

    slots = (branches + 1) // 2
    first_branch = index * branches
    if branches % 2:
        odd_start = first_branch % 2
        paired = lax.dynamic_update_slice_in_dim(
            jnp.zeros((2 * slots,) + mixing.shape[1:], mixing.dtype), mixing, odd_start, 0
        )
    else:
        paired = mixing
    paired = tie(paired, mates[0][0])
    first, second = (paired[n::2].astype(F32) for n in range(2))
    own_pairs = jnp.concatenate([first + second, first - second], axis=0).astype(BF16)
    part_rows = width // row_count
    start = sum(
        jnp.where((row_index & bit) != 0, width >> (n + 1), 0) for n, bit in enumerate(bits)
    )
    own_part = lax.dynamic_slice_in_dim(own_pairs, start, part_rows, 1)
    hidden_own = w_down.shape[0]
    share = hidden_own // row_count
    packed = jnp.stack([w_gate.T, w_up.T, w_down]).reshape(3, row_count, share, width)
    *early_bits, last_bit = grid.spread_bits()
    shares = lax.dynamic_index_in_dim(packed, row_index, 1, keepdims=False)
    shares = grid.join(shares, grid.swap(shares, early_bits[0]), early_bits[0])
    mates = [(keep, tie(received, own_part)) for keep, received in mates]
    fars = [to_far(*values) for values in mates]
    mate_part = grid.swap(tie(own_part, shares, *(pair for pair, _ in fars)), grid.mate)
    received = [received for _, received in fars]
    edge = lax.ppermute(
        tie(states[:, :, -1:], *(pair for pair, _ in fars)),
        "filt",
        [(f, f + 1) for f in range(grid.size - 1)],
    )
    t00, t10, u00, u10 = toeplitz_blocks(
        tie(filters, *(pair for pair, _ in fars)),
        [first_branch // 2, (index ^ grid.mate) * branches // 2],
        slots,
    )
    mate_part, edge = tie_all([mate_part, edge], t00, *received)
    mate_part = tie(mate_part, edge)
    for bit in early_bits[1:]:
        shares = tie(shares, mate_part)
        shares = grid.join(shares, grid.swap(shares, bit), bit)
    quads = [to_near(*values) for values in fars]
    mate_pairs = gather_rows(
        mate_part, [shares, *(value for _, values in quads for value in values)]
    )
    pairs = [own_pairs, mate_pairs]
    cotangent_low = inward(tie(out_grad, *received))

    near = jnp.reshape(index % grid.near, (1,)).astype(jnp.int32)
    late = jnp.concatenate([edge, states[:, :, :-1]], axis=2)
    quads[0] = (quads[0][0], tie_all(quads[0][1], *quads[-1][1]))
    late, inputs_low, cotangent_low, shares, *pieces = tied(
        late, inputs_low, cotangent_low, shares, quads[0][0], *quads[0][1]
    )

    partials, flips, near_received = [], [], []
    received = grid.swap(shares, last_bit)
    for c in range(chunks):
        if c:
            pieces = [quads[c][0], *quads[c][1]]
        *partial, flip = mix_sequences(
            pieces, near, pairs, t00, t10, c * own_seqs, chunks * own_seqs, flips
        )
        if c == 0:
            received = tie(received, partial[0])
            shares = grid.join(shares, received, last_bit)
        else:
            near_received[-1] = tie_all(near_received[-1], partial[0])
            partial = tie_all(partial, *near_received[-1])
        partials.append(partial)
        near_received.append(near_swaps(grid, partial))
        flips = [flip]
    kept_sums, from_fars, turned = [], [], []
    for c in range(chunks):
        kept_sums.append(from_near(partials[c], tie_all(near_received[c], *from_fars, *turned)))
        from_fars.append(grid.swap(kept_sums[c][1], grid.far))
        if c == 0:
            turned = [
                value.transpose(0, 2, 1).reshape(2 * slots * width, width)
                for value in tie_all(pairs, kept_sums[0][1])
            ]
    weights = [shares.reshape(grid.size, 3, share, width)]
    for n, bit in enumerate(reversed(bits)):
        received = [swap_rows(weight, bit) for weight in weights]
        if n == 0:
            received = tie_all(received, from_fars[0])
        weights = weights + received

    block_out, middle_grad, lows, fars, kept = [], [], [], [], []
    gain_mid_part = jnp.zeros((1, width), F32)
    for c in range(chunks):
        part = slice(c * step, (c + 1) * step)
        keep, away = from_far(kept_sums[c][0], from_fars[c])
        arrived = from_mate(keep, grid.swap(away, grid.mate))
        if c:
            arrived = tie(arrived, fars[-1][0])
        if c + 1 < chunks:
            arrived = tie(arrived, kept_sums[c + 1][1])
        cot = cotangent_low[part]
        value, grad, low, gain_part, *rest = feed_forward(
            arrived[None], inputs_low[part], states[part], late[part], regression,
            gain_mid[None], cot, weights, kept, c + 1 == chunks,
        )
        block_out.append(value)
        middle_grad.append(grad)
        gain_mid_part = gain_mid_part + gain_part
        if c + 1 < chunks:
            from_fars[c + 1] = tie(from_fars[c + 1], grad)
            low = tie(low, from_fars[c + 1])
        if c:
            fars[-1] = (fars[-1][0], tie(fars[-1][1], grad))
            low, *rest = tie_all([low, *rest], fars[-1][1])
        lows.append(low[0])
        fars.append(to_far(*to_mate(low[0])))
        if c + 1 < chunks:
            scaled, hidden, gate_back, up_back = rest
            kept.append((gate_back, up_back, hidden, scaled, cot))
    gain_mid_part = gain_mid_part[0]

    quads = [to_near(*values) for values in fars]

    half_count = len(rest) // 2
    values = [swap_rows(away, bits[0]) for away in rest[half_count:]]
    values = tie_all(values, *quads[0][1])
    sums_of = [[stay, value] for stay, value in zip(rest[:half_count], values, strict=True)]

    group = index // grid.far * grid.near + index % grid.near
    own = jnp.reshape(group, (1,)).astype(jnp.int32)
    before = ()
    back_partials, near_received = [], []
    mix_back = jnp.concatenate(lows, axis=0)
    next_edge = lax.ppermute(
        mix_back[:, :, :1], "filt", [(f + 1, f) for f in range(grid.size - 1)]
    )
    for bit in bits[1:-1]:
        half_count = len(sums_of) // 2
        values = [swap_rows(total_of(v).astype(BF16), bit) for v in sums_of[half_count:]]
        sums_of = [[*v, value] for v, value in zip(sums_of[:half_count], values, strict=True)]
    parts, away = sums_of
    half_count = away[0].shape[0] // 2
    away = total_of(away).astype(BF16)
    away = [away[:half_count], away[half_count:]]
    from_rows = [swap_rows(value, bits[-1]) for value in away]
    first_quad, next_edge = tie_all([quads[0][0], next_edge], *away)
    quads[0] = (first_quad, quads[0][1])
    for c in range(chunks):
        quad, received = quads[c]
        if c + 1 < chunks:
            quad = tie(quad, quads[c + 1][0])
        *partial, backs, lag_sum = mix_sequences_back(
            [quad, *received], near, own, turned, u00, u10, lag_count, c * own_seqs, flip, before
        )
        before = (backs, lag_sum)
        if c + 1 < chunks:
            later_received = tie_all(quads[c + 1][1], partial[0])
            quads[c + 1] = (quads[c + 1][0], later_received)
            from_rows[c] = tie(from_rows[c], partial[0])
            partial = tie_all(partial, *later_received, from_rows[c])
        if c:
            near_received[-1] = tie_all(near_received[-1], partial[0])
            from_rows[-1] = tie(from_rows[-1], partial[0])
            lag_sum, backs, *partial = tie_all(
                [lag_sum, backs, *partial], *near_received[-1], from_rows[-1]
            )
        back_partials.append(partial)
        near_received.append(near_swaps(grid, partial))
    sums = [from_near(back_partials[0], near_received[0])]
    kept, value = row_step(tie(lag_sum, sums[0][1]), bits[0])
    lag_share = kept + value.astype(F32)
    kept, value = row_step(lag_share, bits[1])
    core_bit = jnp.reshape(row_index & 1, (1,)).astype(jnp.int32)
    mate_stay, mate_away, mate_gain = mixing_products(
        flip, tie(backs, sums[0][1], kept), mate_pairs, core_bit, 1
    )
    from_fars = [tie(grid.swap(sums[0][1], grid.far), mate_gain)]
    mate_stay, mate_away, mate_gain = tie_all([mate_stay, mate_away, mate_gain], from_fars[0])
    lag_share = kept + tie(value, mate_gain).astype(F32)
    for bit in bits[2:]:
        kept, value = row_step(lag_share, bit)
        lag_share = kept + value.astype(F32)
    lag_rows = lag_share.shape[1] // 2
    lag_share, lag_away = grid.split(
        lag_share.reshape(lag_count, 2, lag_rows, width).transpose(1, 0, 2, 3), grid.mate
    )
    lag_away = lag_away.astype(BF16)
    mate_sends = [from_far(sums[0][0], from_fars[0])]
    mate_share = mate_stay + swap_rows(mate_away, bits[0]).astype(F32)
    for c in range(1, chunks):
        sums.append(from_near(back_partials[c], tie_all(near_received[c], mate_gain)))
        from_fars.append(grid.swap(sums[c][1], grid.far))
    twos = (2,) * len(grid.spread_bits())
    grads = jnp.concatenate(
        [
            total_of([*(part[n * half_count : (n + 1) * half_count] for part in parts), value])
            for n, value in enumerate(tie_all(from_rows, mate_gain))
        ]
    ).reshape(*twos, 3, share, width)
    last_bits = grid.spread_bits()[::-1]
    grads, away = grid.split(grads, last_bits[0])
    away = away.astype(BF16)
    mate_kept, mate_away = row_halves(mate_share, bits[1])
    own_stay, own_away, own_gain = mixing_products(
        flip,
        tie(backs, mate_away, mate_sends[0][1], away, lag_away, *(v for _, v in sums[1:])),
        own_pairs, core_bit, 0,
    )
    from_mates = [tie(grid.swap(mate_sends[0][1], grid.mate), own_gain)]
    value = tie(swap_rows(mate_away, bits[1]), own_gain)
    mate_share = mate_kept + value.astype(F32)
    for bit in bits[2:]:
        kept, value = row_step(mate_share, bit)
        mate_share = kept + value.astype(F32)
    from_fars[1:] = tie_all(from_fars[1:], own_gain)
    own_gain = tie(own_gain, value, *from_mates, *from_fars[1:])
    grads = grads + tie(grid.swap(away, last_bits[0]), own_gain).astype(F32)
    lag_share = lag_share + tie(grid.swap(lag_away, grid.mate), own_gain).astype(F32)
    own_stay, own_away = tie_all([own_stay, own_away], own_gain)
    own_share = own_stay + swap_rows(own_away, bits[0]).astype(F32)
    for bit in bits[1:]:
        kept, value = row_step(own_share, bit)
        own_share = kept + value.astype(F32)
    received = grid.swap(mate_share.astype(BF16), grid.mate)
    mixing_low = (own_share + received.astype(F32)).astype(BF16)
    gain_mid_part, lag_sum, lag_share, mix_back, next_edge, grads, own_gain, *block_out = tie_all(
        [gain_mid_part, lag_sum, lag_share, mix_back, next_edge, grads, own_gain, *block_out],
        mixing_low,
    )
    gain_column = mate_gain + own_gain
    for c in range(1, chunks):
        mate_sends.append(from_far(sums[c][0], from_fars[c]))
    from_mates += [grid.swap(away, grid.mate) for _, away in mate_sends[1:]]
    state_back = [
        from_mate(keep, received).astype(F32)
        for (keep, _), received in zip(mate_sends, from_mates, strict=True)
    ]
    mixing_grad = gather_rows(mixing_low).astype(F32)
    if branches % 2:
        mixing_grad = lax.dynamic_slice_in_dim(mixing_grad, odd_start, branches, 0)

    slab = width // grid.size * 2
    own_regression = lax.dynamic_slice_in_dim(regression, group * slab, slab, 1)
    gain_lag = jnp.sum(own_regression.astype(F32) * lag_sum, axis=(0, 2))
    gain_in_part = gain_column[:, 0]
    gain_in_part = lax.dynamic_update_slice_in_dim(
        gain_in_part,
        lax.dynamic_slice_in_dim(gain_in_part, group * slab, slab, 0) + gain_lag,
        group * slab,
        0,
    ) / gain_in
    gains = all_sum(jnp.pad(jnp.stack([gain_in_part, gain_mid_part]), ((0, 6), (0, 0))))

    own_grads = reduce_filt(grid, grads, last_bits[1:]).astype(BF16)

    spread = gather_filt(grid, lag_share.astype(BF16))
    spread = (
        spread.reshape(grid.near, 2, 2, lag_count, lag_rows, width)
        .transpose(2, 0, 3, 1, 4, 5)
        .reshape(2 * grid.near * lag_count, 2 * lag_rows, width)
    )
    regression_grad = (
        gather_rows(spread)
        .reshape(2 * grid.near, lag_count, slab, width)
        .transpose(1, 0, 2, 3)
        .reshape(lag_count, width, width)
        .astype(F32)
    )

    lag_back = sum(
        jnp.einsum("spae,de->spad", lead, regression[n], preferred_element_type=F32)
        for n, lead in enumerate(leading(mix_back, next_edge))
    )
    input_grad = []
    for c in range(chunks):
        part = slice(c * step, (c + 1) * step)
        back = state_back[c] + lag_back[part]
        input_grad.append(
            middle_grad[c] + norm_backward(back, normed_in[part], factor_in[part], gain_in)
        )

    full = spread_rows(own_grads)
    ordered = jnp.zeros((row_count, 3, share, width), BF16)
    for n, mask in enumerate(row_masks()):
        ordered = lax.dynamic_update_slice_in_dim(ordered, full[n][None], row_index ^ mask, 0)
    ordered = ordered.transpose(1, 0, 2, 3).reshape(3, hidden_own, width).astype(F32)
    return (
        outward(jnp.concatenate(block_out, axis=0)),
        outward(jnp.concatenate(input_grad, axis=0)),
        mixing_grad,
        regression_grad,
        gains[0],
        gains[1],
        ordered[0].T,
        ordered[1].T,
        ordered[2],
    )


def solution(mesh):
    placed = (
        P("filt", "rows", None),
        P(),
        P(),
        P("filt", None, None),
        P(),
        P(),
        P(None, "filt"),
        P(None, "filt"),
        P("filt", None),
        P("filt", "rows", None),
    )
    return jax.shard_map(
        shards,
        mesh=mesh,
        in_specs=placed,
        out_specs=(
            P("filt", "rows", None),
            P("filt", "rows", None),
            P("filt", None, None),
            P(),
            P(),
            P(),
            P(None, "filt"),
            P(None, "filt"),
            P("filt", None),
        ),
        check_vma=False,
    )
```

```python
import functools

import jax
import jax.numpy as jnp
from jax import lax
from jax.experimental import pallas as pl
from jax.experimental.pallas import tpu as pltpu
from jax.sharding import PartitionSpec as P

EPSILON = 1e-05
CHUNKS = 2
F32 = jnp.float32
BF16 = jnp.bfloat16


def dot(left, right):
    return jnp.dot(left, right, preferred_element_type=F32)


def contract_rows(left, right):
    return lax.dot_general(left, right, (((0,), (0,)), ((), ())), preferred_element_type=F32)


def times_transpose(left, right):
    return lax.dot_general(left, right, (((1,), (1,)), ((), ())), preferred_element_type=F32)


def rms_factor(values):
    return lax.rsqrt(jnp.mean(values * values, axis=-1, keepdims=True) + EPSILON)


def norm_backward(grad_out, normed, factor, gain):
    inner = grad_out * gain
    return factor * (inner - normed * jnp.mean(inner * normed, axis=-1, keepdims=True))


class Grid:
    def __init__(self, size):
        self.size = size
        self.near = size // 4
        self.mate = self.near
        self.far = 2 * self.near

    def near_bits(self):
        return [1 << n for n in range(self.near.bit_length() - 1)]

    def near_shift(self, step):
        near = self.near
        return [(f, f // near * near + (f % near + step) % near) for f in range(self.size)]

    def flag(self, bit):
        return (lax.axis_index("filt") & bit) != 0

    def swap(self, values, bit):
        return lax.ppermute(values, "filt", [(f, f ^ bit) for f in range(self.size)])

    def split(self, halves, bit):
        flag = self.flag(bit)
        return jnp.where(flag, halves[1], halves[0]), jnp.where(flag, halves[0], halves[1])

    def join(self, own, other, bit):
        return jnp.where(self.flag(bit), jnp.stack([other, own]), jnp.stack([own, other]))

    def spread_bits(self):
        return [self.far, self.mate, *self.near_bits()]


def gather_filt(grid, values):
    for bit in grid.spread_bits():
        values = grid.join(values, grid.swap(values, bit), bit)
    return values


def reduce_filt(grid, values, bits):
    for bit in bits:
        own, away = grid.split(values, bit)
        values = own.astype(F32) + grid.swap(away.astype(BF16), bit).astype(F32)
    return values


def tie(value, *others):
    return lax.optimization_barrier((value, *others))[0] if others else value


def tied(*values):
    return list(lax.optimization_barrier(values))


def tie_all(values, *others):
    count = len(values)
    return list(lax.optimization_barrier((*values, *others))[:count]) if others else list(values)


def near_swaps(grid, values):
    return [
        lax.ppermute(
            values[j] if isinstance(values, list) else values, "filt", grid.near_shift(j)
        )
        for j in range(1, grid.near)
    ]


def total_of(values):
    total = values[0].astype(F32)
    for value in values[1:]:
        total = total + value.astype(F32)
    return total


def swap_rows(values, bit):
    count = lax.axis_size("rows")
    return lax.ppermute(values, "rows", [(r, r ^ bit) for r in range(count)])


def row_bits():
    count = lax.axis_size("rows")
    return [1 << n for n in range(count.bit_length() - 1)]


def row_halves(values, bit):
    parts, height, width = values.shape
    halves = values.reshape(parts, 2, height // 2, width)
    high = (lax.axis_index("rows") & bit) != 0
    away = jnp.where(high, halves[:, 0], halves[:, 1]).astype(BF16)
    return jnp.where(high, halves[:, 1], halves[:, 0]), away


def row_step(values, bit):
    kept, away = row_halves(values, bit)
    return kept, swap_rows(away, bit)


def gather_rows(full, after=()):
    index = lax.axis_index("rows")
    for n, bit in enumerate(reversed(row_bits())):
        high = (index & bit) != 0
        other = swap_rows(full, bit)
        if n == 0:
            other = tie(other, *after)
        full = jnp.concatenate(
            [jnp.where(high, other, full), jnp.where(high, full, other)], axis=1
        )
    return full


def pair_sum(values, axis):
    count = lax.axis_size(axis)
    for bit in (1 << n for n in range(count.bit_length() - 1)):
        values = values + lax.ppermute(values, axis, [(r, r ^ bit) for r in range(count)])
    return values


def toeplitz_kernel(half, up_ref, t00_ref, t10_ref, u00_ref, u10_ref):
    width = up_ref.shape[-1]
    up = up_ref[0]

    def build(row, parities):
        block = pltpu.roll(
            jnp.broadcast_to(row, (half, width)), 0, axis=1, stride=1, stride_axis=0
        )
        u00, u10 = block[:, :half], block[:, half : 2 * half]
        for parity in parities:
            u00_ref[parity] = u00.astype(BF16)
            u10_ref[parity] = u10.astype(BF16)
            t00_ref[parity] = u00.T.astype(BF16)
            t10_ref[parity] = u10.T.astype(BF16)

    @pl.when(pl.program_id(0) % 2 == 0)
    def _():
        build(up, (0, 1))

    @pl.when(pl.program_id(0) % 2 == 1)
    def _():
        first = lax.broadcasted_iota(jnp.int32, up.shape, 1) == 0
        build(jnp.where(first, 0.0, pltpu.roll(up, 1, axis=1)), (0,))
        build(up, (1,))


def toeplitz_blocks(filters, firsts, each):
    count = each * len(firsts)
    length = filters.shape[1] // 2
    half = length // 2
    taps = jnp.concatenate(
        [lax.dynamic_slice_in_dim(filters, first, each, 0) for first in firsts], axis=0
    ).astype(BF16).astype(F32)
    taps = taps.reshape(count, length, 2).transpose(0, 2, 1).reshape(2 * count, 1, length)
    up = jnp.pad(taps, ((0, 0), (0, 0), (0, half)))
    by_column = pl.BlockSpec((2, half, half), lambda n: (0, 0, n))
    by_row = pl.BlockSpec((2, half, half), lambda n: (0, n, 0))
    line = pl.BlockSpec((1, 1, length + half), lambda n: (n, 0, 0))
    wide = jax.ShapeDtypeStruct((2, half, 2 * count * half), BF16)
    tall = jax.ShapeDtypeStruct((2, 2 * count * half, half), BF16)
    return pl.pallas_call(
        functools.partial(toeplitz_kernel, half),
        grid=(2 * count,),
        in_specs=[line],
        out_specs=[by_column, by_column, by_row, by_row],
        out_shape=[wide, wide, tall, tall],
        cost_estimate=pl.CostEstimate(
            flops=0, bytes_accessed=48 * count * half * half * 4, transcendentals=0
        ),
        name="toeplitz",
    )(up)


def places(near, pieces, whole_ref, sign):
    length = whole_ref.shape[0] // 2
    nears = len(pieces)
    fars, _, _, height, _ = pieces[0].shape
    for j, piece in enumerate(pieces):
        at = lax.rem(near + sign * j + nears, nears)
        for i in range(fars):
            for parity in range(2):
                start = parity * length + (i * nears + at) * height
                yield piece.at[i, 0, parity], pl.ds(pl.multiple_of(start, height), height)


def assemble(near, pieces, whole_ref):
    for piece, rows in places(near, pieces, whole_ref, -1):
        whole_ref[rows, :] = piece[...]


def scatter(near, whole_ref, pieces):
    for piece, rows in places(near, pieces, whole_ref, 1):
        piece[...] = whole_ref[rows, :].astype(piece.dtype)


def mix_kernel(parts, near_ref, *refs):
    pieces = refs[:parts]
    mixes = refs[parts : parts + 2]
    t00_ref, t10_ref = refs[parts + 2 : parts + 4]
    outs = refs[-parts - 5 : -5]
    flip_ref, states_ref, low_ref, high_ref, sum_ref = refs[-5:]
    half = t00_ref.shape[1]
    branches = 2 * mixes[0].shape[0]
    slots = branches // 4
    assemble(near_ref[0], pieces, states_ref)

    for branch in range(branches):
        slot = pl.ds(branch * half, half)
        for quarter in range(4):
            value = dot(
                states_ref[pl.ds(quarter * half, half), :],
                mixes[branch // 2 // slots][branch % 2 * slots + branch // 2 % slots],
            ).astype(BF16)
            target = (quarter // 2) ^ (branch % 2)
            (low_ref, high_ref)[quarter % 2][target, slot, :] = value

    for parity in range(2):
        base = 2 * parity * half
        sum_ref[pl.ds(base, half), :] = dot(t00_ref[parity], low_ref[parity]).astype(
            sum_ref.dtype
        )
        sum_ref[pl.ds(base + half, half), :] = (
            dot(t10_ref[parity], low_ref[parity]) + dot(t00_ref[parity], high_ref[parity])
        ).astype(sum_ref.dtype)
    scatter(near_ref[0], sum_ref, outs)
    flip_ref[0] = states_ref[...].T


def mix_back_kernel(parts, near_ref, own_ref, *refs):
    pieces = refs[:parts]
    turned = refs[parts : parts + 2]
    u00_ref, u10_ref, slab_ref = refs[parts + 2 : parts + 5]
    before = refs[parts + 5 : -parts - 4]
    outs = refs[-parts - 4 : -4]
    back_ref, lag_ref, grad_ref, sum_ref = refs[-4:]
    half = u00_ref.shape[2]
    width = grad_ref.shape[1]
    length = grad_ref.shape[0] // 2
    branches = back_ref.shape[2] // width
    slots = branches // 4

    @pl.when(pl.program_id(0) == 0)
    def _():
        lag_ref[...] = before[1][...] if before else jnp.zeros_like(lag_ref)

    assemble(near_ref[0], pieces, grad_ref)

    for parity in range(2):
        base = 2 * parity * half
        low = grad_ref[pl.ds(base, half), :]
        high = grad_ref[pl.ds(base + half, half), :]
        for branch in range(branches):
            rows = pl.ds(branch * half, half)
            set_of, slot = branch // 2 // slots, branch // 2 % slots
            columns = pl.ds(((2 * set_of + branch % 2) * slots + slot) * width, width)
            target = 2 * half * (parity ^ (branch % 2))
            back_ref[0, pl.ds(target, half), columns] = (
                dot(u00_ref[parity, rows, :], low) + dot(u10_ref[parity, rows, :], high)
            ).astype(BF16)
            back_ref[0, pl.ds(target + half, half), columns] = dot(
                u00_ref[parity, rows, :], high
            ).astype(BF16)

    for quarter in range(4):
        rows = pl.ds(quarter * half, half)
        sum_ref[rows, :] = dot(back_ref[0, rows, : 2 * slots * width], turned[0][...]) + dot(
            back_ref[0, rows, 2 * slots * width :], turned[1][...]
        )
    scatter(near_ref[0], sum_ref, outs)

    own = slab_ref[0].astype(F32)
    even, odd = own[:, :length], own[:, length:]
    first = lax.broadcasted_iota(jnp.int32, even.shape, 1) == 0
    even_late = jnp.where(first, 0.0, pltpu.roll(even, 1, axis=1))
    odd_late = jnp.where(first, 0.0, pltpu.roll(odd, 1, axis=1))
    for lag, (on_even, on_odd) in enumerate(
        ((even, odd), (odd_late, even), (even_late, odd_late))
    ):
        lag_ref[lag] += dot(on_even.astype(BF16), grad_ref[:length, :]) + dot(
            on_odd.astype(BF16), grad_ref[length:, :]
        )


def feed_forward_kernel(
    shares, earlier, last, arrived, inputs, states, late, lag_ref, gain_ref, cot_ref, *refs
):
    weights = refs[:shares]
    saved = refs[shares : shares + 5 * earlier]
    block, grad, low, gain_out, *rest = refs[shares + 5 * earlier :]
    if last:
        sum_refs = rest
    else:
        scaled_ref, hidden_ref, gate_ref, up_ref = rest
    width = gain_ref.shape[1]
    shape = inputs.shape
    flat = (shape[0] * shape[1] * shape[2], width)

    spectral = arrived[0].astype(F32)
    for i in range(1, arrived.shape[0]):
        spectral = spectral + arrived[i].astype(F32)
    lags = (
        states[...],
        jnp.stack([late[:, 1], states[:, 0]], axis=1),
        late[...],
    )
    regress = sum(dot(lag.reshape(flat), lag_ref[n]) for n, lag in enumerate(lags))
    middle = (inputs[...].astype(F32) + spectral).reshape(flat) + regress
    factor = rms_factor(middle)
    normed = middle * factor
    gain = gain_ref[...]
    scaled = (normed * gain).astype(BF16)
    if not last:
        scaled_ref[...] = scaled
    cot = cot_ref[...].reshape(flat)
    value = middle
    mid_back = jnp.zeros(flat, F32)
    for n, weight in enumerate(weights):
        units = weight.shape[0] * weight.shape[2]
        columns = pl.ds(n * units, units)
        gate_t, up_t, down = (weight[:, m].reshape(units, width) for m in range(3))
        gate_pre = times_transpose(scaled, gate_t)
        up_values = times_transpose(scaled, up_t)
        grad_hidden = times_transpose(cot, down)
        sigmoid = 1.0 / (1.0 + jnp.exp(-gate_pre))
        silu = gate_pre * sigmoid
        hidden = (silu * up_values).astype(BF16)
        gate_back = (
            grad_hidden * up_values * (sigmoid * (1.0 + gate_pre * (1.0 - sigmoid)))
        ).astype(BF16)
        up_back = (grad_hidden * silu).astype(BF16)
        if last:
            sums = [
                contract_rows(gate_back, scaled),
                contract_rows(up_back, scaled),
                contract_rows(hidden, cot),
            ]
            for e in range(earlier):
                *parts, right, right_cot = saved[5 * e : 5 * e + 5]
                right_cot = right_cot[...].reshape(-1, width)
                for m, part in enumerate(parts):
                    sums[m] += contract_rows(
                        part[:, columns], right_cot if m == 2 else right[...]
                    )
            for m in range(3):
                split = (weight.shape[0], weight.shape[2], width)
                sum_refs[n][:, m] = sums[m].astype(sum_refs[n].dtype).reshape(split)
        else:
            hidden_ref[:, columns] = hidden
            gate_ref[:, columns] = gate_back
            up_ref[:, columns] = up_back
        value = value + dot(hidden, down)
        mid_back = mid_back + (dot(gate_back, gate_t) + dot(up_back, up_t))
    block[...] = value.astype(BF16).reshape(shape)
    gain_out[...] = jnp.sum(mid_back * normed, axis=0, keepdims=True)
    total = cot.astype(F32) + norm_backward(mid_back, normed, factor, gain)
    grad[...] = total.reshape(shape)
    rounded = total.astype(BF16).reshape(shape)
    for i in range(low.shape[0]):
        low[i] = rounded


def mixing_kernel(
    bit_ref, flip_ref, plus_ref, minus_ref, sum_ref, rest_ref, stay_ref, away_ref, gain_ref
):
    rows = stay_ref.shape[1]

    @pl.when(pl.program_id(0) == 0)
    def _():
        gain_ref[...] = jnp.zeros_like(gain_ref)

    for n, out_ref in enumerate((stay_ref, away_ref)):
        here = pl.ds(pl.multiple_of((bit_ref[0] ^ n) * rows, rows), rows)
        plus, minus = (
            sum(dot(flip_ref[s, here, :], ref[s]) for s in range(flip_ref.shape[0]))
            for ref in (plus_ref, minus_ref)
        )
        out_ref[0] = (plus + minus).astype(out_ref.dtype)
        out_ref[1] = (plus - minus).astype(out_ref.dtype)
        gain_ref[here, :] += jnp.sum(
            plus * sum_ref[0, here, :].astype(F32) + minus * rest_ref[0, here, :].astype(F32),
            axis=1,
            keepdims=True,
        )


def resident(shape):
    zeros = (0,) * len(shape)
    return pl.BlockSpec(shape, lambda *_: zeros, pipeline_mode=pl.Buffered(1))


def mix_sequences(pieces, near, pairs, t00, t10, start, total, flips):
    parts = len(pieces)
    fars, count, _, height, width = pieces[0].shape
    half = t00.shape[1]
    block = pl.BlockSpec((fars, 1, 2, height, width), lambda n, *_: (0, n, 0, 0, 0))
    rows = t00.shape[2]
    flip = pl.BlockSpec((1, width, 4 * half), lambda n, *_: (start + n, 0, 0))
    return pl.pallas_call(
        functools.partial(mix_kernel, parts),
        grid_spec=pltpu.PrefetchScalarGridSpec(
            num_scalar_prefetch=1,
            grid=(count,),
            in_specs=[block] * parts
            + [resident(a.shape) for a in (*pairs, t00, t10)]
            + [pl.BlockSpec(memory_space=pl.ANY)] * len(flips),
            out_specs=[block] * parts + [flip],
            scratch_shapes=[
                pltpu.VMEM((4 * half, width), BF16),
                pltpu.VMEM((2, rows, width), BF16),
                pltpu.VMEM((2, rows, width), BF16),
                pltpu.VMEM((4 * half, width), F32),
            ],
        ),
        out_shape=[jax.ShapeDtypeStruct(pieces[0].shape, BF16)] * parts
        + [jax.ShapeDtypeStruct((total, width, 4 * half), BF16)],
        input_output_aliases={parts + 5: parts} if flips else {},
        compiler_params=pltpu.CompilerParams(vmem_limit_bytes=48 << 20),
        cost_estimate=pl.CostEstimate(
            flops=count * (16 * half * pairs[0].size + 12 * half * rows * width),
            bytes_accessed=4 * parts * pieces[0].size + 4 * pairs[0].size + 4 * t00.size,
            transcendentals=0,
        ),
        name="mix",
    )(near, *pieces, *pairs, t00, t10, *flips)


def mix_sequences_back(pieces, near, own, turned, u00, u10, lag_count, start, flips, before):
    parts = len(pieces)
    fars, count, _, height, width = pieces[0].shape
    half = u00.shape[2]
    block = pl.BlockSpec((fars, 1, 2, height, width), lambda n, *_: (0, n, 0, 0, 0))
    rows = u00.shape[1]
    slab = 2 * width // (parts * fars)
    lag_shape = (lag_count, slab, width)
    back_shape = (flips.shape[0], 4 * half, 2 * turned[0].shape[0])
    back = pl.BlockSpec((1, *back_shape[1:]), lambda n, *_: (start + n, 0, 0))
    slab_spec = pl.BlockSpec((1, slab, 4 * half), lambda n, _, own: (start + n, own[0], 0))
    return pl.pallas_call(
        functools.partial(mix_back_kernel, parts),
        grid_spec=pltpu.PrefetchScalarGridSpec(
            num_scalar_prefetch=2,
            grid=(count,),
            in_specs=[block] * parts
            + [resident(a.shape) for a in (*turned, u00, u10)]
            + [slab_spec]
            + ([pl.BlockSpec(memory_space=pl.ANY), resident(lag_shape)] if before else []),
            out_specs=[block] * parts + [back, resident(lag_shape)],
            scratch_shapes=[
                pltpu.VMEM((4 * half, width), BF16),
                pltpu.VMEM((4 * half, width), F32),
            ],
        ),
        out_shape=[jax.ShapeDtypeStruct(pieces[0].shape, BF16)] * parts
        + [
            jax.ShapeDtypeStruct(back_shape, BF16),
            jax.ShapeDtypeStruct(lag_shape, F32),
        ],
        input_output_aliases={parts + 7: parts} if before else {},
        compiler_params=pltpu.CompilerParams(vmem_limit_bytes=56 << 20),
        cost_estimate=pl.CostEstimate(
            flops=count * (16 * half * turned[0].size + 12 * half * rows * width),
            bytes_accessed=4 * parts * pieces[0].size + 8 * turned[0].size,
            transcendentals=0,
        ),
        name="mix_back",
    )(near, own, *pieces, *turned, u00, u10, flips, *before)


def mixing_products(flips, backs, pairs, bit, set_of):
    count, width, length = flips.shape
    slots = pairs.shape[0] // 2
    plus = pl.BlockSpec((count, length, width), lambda k, _: (0, 0, 2 * set_of * slots + k))
    minus = pl.BlockSpec(
        (count, length, width), lambda k, _: (0, 0, (2 * set_of + 1) * slots + k)
    )
    pair = pl.BlockSpec((1, width, width), lambda k, _: (k, 0, 0))
    rest = pl.BlockSpec((1, width, width), lambda k, _: (slots + k, 0, 0))
    half = pl.BlockSpec((2, width // 2, width), lambda k, _: (k, 0, 0))
    return pl.pallas_call(
        mixing_kernel,
        grid_spec=pltpu.PrefetchScalarGridSpec(
            num_scalar_prefetch=1,
            grid=(slots,),
            in_specs=[resident(flips.shape), plus, minus, pair, rest],
            out_specs=[half, half, resident((width, 1))],
        ),
        out_shape=[
            jax.ShapeDtypeStruct((2 * slots, width // 2, width), F32),
            jax.ShapeDtypeStruct((2 * slots, width // 2, width), BF16),
            jax.ShapeDtypeStruct((width, 1), F32),
        ],
        compiler_params=pltpu.CompilerParams(vmem_limit_bytes=56 << 20),
        cost_estimate=pl.CostEstimate(
            flops=backs.size * width,
            bytes_accessed=2 * flips.size + backs.size + 8 * slots * width * width,
            transcendentals=0,
        ),
        name="mixing_products",
    )(bit, flips, backs, backs, pairs, pairs)


def feed_forward(arrived, inputs, states, late, lag, gain, cot, weights, saved, last):
    rows, width = inputs.size // inputs.shape[-1], inputs.shape[-1]
    shares = len(weights)
    units = weights[0].shape[0] * weights[0].shape[2]
    flat_saved = [value for values in saved for value in values] if last else []
    operands = (arrived, inputs, states, late, lag, gain, cot, *weights, *flat_saved)
    whole = pl.BlockSpec(memory_space=pltpu.VMEM)
    if last:
        extra = [
            jax.ShapeDtypeStruct(weights[0].shape, F32 if n < shares // 2 else BF16)
            for n in range(shares)
        ]
    else:
        extra = [jax.ShapeDtypeStruct((rows, width), BF16)] + [
            jax.ShapeDtypeStruct((rows, shares * units), BF16)
        ] * 3
    return pl.pallas_call(
        functools.partial(feed_forward_kernel, shares, len(flat_saved) // 5, last),
        in_specs=[whole] * len(operands),
        out_specs=[whole] * (4 + len(extra)),
        out_shape=[
            jax.ShapeDtypeStruct(inputs.shape, BF16),
            jax.ShapeDtypeStruct(inputs.shape, F32),
            jax.ShapeDtypeStruct(arrived.shape, BF16),
            jax.ShapeDtypeStruct((1, width), F32),
            *extra,
        ],
        compiler_params=pltpu.CompilerParams(vmem_limit_bytes=56 << 20),
        cost_estimate=pl.CostEstimate(
            flops=(24 if last else 12) * rows * width * shares * units,
            bytes_accessed=6 * shares * units * width + 40 * rows * width,
            transcendentals=rows * shares * units,
        ),
        name="feed_forward",
    )(*operands)


def leading(values, edge):
    early = jnp.concatenate([values[:, :, 1:], edge], axis=2)
    return values, jnp.stack([values[:, 1], early[:, 0]], axis=1), early


def shards(inputs, filters, gain_in, mixing, regression, gain_mid, w_gate, w_up, w_down, out_grad):
    shard_rows, local_seqs, width = inputs.shape
    grid = Grid(lax.axis_size("filt"))
    row_count = lax.axis_size("rows")
    row_index = lax.axis_index("rows")
    bits = row_bits()
    index = lax.axis_index("filt")
    branches = mixing.shape[0]
    lag_count = regression.shape[0]
    height = shard_rows // 2
    chunks = CHUNKS
    step = local_seqs // chunks
    own_seqs = step // 2
    block = (own_seqs, 2, height, width)

    def inward(values):
        return values.reshape(height, 2, local_seqs, width).transpose(2, 1, 0, 3)

    def outward(values):
        return values.transpose(2, 1, 0, 3).reshape(shard_rows, local_seqs, width)

    def cut(values):
        return [values[c * step : (c + 1) * step] for c in range(chunks)]

    def to_mate(part):
        keep, away = grid.split(part.reshape(2, *block), grid.mate)
        return keep, grid.swap(away, grid.mate)

    def to_far(keep, received):
        pair = grid.join(keep, received, grid.mate)
        return pair, grid.swap(pair, grid.far)

    def to_near(pair, received):
        quad = grid.join(pair, received, grid.far).reshape(4, *block)
        return quad, near_swaps(grid, quad)

    def from_near(partial, received):
        total = total_of([partial[0], *received]).reshape(2, 2, *block)
        keep, away = grid.split(total, grid.far)
        return keep, away.astype(BF16)

    def from_far(keep, received):
        return grid.split((keep + received.astype(F32)).astype(BF16), grid.mate)

    def from_mate(keep, received):
        return grid.join(keep, received, grid.mate).reshape(step, 2, height, width)

    inputs_low = inward(inputs)
    residual = inputs_low.astype(F32)
    factor_in = rms_factor(residual)
    normed_in = residual * factor_in
    states = (normed_in * gain_in).astype(BF16)
    mates = [to_mate(part) for part in cut(states)]

    slots = (branches + 1) // 2
    first_branch = index * branches
    if branches % 2:
        odd_start = first_branch % 2
        paired = lax.dynamic_update_slice_in_dim(
            jnp.zeros((2 * slots,) + mixing.shape[1:], mixing.dtype), mixing, odd_start, 0
        )
    else:
        paired = mixing
    paired = tie(paired, mates[0][0])
    first, second = (paired[n::2].astype(F32) for n in range(2))
    own_pairs = jnp.concatenate([first + second, first - second], axis=0).astype(BF16)
    part_rows = width // row_count
    start = sum(
        jnp.where((row_index & bit) != 0, width >> (n + 1), 0) for n, bit in enumerate(bits)
    )
    own_part = lax.dynamic_slice_in_dim(own_pairs, start, part_rows, 1)
    hidden_own = w_down.shape[0]
    share = hidden_own // row_count
    w_gate, w_up, w_down = tie_all([w_gate, w_up, w_down], mates[0][0])
    packed = jnp.stack([w_gate.T, w_up.T, w_down])
    *early_bits, last_bit = grid.spread_bits()
    start = sum(
        jnp.where((row_index & bit) != 0, hidden_own >> (n + 1), 0) for n, bit in enumerate(bits)
    )
    shares = lax.dynamic_slice_in_dim(packed, start, share, 1)
    shares = grid.join(shares, grid.swap(shares, early_bits[0]), early_bits[0])
    mates = [(keep, tie(received, own_part)) for keep, received in mates]
    mate_part = grid.swap(tie(own_part, *(received for _, received in mates)), grid.mate)
    fars = [to_far(*values) for values in mates]
    received = [received for _, received in fars]
    edge = lax.ppermute(
        tie(states[:, :, -1:], *(pair for pair, _ in fars)),
        "filt",
        [(f, f + 1) for f in range(grid.size - 1)],
    )
    t00, t10, u00, u10 = toeplitz_blocks(
        tie(filters, *(pair for pair, _ in fars)),
        [first_branch // 2, (index ^ grid.mate) * branches // 2],
        slots,
    )
    mate_part, edge = tie_all([mate_part, edge], t00, received[0])
    mate_part = tie(mate_part, edge)
    for bit in early_bits[1:]:
        shares = tie(shares, mate_part)
        shares = grid.join(shares, grid.swap(shares, bit), bit)
    quads = [to_near(*values) for values in fars]
    mate_pairs = gather_rows(
        mate_part, [shares, *(value for _, values in quads for value in values)]
    )
    pairs = [own_pairs, mate_pairs]
    cotangent_low = inward(tie(out_grad, *received))

    near = jnp.reshape(index % grid.near, (1,)).astype(jnp.int32)
    late = jnp.concatenate([edge, states[:, :, :-1]], axis=2)
    quads[0] = (quads[0][0], tie_all(quads[0][1], *quads[-1][1]))
    late, inputs_low, cotangent_low, shares, *pieces = tied(
        late, inputs_low, cotangent_low, shares, quads[0][0], *quads[0][1]
    )

    partials, flips, near_received = [], [], []
    received = grid.swap(shares, last_bit)
    for c in range(chunks):
        if c:
            pieces = [quads[c][0], *quads[c][1]]
        *partial, flip = mix_sequences(
            pieces, near, pairs, t00, t10, c * own_seqs, chunks * own_seqs, flips
        )
        if c == 0:
            received = tie(received, partial[0])
            shares = grid.join(shares, received, last_bit)
        else:
            near_received[-1] = tie_all(near_received[-1], partial[0])
            partial = tie_all(partial, *near_received[-1])
        partials.append(partial)
        near_received.append(near_swaps(grid, partial))
        flips = [flip]
    kept_sums, from_fars, turned = [], [], []
    for c in range(chunks):
        kept_sums.append(from_near(partials[c], near_received[c]))
        from_fars.append(grid.swap(kept_sums[c][1], grid.far))
        if c == 0:
            turned = [
                value.transpose(0, 2, 1).reshape(2 * slots * width, width)
                for value in tie_all(pairs, kept_sums[0][1])
            ]
            from_fars[0] = tie(from_fars[0], *turned, *near_received[1])
    weights = [shares.reshape(grid.size, 3, share, width)]
    for n, bit in enumerate(reversed(bits)):
        received = [swap_rows(weight, bit) for weight in weights]
        if n == 0:
            received = tie_all(received, from_fars[0])
        weights = weights + received

    block_out, middle_grad, lows, fars, kept = [], [], [], [], []
    gain_mid_part = jnp.zeros((1, width), F32)
    for c in range(chunks):
        part = slice(c * step, (c + 1) * step)
        keep, away = from_far(kept_sums[c][0], from_fars[c])
        arrived = from_mate(keep, grid.swap(away, grid.mate))
        if c:
            arrived = tie(arrived, fars[-1][0])
        if c + 1 < chunks:
            arrived = tie(arrived, kept_sums[c + 1][1])
        cot = cotangent_low[part]
        value, grad, low, gain_part, *rest = feed_forward(
            arrived[None], inputs_low[part], states[part], late[part], regression,
            gain_mid[None], cot, weights, kept, c + 1 == chunks,
        )
        block_out.append(value)
        middle_grad.append(grad)
        gain_mid_part = gain_mid_part + gain_part
        if c + 1 < chunks:
            from_fars[c + 1] = tie(from_fars[c + 1], grad)
            low = tie(low, from_fars[c + 1])
        if c:
            fars[-1] = (fars[-1][0], tie(fars[-1][1], grad))
            low, *rest = tie_all([low, *rest], fars[-1][1])
        lows.append(low[0])
        fars.append(to_far(*to_mate(low[0])))
        if c + 1 < chunks:
            scaled, hidden, gate_back, up_back = rest
            kept.append((gate_back, up_back, hidden, scaled, cot))
    gain_mid_part = gain_mid_part[0]

    quads = [to_near(*values) for values in fars]

    half_count = len(rest) // 2
    values = [swap_rows(away, bits[0]) for away in rest[half_count:]]
    values = tie_all(values, *quads[0][1])
    sums_of = [[stay, value] for stay, value in zip(rest[:half_count], values, strict=True)]

    group = index // grid.far * grid.near + index % grid.near
    own = jnp.reshape(group, (1,)).astype(jnp.int32)
    before = ()
    back_partials, near_received = [], []
    mix_back = jnp.concatenate(lows, axis=0)
    next_edge = lax.ppermute(
        mix_back[:, :, :1], "filt", [(f + 1, f) for f in range(grid.size - 1)]
    )
    for bit in bits[1:-1]:
        half_count = len(sums_of) // 2
        values = [swap_rows(total_of(v).astype(BF16), bit) for v in sums_of[half_count:]]
        sums_of = [[*v, value] for v, value in zip(sums_of[:half_count], values, strict=True)]
    parts, away = sums_of
    half_count = away[0].shape[0] // 2
    away = total_of(away).astype(BF16)
    away = [away[:half_count], away[half_count:]]
    from_rows = [swap_rows(away[0], bits[-1])]
    first_quad, next_edge = tie_all([quads[0][0], next_edge], *away)
    quads[0] = (first_quad, quads[0][1])
    for c in range(chunks):
        quad, received = quads[c]
        if c + 1 < chunks:
            quad = tie(quad, quads[c + 1][0])
        *partial, backs, lag_sum = mix_sequences_back(
            [quad, *received], near, own, turned, u00, u10, lag_count, c * own_seqs, flip, before
        )
        before = (backs, lag_sum)
        if c + 1 < chunks:
            later_received = tie_all(quads[c + 1][1], partial[0])
            quads[c + 1] = (quads[c + 1][0], later_received)
            from_rows = [
                tie(from_rows[0], partial[0]), swap_rows(tie(away[1], partial[0]), bits[-1])
            ]
            partial = tie_all(partial, *later_received, from_rows[0])
        if c:
            near_received[-1] = tie_all(near_received[-1], partial[0])
            from_rows[-1] = tie(from_rows[-1], partial[0])
            lag_sum, backs, *partial = tie_all(
                [lag_sum, backs, *partial], *near_received[-1], from_rows[-1]
            )
        back_partials.append(partial)
        near_received.append(near_swaps(grid, partial))
    sums = [from_near(back_partials[0], near_received[0])]
    kept, value = row_step(tie(lag_sum, sums[0][1]), bits[0])
    lag_share = kept + value.astype(F32)
    kept, value = row_step(lag_share, bits[1])
    core_bit = jnp.reshape(row_index & 1, (1,)).astype(jnp.int32)
    mate_stay, mate_away, mate_gain = mixing_products(
        flip, tie(backs, sums[0][1], kept), mate_pairs, core_bit, 1
    )
    from_fars = [tie(grid.swap(sums[0][1], grid.far), mate_gain)]
    mate_stay, mate_away, mate_gain = tie_all([mate_stay, mate_away, mate_gain], from_fars[0])
    lag_share = kept + tie(value, mate_gain).astype(F32)
    for bit in bits[2:]:
        kept, value = row_step(lag_share, bit)
        lag_share = kept + value.astype(F32)
    lag_rows = lag_share.shape[1] // 2
    lag_share, lag_away = grid.split(
        lag_share.reshape(lag_count, 2, lag_rows, width).transpose(1, 0, 2, 3), grid.mate
    )
    lag_away = lag_away.astype(BF16)
    mate_sends = [from_far(sums[0][0], from_fars[0])]
    mate_share = mate_stay + swap_rows(mate_away, bits[0]).astype(F32)
    for c in range(1, chunks):
        sums.append(from_near(back_partials[c], tie_all(near_received[c], mate_gain)))
        from_fars.append(grid.swap(sums[c][1], grid.far))
    twos = (2,) * len(grid.spread_bits())
    grads = jnp.concatenate(
        [
            total_of([*(part[n * half_count : (n + 1) * half_count] for part in parts), value])
            for n, value in enumerate(tie_all(from_rows, mate_gain))
        ]
    ).reshape(*twos, 3, share, width)
    last_bits = grid.spread_bits()[::-1]
    grads, away = grid.split(grads, last_bits[0])
    away = away.astype(BF16)
    mate_kept, mate_away = row_halves(mate_share, bits[1])
    own_stay, own_away, own_gain = mixing_products(
        flip,
        tie(backs, mate_away, mate_sends[0][1], away, lag_away, *(v for _, v in sums[1:])),
        own_pairs, core_bit, 0,
    )
    from_mates = [tie(grid.swap(mate_sends[0][1], grid.mate), own_gain)]
    value = tie(swap_rows(mate_away, bits[1]), own_gain)
    mate_share = mate_kept + value.astype(F32)
    for bit in bits[2:]:
        kept, value = row_step(mate_share, bit)
        mate_share = kept + value.astype(F32)
    from_fars[1:] = tie_all(from_fars[1:], own_gain)
    own_gain = tie(own_gain, value, *from_mates, *from_fars[1:])
    grads = grads + tie(grid.swap(away, last_bits[0]), own_gain).astype(F32)
    lag_share = lag_share + tie(grid.swap(lag_away, grid.mate), own_gain).astype(F32)
    own_stay, own_away = tie_all([own_stay, own_away], own_gain)
    own_share = own_stay + swap_rows(own_away, bits[0]).astype(F32)
    for bit in bits[1:]:
        kept, value = row_step(own_share, bit)
        own_share = kept + value.astype(F32)
    received = grid.swap(mate_share.astype(BF16), grid.mate)
    mixing_low = (own_share + received.astype(F32)).astype(BF16)
    lag_share, mix_back, next_edge, grads, *block_out = tie_all(
        [lag_share, mix_back, next_edge, grads, *block_out], mixing_low
    )
    gain_column = mate_gain + own_gain
    for c in range(1, chunks):
        mate_sends.append(from_far(sums[c][0], from_fars[c]))
    from_mates += [grid.swap(away, grid.mate) for _, away in mate_sends[1:]]
    state_back = [
        from_mate(keep, received).astype(F32)
        for (keep, _), received in zip(mate_sends, from_mates, strict=True)
    ]
    mixing_grad = gather_rows(mixing_low).astype(F32)
    if branches % 2:
        mixing_grad = lax.dynamic_slice_in_dim(mixing_grad, odd_start, branches, 0)

    slab = width // grid.size * 2
    own_regression = lax.dynamic_slice_in_dim(regression, group * slab, slab, 1)
    gain_lag = jnp.sum(own_regression.astype(F32) * lag_sum, axis=(0, 2))
    gain_in_part = gain_column[:, 0]
    gain_in_part = lax.dynamic_update_slice_in_dim(
        gain_in_part,
        lax.dynamic_slice_in_dim(gain_in_part, group * slab, slab, 0) + gain_lag,
        group * slab,
        0,
    ) / gain_in
    gains = pair_sum(
        jnp.pad(jnp.stack([gain_in_part, gain_mid_part]), ((0, 6), (0, 0))), "rows"
    )
    gains = pair_sum(tie(gains, mixing_low), "filt")

    own_grads = reduce_filt(grid, grads, last_bits[1:]).astype(BF16)

    spread = gather_filt(grid, lag_share.astype(BF16))
    spread = (
        spread.reshape(grid.near, 2, 2, lag_count, lag_rows, width)
        .transpose(2, 0, 3, 1, 4, 5)
        .reshape(2 * grid.near * lag_count, 2 * lag_rows, width)
    )
    regression_grad = (
        gather_rows(spread)
        .reshape(2 * grid.near, lag_count, slab, width)
        .transpose(1, 0, 2, 3)
        .reshape(lag_count, width, width)
        .astype(F32)
    )

    lag_back = sum(
        jnp.einsum("spae,de->spad", lead, regression[n], preferred_element_type=F32)
        for n, lead in enumerate(leading(mix_back, next_edge))
    )
    input_grad = []
    for c in range(chunks):
        part = slice(c * step, (c + 1) * step)
        back = state_back[c] + lag_back[part]
        input_grad.append(
            middle_grad[c] + norm_backward(back, normed_in[part], factor_in[part], gain_in)
        )

    ordered = gather_rows(own_grads).astype(F32)
    return (
        outward(jnp.concatenate(block_out, axis=0)),
        outward(jnp.concatenate(input_grad, axis=0)),
        mixing_grad,
        regression_grad,
        gains[0],
        gains[1],
        ordered[0].T,
        ordered[1].T,
        ordered[2],
    )


def solution(mesh):
    placed = (
        P("filt", "rows", None),
        P(),
        P(),
        P("filt", None, None),
        P(),
        P(),
        P(None, "filt"),
        P(None, "filt"),
        P("filt", None),
        P("filt", "rows", None),
    )
    return jax.shard_map(
        shards,
        mesh=mesh,
        in_specs=placed,
        out_specs=(
            P("filt", "rows", None),
            P("filt", "rows", None),
            P("filt", None, None),
            P(),
            P(),
            P(),
            P(None, "filt"),
            P(None, "filt"),
            P("filt", None),
        ),
        check_vma=False,
    )
```

```python
import functools

import jax
import jax.numpy as jnp
from jax import lax
from jax.experimental import pallas as pl
from jax.experimental.pallas import tpu as pltpu
from jax.sharding import PartitionSpec as P

EPSILON = 1e-05
CHUNKS = 2
F32 = jnp.float32
BF16 = jnp.bfloat16


def dot(left, right):
    return jnp.dot(left, right, preferred_element_type=F32)


def contract_rows(left, right):
    return lax.dot_general(left, right, (((0,), (0,)), ((), ())), preferred_element_type=F32)


def times_transpose(left, right):
    return lax.dot_general(left, right, (((1,), (1,)), ((), ())), preferred_element_type=F32)


def rms_factor(values):
    return lax.rsqrt(jnp.mean(values * values, axis=-1, keepdims=True) + EPSILON)


def norm_backward(grad_out, normed, factor, gain):
    inner = grad_out * gain
    return factor * (inner - normed * jnp.mean(inner * normed, axis=-1, keepdims=True))


class Grid:
    def __init__(self, size):
        self.size = size
        self.near = size // 4
        self.mate = self.near
        self.far = 2 * self.near

    def near_bits(self):
        return [1 << n for n in range(self.near.bit_length() - 1)]

    def near_shift(self, step):
        near = self.near
        return [(f, f // near * near + (f % near + step) % near) for f in range(self.size)]

    def flag(self, bit):
        return (lax.axis_index("filt") & bit) != 0

    def swap(self, values, bit):
        return lax.ppermute(values, "filt", [(f, f ^ bit) for f in range(self.size)])

    def split(self, halves, bit):
        flag = self.flag(bit)
        return jnp.where(flag, halves[1], halves[0]), jnp.where(flag, halves[0], halves[1])

    def join(self, own, other, bit):
        return jnp.where(self.flag(bit), jnp.stack([other, own]), jnp.stack([own, other]))

    def spread_bits(self):
        return [self.far, self.mate, *self.near_bits()]


def gather_filt(grid, values):
    for bit in grid.spread_bits():
        values = grid.join(values, grid.swap(values, bit), bit)
    return values


def reduce_filt(grid, values, bits):
    for bit in bits:
        own, away = grid.split(values, bit)
        values = own.astype(F32) + grid.swap(away.astype(BF16), bit).astype(F32)
    return values


def tie(value, *others):
    return lax.optimization_barrier((value, *others))[0] if others else value


def tied(*values):
    return list(lax.optimization_barrier(values))


def tie_all(values, *others):
    count = len(values)
    return list(lax.optimization_barrier((*values, *others))[:count]) if others else list(values)


def near_swaps(grid, values):
    return [
        lax.ppermute(
            values[j] if isinstance(values, list) else values, "filt", grid.near_shift(j)
        )
        for j in range(1, grid.near)
    ]


def total_of(values):
    total = values[0].astype(F32)
    for value in values[1:]:
        total = total + value.astype(F32)
    return total


def swap_rows(values, bit):
    count = lax.axis_size("rows")
    return lax.ppermute(values, "rows", [(r, r ^ bit) for r in range(count)])


def row_bits():
    count = lax.axis_size("rows")
    return [1 << n for n in range(count.bit_length() - 1)]


def row_halves(values, bit):
    parts, height, width = values.shape
    halves = values.reshape(parts, 2, height // 2, width)
    high = (lax.axis_index("rows") & bit) != 0
    away = jnp.where(high, halves[:, 0], halves[:, 1]).astype(BF16)
    return jnp.where(high, halves[:, 1], halves[:, 0]), away


def row_step(values, bit):
    kept, away = row_halves(values, bit)
    return kept, swap_rows(away, bit)


def gather_rows(full, after=()):
    index = lax.axis_index("rows")
    for n, bit in enumerate(reversed(row_bits())):
        high = (index & bit) != 0
        other = swap_rows(full, bit)
        if n == 0:
            other = tie(other, *after)
        full = jnp.concatenate(
            [jnp.where(high, other, full), jnp.where(high, full, other)], axis=1
        )
    return full


def pair_sum(values, axis):
    count = lax.axis_size(axis)
    for bit in (1 << n for n in range(count.bit_length() - 1)):
        values = values + lax.ppermute(values, axis, [(r, r ^ bit) for r in range(count)])
    return values


def toeplitz_kernel(half, up_ref, t00_ref, t10_ref, u00_ref, u10_ref):
    width = up_ref.shape[-1]
    up = up_ref[0]

    def build(row, parities):
        block = pltpu.roll(
            jnp.broadcast_to(row, (half, width)), 0, axis=1, stride=1, stride_axis=0
        )
        u00, u10 = block[:, :half], block[:, half : 2 * half]
        for parity in parities:
            u00_ref[parity] = u00.astype(BF16)
            u10_ref[parity] = u10.astype(BF16)
            t00_ref[parity] = u00.T.astype(BF16)
            t10_ref[parity] = u10.T.astype(BF16)

    @pl.when(pl.program_id(0) % 2 == 0)
    def _():
        build(up, (0, 1))

    @pl.when(pl.program_id(0) % 2 == 1)
    def _():
        first = lax.broadcasted_iota(jnp.int32, up.shape, 1) == 0
        build(jnp.where(first, 0.0, pltpu.roll(up, 1, axis=1)), (0,))
        build(up, (1,))


def toeplitz_blocks(filters, firsts, each):
    count = each * len(firsts)
    length = filters.shape[1] // 2
    half = length // 2
    taps = jnp.concatenate(
        [lax.dynamic_slice_in_dim(filters, first, each, 0) for first in firsts], axis=0
    ).astype(BF16).astype(F32)
    taps = taps.reshape(count, length, 2).transpose(0, 2, 1).reshape(2 * count, 1, length)
    up = jnp.pad(taps, ((0, 0), (0, 0), (0, half)))
    by_column = pl.BlockSpec((2, half, half), lambda n: (0, 0, n))
    by_row = pl.BlockSpec((2, half, half), lambda n: (0, n, 0))
    line = pl.BlockSpec((1, 1, length + half), lambda n: (n, 0, 0))
    wide = jax.ShapeDtypeStruct((2, half, 2 * count * half), BF16)
    tall = jax.ShapeDtypeStruct((2, 2 * count * half, half), BF16)
    return pl.pallas_call(
        functools.partial(toeplitz_kernel, half),
        grid=(2 * count,),
        in_specs=[line],
        out_specs=[by_column, by_column, by_row, by_row],
        out_shape=[wide, wide, tall, tall],
        cost_estimate=pl.CostEstimate(
            flops=0, bytes_accessed=48 * count * half * half * 4, transcendentals=0
        ),
        name="toeplitz",
    )(up)


def places(near, pieces, whole_ref, sign):
    length = whole_ref.shape[0] // 2
    nears = len(pieces)
    fars, _, _, height, _ = pieces[0].shape
    for j, piece in enumerate(pieces):
        at = lax.rem(near + sign * j + nears, nears)
        for i in range(fars):
            for parity in range(2):
                start = parity * length + (i * nears + at) * height
                yield piece.at[i, 0, parity], pl.ds(pl.multiple_of(start, height), height)


def assemble(near, pieces, whole_ref):
    for piece, rows in places(near, pieces, whole_ref, -1):
        whole_ref[rows, :] = piece[...]


def scatter(near, whole_ref, pieces):
    for piece, rows in places(near, pieces, whole_ref, 1):
        piece[...] = whole_ref[rows, :].astype(piece.dtype)


def mix_kernel(parts, near_ref, *refs):
    pieces = refs[:parts]
    own_pair = refs[parts : parts + 2]
    mate_pair = refs[parts + 2 : parts + 4]
    t00_ref, t10_ref = refs[parts + 4 : parts + 6]
    outs = refs[-parts - 5 : -5]
    flip_ref, states_ref, low_ref, high_ref, sum_ref = refs[-5:]
    half = t00_ref.shape[1]
    slot = pl.program_id(1)
    slots = pl.num_programs(1)

    @pl.when(slot == 0)
    def _():
        assemble(near_ref[0], pieces, states_ref)
        sum_ref[...] = jnp.zeros_like(sum_ref)
        flip_ref[0] = states_ref[...].T

    for pm in range(2):
        mixing = jnp.where(slot < slots // 2, own_pair[pm][0], mate_pair[pm][0])
        rows = pl.ds(pm * half, half)
        value = dot(states_ref[...], mixing).astype(BF16)
        for quarter in range(4):
            part = value[quarter * half : (quarter + 1) * half]
            (low_ref, high_ref)[quarter % 2][quarter // 2 ^ pm, rows, :] = part

    for parity in range(2):
        base = 2 * parity * half
        sum_ref[pl.ds(base, half), :] += dot(t00_ref[parity], low_ref[parity])
        sum_ref[pl.ds(base + half, half), :] += dot(t10_ref[parity], low_ref[parity]) + dot(
            t00_ref[parity], high_ref[parity]
        )

    @pl.when(slot == slots - 1)
    def _():
        scatter(near_ref[0], sum_ref, outs)


def mix_back_kernel(parts, near_ref, own_ref, *refs):
    pieces = refs[:parts]
    turned = refs[parts : parts + 2]
    u00_ref, u10_ref, slab_ref = refs[parts + 2 : parts + 5]
    before = refs[parts + 5 : -parts - 4]
    outs = refs[-parts - 4 : -4]
    back_ref, lag_ref, grad_ref, sum_ref = refs[-4:]
    half = u00_ref.shape[2]
    width = grad_ref.shape[1]
    length = grad_ref.shape[0] // 2
    slot = pl.program_id(1)
    slots = pl.num_programs(1)

    @pl.when((pl.program_id(0) == 0) & (slot == 0))
    def _():
        lag_ref[...] = before[1][...] if before else jnp.zeros_like(lag_ref)

    @pl.when(slot == 0)
    def _():
        assemble(near_ref[0], pieces, grad_ref)
        sum_ref[...] = jnp.zeros_like(sum_ref)
        own = slab_ref[0].astype(F32)
        even, odd = own[:, :length], own[:, length:]
        first = lax.broadcasted_iota(jnp.int32, even.shape, 1) == 0
        even_late = jnp.where(first, 0.0, pltpu.roll(even, 1, axis=1))
        odd_late = jnp.where(first, 0.0, pltpu.roll(odd, 1, axis=1))
        for lag, (on_even, on_odd) in enumerate(
            ((even, odd), (odd_late, even), (even_late, odd_late))
        ):
            lag_ref[lag] += dot(on_even.astype(BF16), grad_ref[:length, :]) + dot(
                on_odd.astype(BF16), grad_ref[length:, :]
            )

    for parity in range(2):
        base = 2 * parity * half
        low = grad_ref[pl.ds(base, half), :]
        high = grad_ref[pl.ds(base + half, half), :]
        both = (dot(u00_ref[parity], low) + dot(u10_ref[parity], high)).astype(BF16)
        last = dot(u00_ref[parity], high).astype(BF16)
        for pm in range(2):
            columns = pl.ds(pm * width, width)
            target = 2 * half * (parity ^ pm)
            rows = slice(pm * half, (pm + 1) * half)
            back_ref[0, pl.ds(target, half), columns] = both[rows]
            back_ref[0, pl.ds(target + half, half), columns] = last[rows]

    for set_of in range(2):

        @pl.when((slot >= slots // 2) == bool(set_of))
        def _():
            sum_ref[...] += dot(back_ref[0], turned[set_of][...])

    @pl.when(slot == slots - 1)
    def _():
        scatter(near_ref[0], sum_ref, outs)


def feed_forward_kernel(
    shares, earlier, last, arrived, inputs, states, late, lag_ref, gain_ref, cot_ref, *refs
):
    weights = refs[:shares]
    saved = refs[shares : shares + 5 * earlier]
    block, grad, low, gain_out, *rest = refs[shares + 5 * earlier :]
    if last:
        sum_refs = rest
    else:
        scaled_ref, hidden_ref, gate_ref, up_ref = rest
    width = gain_ref.shape[1]
    shape = inputs.shape
    flat = (shape[0] * shape[1] * shape[2], width)

    spectral = arrived[0].astype(F32)
    for i in range(1, arrived.shape[0]):
        spectral = spectral + arrived[i].astype(F32)
    lags = (
        states[...],
        jnp.stack([late[:, 1], states[:, 0]], axis=1),
        late[...],
    )
    regress = sum(dot(lag.reshape(flat), lag_ref[n]) for n, lag in enumerate(lags))
    middle = (inputs[...].astype(F32) + spectral).reshape(flat) + regress
    factor = rms_factor(middle)
    normed = middle * factor
    gain = gain_ref[...]
    scaled = (normed * gain).astype(BF16)
    if not last:
        scaled_ref[...] = scaled
    cot = cot_ref[...].reshape(flat)
    value = middle
    mid_back = jnp.zeros(flat, F32)
    for n, weight in enumerate(weights):
        units = weight.shape[0] * weight.shape[2]
        columns = pl.ds(n * units, units)
        gate_t, up_t, down = (weight[:, m].reshape(units, width) for m in range(3))
        gate_pre = times_transpose(scaled, gate_t)
        up_values = times_transpose(scaled, up_t)
        grad_hidden = times_transpose(cot, down)
        sigmoid = 1.0 / (1.0 + jnp.exp(-gate_pre))
        silu = gate_pre * sigmoid
        hidden = (silu * up_values).astype(BF16)
        gate_back = (
            grad_hidden * up_values * (sigmoid * (1.0 + gate_pre * (1.0 - sigmoid)))
        ).astype(BF16)
        up_back = (grad_hidden * silu).astype(BF16)
        if last:
            sums = [
                contract_rows(gate_back, scaled),
                contract_rows(up_back, scaled),
                contract_rows(hidden, cot),
            ]
            for e in range(earlier):
                *parts, right, right_cot = saved[5 * e : 5 * e + 5]
                right_cot = right_cot[...].reshape(-1, width)
                for m, part in enumerate(parts):
                    sums[m] += contract_rows(
                        part[:, columns], right_cot if m == 2 else right[...]
                    )
            for m in range(3):
                split = (weight.shape[0], weight.shape[2], width)
                sum_refs[n][:, m] = sums[m].astype(sum_refs[n].dtype).reshape(split)
        else:
            hidden_ref[:, columns] = hidden
            gate_ref[:, columns] = gate_back
            up_ref[:, columns] = up_back
        value = value + dot(hidden, down)
        mid_back = mid_back + (dot(gate_back, gate_t) + dot(up_back, up_t))
    block[...] = value.astype(BF16).reshape(shape)
    gain_out[...] = jnp.sum(mid_back * normed, axis=0, keepdims=True)
    total = cot.astype(F32) + norm_backward(mid_back, normed, factor, gain)
    grad[...] = total.reshape(shape)
    rounded = total.astype(BF16).reshape(shape)
    for i in range(low.shape[0]):
        low[i] = rounded


def mixing_kernel(
    bit_ref, flip_ref, plus_ref, minus_ref, sum_ref, rest_ref, stay_ref, away_ref, gain_ref
):
    rows = stay_ref.shape[1]

    @pl.when(pl.program_id(0) == 0)
    def _():
        gain_ref[...] = jnp.zeros_like(gain_ref)

    for n, out_ref in enumerate((stay_ref, away_ref)):
        here = pl.ds(pl.multiple_of((bit_ref[0] ^ n) * rows, rows), rows)
        plus, minus = (
            sum(dot(flip_ref[s, here, :], ref[s]) for s in range(flip_ref.shape[0]))
            for ref in (plus_ref, minus_ref)
        )
        out_ref[0] = (plus + minus).astype(out_ref.dtype)
        out_ref[1] = (plus - minus).astype(out_ref.dtype)
        gain_ref[here, :] += jnp.sum(
            plus * sum_ref[0, here, :].astype(F32) + minus * rest_ref[0, here, :].astype(F32),
            axis=1,
            keepdims=True,
        )


def resident(shape):
    zeros = (0,) * len(shape)
    return pl.BlockSpec(shape, lambda *_: zeros, pipeline_mode=pl.Buffered(1))


def mix_sequences(pieces, near, pairs, t00, t10, start, total, flips):
    parts = len(pieces)
    fars, count, _, height, width = pieces[0].shape
    half = t00.shape[1]
    slots = pairs[0].shape[0] // 2
    block = pl.BlockSpec((fars, 1, 2, height, width), lambda n, *_: (0, n, 0, 0, 0))
    pair_specs = [
        pl.BlockSpec((1, width, width), lambda n, q, *_, pm=pm: (pm + jnp.minimum(q, slots - 1), 0, 0))
        for pm in (0, slots)
    ] + [
        pl.BlockSpec((1, width, width), lambda n, q, *_, pm=pm: (pm + jnp.maximum(q - slots, 0), 0, 0))
        for pm in (0, slots)
    ]
    line = pl.BlockSpec((2, half, 2 * half), lambda n, q, *_: (0, 0, q))
    flip = pl.BlockSpec((1, width, 4 * half), lambda n, *_: (start + n, 0, 0))
    return pl.pallas_call(
        functools.partial(mix_kernel, parts),
        grid_spec=pltpu.PrefetchScalarGridSpec(
            num_scalar_prefetch=1,
            grid=(count, 2 * slots),
            in_specs=[block] * parts
            + [*pair_specs, line, line]
            + [pl.BlockSpec(memory_space=pl.ANY)] * len(flips),
            out_specs=[block] * parts + [flip],
            scratch_shapes=[
                pltpu.VMEM((4 * half, width), BF16),
                pltpu.VMEM((2, 2 * half, width), BF16),
                pltpu.VMEM((2, 2 * half, width), BF16),
                pltpu.VMEM((4 * half, width), F32),
            ],
        ),
        out_shape=[jax.ShapeDtypeStruct(pieces[0].shape, BF16)] * parts
        + [jax.ShapeDtypeStruct((total, width, 4 * half), BF16)],
        input_output_aliases={parts + 7: parts} if flips else {},
        compiler_params=pltpu.CompilerParams(vmem_limit_bytes=48 << 20),
        cost_estimate=pl.CostEstimate(
            flops=count * (16 * half * pairs[0].size + 12 * half * t00.shape[2] * width),
            bytes_accessed=4 * parts * pieces[0].size + 4 * pairs[0].size + 4 * t00.size,
            transcendentals=0,
        ),
        name="mix",
    )(near, *pieces, pairs[0], pairs[0], pairs[1], pairs[1], t00, t10, *flips)


def mix_sequences_back(pieces, near, own, turned, u00, u10, lag_count, start, flips, before):
    parts = len(pieces)
    fars, count, _, height, width = pieces[0].shape
    half = u00.shape[2]
    block = pl.BlockSpec((fars, 1, 2, height, width), lambda n, *_: (0, n, 0, 0, 0))
    rows = u00.shape[1]
    slab = 2 * width // (parts * fars)
    lag_shape = (lag_count, slab, width)
    back_shape = (flips.shape[0], 4 * half, 2 * turned[0].shape[0])
    slots = turned[0].shape[0] // width // 2
    back = pl.BlockSpec((1, 4 * half, 2 * width), lambda n, q, *_: (start + n, 0, q))
    slab_spec = pl.BlockSpec((1, slab, 4 * half), lambda n, q, _, own: (start + n, own[0], 0))
    turned_specs = [
        pl.BlockSpec((2 * width, width), lambda n, q, *_: (jnp.minimum(q, slots - 1), 0)),
        pl.BlockSpec((2 * width, width), lambda n, q, *_: (jnp.maximum(q - slots, 0), 0)),
    ]
    line = pl.BlockSpec((2, 2 * half, half), lambda n, q, *_: (0, q, 0))
    return pl.pallas_call(
        functools.partial(mix_back_kernel, parts),
        grid_spec=pltpu.PrefetchScalarGridSpec(
            num_scalar_prefetch=2,
            grid=(count, 2 * slots),
            in_specs=[block] * parts
            + [*turned_specs, line, line, slab_spec]
            + ([pl.BlockSpec(memory_space=pl.ANY), resident(lag_shape)] if before else []),
            out_specs=[block] * parts + [back, resident(lag_shape)],
            scratch_shapes=[
                pltpu.VMEM((4 * half, width), BF16),
                pltpu.VMEM((4 * half, width), F32),
            ],
        ),
        out_shape=[jax.ShapeDtypeStruct(pieces[0].shape, BF16)] * parts
        + [
            jax.ShapeDtypeStruct(back_shape, BF16),
            jax.ShapeDtypeStruct(lag_shape, F32),
        ],
        input_output_aliases={parts + 7: parts} if before else {},
        compiler_params=pltpu.CompilerParams(vmem_limit_bytes=56 << 20),
        cost_estimate=pl.CostEstimate(
            flops=count * (16 * half * turned[0].size + 12 * half * rows * width),
            bytes_accessed=4 * parts * pieces[0].size + 8 * turned[0].size,
            transcendentals=0,
        ),
        name="mix_back",
    )(near, own, *pieces, *turned, u00, u10, flips, *before)


def mixing_products(flips, backs, pairs, bit, set_of):
    count, width, length = flips.shape
    slots = pairs.shape[0] // 2
    plus = pl.BlockSpec((count, length, width), lambda k, _: (0, 0, 2 * (set_of * slots + k)))
    minus = pl.BlockSpec(
        (count, length, width), lambda k, _: (0, 0, 2 * (set_of * slots + k) + 1)
    )
    pair = pl.BlockSpec((1, width, width), lambda k, _: (k, 0, 0))
    rest = pl.BlockSpec((1, width, width), lambda k, _: (slots + k, 0, 0))
    half = pl.BlockSpec((2, width // 2, width), lambda k, _: (k, 0, 0))
    return pl.pallas_call(
        mixing_kernel,
        grid_spec=pltpu.PrefetchScalarGridSpec(
            num_scalar_prefetch=1,
            grid=(slots,),
            in_specs=[resident(flips.shape), plus, minus, pair, rest],
            out_specs=[half, half, resident((width, 1))],
        ),
        out_shape=[
            jax.ShapeDtypeStruct((2 * slots, width // 2, width), F32),
            jax.ShapeDtypeStruct((2 * slots, width // 2, width), BF16),
            jax.ShapeDtypeStruct((width, 1), F32),
        ],
        compiler_params=pltpu.CompilerParams(vmem_limit_bytes=56 << 20),
        cost_estimate=pl.CostEstimate(
            flops=backs.size * width,
            bytes_accessed=2 * flips.size + backs.size + 8 * slots * width * width,
            transcendentals=0,
        ),
        name="mixing_products",
    )(bit, flips, backs, backs, pairs, pairs)


def feed_forward(arrived, inputs, states, late, lag, gain, cot, weights, saved, last):
    rows, width = inputs.size // inputs.shape[-1], inputs.shape[-1]
    shares = len(weights)
    units = weights[0].shape[0] * weights[0].shape[2]
    flat_saved = [value for values in saved for value in values] if last else []
    operands = (arrived, inputs, states, late, lag, gain, cot, *weights, *flat_saved)
    whole = pl.BlockSpec(memory_space=pltpu.VMEM)
    if last:
        extra = [
            jax.ShapeDtypeStruct(weights[0].shape, F32 if n < shares // 2 else BF16)
            for n in range(shares)
        ]
    else:
        extra = [jax.ShapeDtypeStruct((rows, width), BF16)] + [
            jax.ShapeDtypeStruct((rows, shares * units), BF16)
        ] * 3
    return pl.pallas_call(
        functools.partial(feed_forward_kernel, shares, len(flat_saved) // 5, last),
        in_specs=[whole] * len(operands),
        out_specs=[whole] * (4 + len(extra)),
        out_shape=[
            jax.ShapeDtypeStruct(inputs.shape, BF16),
            jax.ShapeDtypeStruct(inputs.shape, F32),
            jax.ShapeDtypeStruct(arrived.shape, BF16),
            jax.ShapeDtypeStruct((1, width), F32),
            *extra,
        ],
        compiler_params=pltpu.CompilerParams(vmem_limit_bytes=56 << 20),
        cost_estimate=pl.CostEstimate(
            flops=(24 if last else 12) * rows * width * shares * units,
            bytes_accessed=6 * shares * units * width + 40 * rows * width,
            transcendentals=rows * shares * units,
        ),
        name="feed_forward",
    )(*operands)


def leading(values, edge):
    early = jnp.concatenate([values[:, :, 1:], edge], axis=2)
    return values, jnp.stack([values[:, 1], early[:, 0]], axis=1), early


def shards(inputs, filters, gain_in, mixing, regression, gain_mid, w_gate, w_up, w_down, out_grad):
    shard_rows, local_seqs, width = inputs.shape
    grid = Grid(lax.axis_size("filt"))
    row_count = lax.axis_size("rows")
    row_index = lax.axis_index("rows")
    bits = row_bits()
    index = lax.axis_index("filt")
    branches = mixing.shape[0]
    lag_count = regression.shape[0]
    height = shard_rows // 2
    chunks = CHUNKS
    step = local_seqs // chunks
    own_seqs = step // 2
    block = (own_seqs, 2, height, width)

    def inward(values):
        return values.reshape(height, 2, local_seqs, width).transpose(2, 1, 0, 3)

    def outward(values):
        return values.transpose(2, 1, 0, 3).reshape(shard_rows, local_seqs, width)

    def cut(values):
        return [values[c * step : (c + 1) * step] for c in range(chunks)]

    def to_mate(part):
        keep, away = grid.split(part.reshape(2, *block), grid.mate)
        return keep, grid.swap(away, grid.mate)

    def to_far(keep, received):
        pair = grid.join(keep, received, grid.mate)
        return pair, grid.swap(pair, grid.far)

    def to_near(pair, received):
        quad = grid.join(pair, received, grid.far).reshape(4, *block)
        return quad, near_swaps(grid, quad)

    def from_near(partial, received):
        total = total_of([partial[0], *received]).reshape(2, 2, *block)
        keep, away = grid.split(total, grid.far)
        return keep, away.astype(BF16)

    def from_far(keep, received):
        return grid.split((keep + received.astype(F32)).astype(BF16), grid.mate)

    def from_mate(keep, received):
        return grid.join(keep, received, grid.mate).reshape(step, 2, height, width)

    inputs_low = inward(inputs)
    residual = inputs_low.astype(F32)
    factor_in = rms_factor(residual)
    normed_in = residual * factor_in
    states = (normed_in * gain_in).astype(BF16)
    mates = [to_mate(part) for part in cut(states)]

    slots = (branches + 1) // 2
    first_branch = index * branches
    if branches % 2:
        odd_start = first_branch % 2
        paired = lax.dynamic_update_slice_in_dim(
            jnp.zeros((2 * slots,) + mixing.shape[1:], mixing.dtype), mixing, odd_start, 0
        )
    else:
        paired = mixing
    paired = tie(paired, mates[0][0])
    first, second = (paired[n::2].astype(F32) for n in range(2))
    own_pairs = jnp.concatenate([first + second, first - second], axis=0).astype(BF16)
    part_rows = width // row_count
    start = sum(
        jnp.where((row_index & bit) != 0, width >> (n + 1), 0) for n, bit in enumerate(bits)
    )
    own_part = lax.dynamic_slice_in_dim(own_pairs, start, part_rows, 1)
    hidden_own = w_down.shape[0]
    share = hidden_own // row_count
    w_gate, w_up, w_down = tie_all([w_gate, w_up, w_down], mates[0][0])
    packed = jnp.stack([w_gate.T, w_up.T, w_down])
    *early_bits, last_bit = grid.spread_bits()
    start = sum(
        jnp.where((row_index & bit) != 0, hidden_own >> (n + 1), 0) for n, bit in enumerate(bits)
    )
    shares = lax.dynamic_slice_in_dim(packed, start, share, 1)
    shares = grid.join(shares, grid.swap(shares, early_bits[0]), early_bits[0])
    mates = [(keep, tie(received, own_part)) for keep, received in mates]
    mate_part = grid.swap(tie(own_part, *(received for _, received in mates)), grid.mate)
    fars = [to_far(*values) for values in mates]
    received = [received for _, received in fars]
    edge = lax.ppermute(
        tie(states[:, :, -1:], *(pair for pair, _ in fars)),
        "filt",
        [(f, f + 1) for f in range(grid.size - 1)],
    )
    t00, t10, u00, u10 = toeplitz_blocks(
        tie(filters, *(pair for pair, _ in fars)),
        [first_branch // 2, (index ^ grid.mate) * branches // 2],
        slots,
    )
    mate_part, edge = tie_all([mate_part, edge], t00, received[0])
    mate_part = tie(mate_part, edge)
    for bit in early_bits[1:]:
        shares = tie(shares, mate_part)
        shares = grid.join(shares, grid.swap(shares, bit), bit)
    quads = [to_near(*values) for values in fars]
    mate_pairs = gather_rows(
        mate_part, [shares, *(value for _, values in quads for value in values)]
    )
    pairs = [own_pairs, mate_pairs]
    cotangent_low = inward(tie(out_grad, *received))

    near = jnp.reshape(index % grid.near, (1,)).astype(jnp.int32)
    late = jnp.concatenate([edge, states[:, :, :-1]], axis=2)
    quads[0] = (quads[0][0], tie_all(quads[0][1], *quads[-1][1]))
    late, inputs_low, cotangent_low, shares, *pieces = tied(
        late, inputs_low, cotangent_low, shares, quads[0][0], *quads[0][1]
    )

    partials, flips, near_received = [], [], []
    received = grid.swap(shares, last_bit)
    for c in range(chunks):
        if c:
            pieces = [quads[c][0], *quads[c][1]]
        *partial, flip = mix_sequences(
            pieces, near, pairs, t00, t10, c * own_seqs, chunks * own_seqs, flips
        )
        if c == 0:
            received = tie(received, partial[0])
            shares = grid.join(shares, received, last_bit)
        else:
            near_received[-1] = tie_all(near_received[-1], partial[0])
            partial = tie_all(partial, *near_received[-1])
        partials.append(partial)
        near_received.append(near_swaps(grid, partial))
        flips = [flip]
    kept_sums, from_fars, turned = [], [], []
    for c in range(chunks):
        kept_sums.append(from_near(partials[c], near_received[c]))
        from_fars.append(grid.swap(kept_sums[c][1], grid.far))
        if c == 0:
            turned = [
                value.reshape(2, slots, width, width)
                .transpose(1, 0, 3, 2)
                .reshape(2 * slots * width, width)
                for value in tie_all(pairs, kept_sums[0][1])
            ]
            from_fars[0] = tie(from_fars[0], *turned, *near_received[1])
    weights = [shares.reshape(grid.size, 3, share, width)]
    for n, bit in enumerate(reversed(bits)):
        received = [swap_rows(weight, bit) for weight in weights]
        if n == 0:
            received = tie_all(received, from_fars[0])
        weights = weights + received

    block_out, middle_grad, lows, fars, kept = [], [], [], [], []
    gain_mid_part = jnp.zeros((1, width), F32)
    for c in range(chunks):
        part = slice(c * step, (c + 1) * step)
        keep, away = from_far(kept_sums[c][0], from_fars[c])
        arrived = from_mate(keep, grid.swap(away, grid.mate))
        if c:
            arrived = tie(arrived, fars[-1][0])
        if c + 1 < chunks:
            arrived = tie(arrived, kept_sums[c + 1][1])
        cot = cotangent_low[part]
        value, grad, low, gain_part, *rest = feed_forward(
            arrived[None], inputs_low[part], states[part], late[part], regression,
            gain_mid[None], cot, weights, kept, c + 1 == chunks,
        )
        block_out.append(value)
        middle_grad.append(grad)
        gain_mid_part = gain_mid_part + gain_part
        if c + 1 < chunks:
            from_fars[c + 1] = tie(from_fars[c + 1], grad)
            low = tie(low, from_fars[c + 1])
        if c:
            fars[-1] = (fars[-1][0], tie(fars[-1][1], grad))
            low, *rest = tie_all([low, *rest], fars[-1][1])
        lows.append(low[0])
        fars.append(to_far(*to_mate(low[0])))
        if c + 1 < chunks:
            scaled, hidden, gate_back, up_back = rest
            kept.append((gate_back, up_back, hidden, scaled, cot))
    gain_mid_part = gain_mid_part[0]

    quads = [to_near(*values) for values in fars]

    half_count = len(rest) // 2
    values = [swap_rows(away, bits[0]) for away in rest[half_count:]]
    values = tie_all(values, *quads[0][1])
    sums_of = [[stay, value] for stay, value in zip(rest[:half_count], values, strict=True)]

    group = index // grid.far * grid.near + index % grid.near
    own = jnp.reshape(group, (1,)).astype(jnp.int32)
    before = ()
    back_partials, near_received = [], []
    mix_back = jnp.concatenate(lows, axis=0)
    next_edge = lax.ppermute(
        mix_back[:, :, :1], "filt", [(f + 1, f) for f in range(grid.size - 1)]
    )
    for bit in bits[1:-1]:
        half_count = len(sums_of) // 2
        values = [swap_rows(total_of(v).astype(BF16), bit) for v in sums_of[half_count:]]
        sums_of = [[*v, value] for v, value in zip(sums_of[:half_count], values, strict=True)]
    parts, away = sums_of
    half_count = away[0].shape[0] // 2
    away = total_of(away).astype(BF16)
    away = [away[:half_count], away[half_count:]]
    from_rows = [swap_rows(away[0], bits[-1])]
    first_quad, next_edge = tie_all([quads[0][0], next_edge], *away)
    quads[0] = (first_quad, quads[0][1])
    for c in range(chunks):
        quad, received = quads[c]
        if c + 1 < chunks:
            quad = tie(quad, quads[c + 1][0])
        *partial, backs, lag_sum = mix_sequences_back(
            [quad, *received], near, own, turned, u00, u10, lag_count, c * own_seqs, flip, before
        )
        before = (backs, lag_sum)
        if c + 1 < chunks:
            later_received = tie_all(quads[c + 1][1], partial[0])
            quads[c + 1] = (quads[c + 1][0], later_received)
            from_rows = [
                tie(from_rows[0], partial[0]), swap_rows(tie(away[1], partial[0]), bits[-1])
            ]
            partial = tie_all(partial, *later_received, from_rows[0])
        if c:
            near_received[-1] = tie_all(near_received[-1], partial[0])
            from_rows[-1] = tie(from_rows[-1], partial[0])
            lag_sum, backs, *partial = tie_all(
                [lag_sum, backs, *partial], *near_received[-1], from_rows[-1]
            )
        back_partials.append(partial)
        near_received.append(near_swaps(grid, partial))
    sums = [from_near(back_partials[0], near_received[0])]
    kept, value = row_step(tie(lag_sum, sums[0][1]), bits[0])
    lag_share = kept + value.astype(F32)
    kept, value = row_step(lag_share, bits[1])
    core_bit = jnp.reshape(row_index & 1, (1,)).astype(jnp.int32)
    mate_stay, mate_away, mate_gain = mixing_products(
        flip, tie(backs, sums[0][1], kept), mate_pairs, core_bit, 1
    )
    from_fars = [tie(grid.swap(sums[0][1], grid.far), mate_gain)]
    mate_stay, mate_away, mate_gain = tie_all([mate_stay, mate_away, mate_gain], from_fars[0])
    lag_share = kept + tie(value, mate_gain).astype(F32)
    for bit in bits[2:]:
        kept, value = row_step(lag_share, bit)
        lag_share = kept + value.astype(F32)
    lag_rows = lag_share.shape[1] // 2
    lag_share, lag_away = grid.split(
        lag_share.reshape(lag_count, 2, lag_rows, width).transpose(1, 0, 2, 3), grid.mate
    )
    lag_away = lag_away.astype(BF16)
    mate_sends = [from_far(sums[0][0], from_fars[0])]
    mate_share = mate_stay + swap_rows(mate_away, bits[0]).astype(F32)
    for c in range(1, chunks):
        sums.append(from_near(back_partials[c], tie_all(near_received[c], mate_gain)))
        from_fars.append(grid.swap(sums[c][1], grid.far))
    twos = (2,) * len(grid.spread_bits())
    grads = jnp.concatenate(
        [
            total_of([*(part[n * half_count : (n + 1) * half_count] for part in parts), value])
            for n, value in enumerate(tie_all(from_rows, mate_gain))
        ]
    ).reshape(*twos, 3, share, width)
    last_bits = grid.spread_bits()[::-1]
    grads, away = grid.split(grads, last_bits[0])
    away = away.astype(BF16)
    mate_kept, mate_away = row_halves(mate_share, bits[1])
    own_stay, own_away, own_gain = mixing_products(
        flip,
        tie(backs, mate_away, mate_sends[0][1], away, lag_away, *(v for _, v in sums[1:])),
        own_pairs, core_bit, 0,
    )
    from_mates = [tie(grid.swap(mate_sends[0][1], grid.mate), own_gain)]
    value = tie(swap_rows(mate_away, bits[1]), own_gain)
    mate_share = mate_kept + value.astype(F32)
    for bit in bits[2:]:
        kept, value = row_step(mate_share, bit)
        mate_share = kept + value.astype(F32)
    from_fars[1:] = tie_all(from_fars[1:], own_gain)
    own_gain = tie(own_gain, value, *from_mates, *from_fars[1:])
    grads = grads + tie(grid.swap(away, last_bits[0]), own_gain).astype(F32)
    lag_share = lag_share + tie(grid.swap(lag_away, grid.mate), own_gain).astype(F32)
    own_stay, own_away = tie_all([own_stay, own_away], own_gain)
    own_share = own_stay + swap_rows(own_away, bits[0]).astype(F32)
    for bit in bits[1:]:
        kept, value = row_step(own_share, bit)
        own_share = kept + value.astype(F32)
    received = grid.swap(mate_share.astype(BF16), grid.mate)
    mixing_low = (own_share + received.astype(F32)).astype(BF16)
    lag_share, mix_back, next_edge, grads, *block_out = tie_all(
        [lag_share, mix_back, next_edge, grads, *block_out], mixing_low
    )
    gain_column = mate_gain + own_gain
    for c in range(1, chunks):
        mate_sends.append(from_far(sums[c][0], from_fars[c]))
    from_mates += [grid.swap(away, grid.mate) for _, away in mate_sends[1:]]
    state_back = [
        from_mate(keep, received).astype(F32)
        for (keep, _), received in zip(mate_sends, from_mates, strict=True)
    ]
    mixing_grad = gather_rows(mixing_low).astype(F32)
    if branches % 2:
        mixing_grad = lax.dynamic_slice_in_dim(mixing_grad, odd_start, branches, 0)

    slab = width // grid.size * 2
    own_regression = lax.dynamic_slice_in_dim(regression, group * slab, slab, 1)
    gain_lag = jnp.sum(own_regression.astype(F32) * lag_sum, axis=(0, 2))
    gain_in_part = gain_column[:, 0]
    gain_in_part = lax.dynamic_update_slice_in_dim(
        gain_in_part,
        lax.dynamic_slice_in_dim(gain_in_part, group * slab, slab, 0) + gain_lag,
        group * slab,
        0,
    ) / gain_in
    gains = pair_sum(
        jnp.pad(jnp.stack([gain_in_part, gain_mid_part]), ((0, 6), (0, 0))), "rows"
    )
    gains = pair_sum(tie(gains, mixing_low), "filt")

    own_grads = reduce_filt(grid, grads, last_bits[1:]).astype(BF16)

    spread = gather_filt(grid, lag_share.astype(BF16))
    spread = (
        spread.reshape(grid.near, 2, 2, lag_count, lag_rows, width)
        .transpose(2, 0, 3, 1, 4, 5)
        .reshape(2 * grid.near * lag_count, 2 * lag_rows, width)
    )
    regression_grad = (
        gather_rows(spread)
        .reshape(2 * grid.near, lag_count, slab, width)
        .transpose(1, 0, 2, 3)
        .reshape(lag_count, width, width)
        .astype(F32)
    )

    lag_back = sum(
        jnp.einsum("spae,de->spad", lead, regression[n], preferred_element_type=F32)
        for n, lead in enumerate(leading(mix_back, next_edge))
    )
    input_grad = []
    for c in range(chunks):
        part = slice(c * step, (c + 1) * step)
        back = state_back[c] + lag_back[part]
        input_grad.append(
            middle_grad[c] + norm_backward(back, normed_in[part], factor_in[part], gain_in)
        )

    ordered = gather_rows(own_grads).astype(F32)
    return (
        outward(jnp.concatenate(block_out, axis=0)),
        outward(jnp.concatenate(input_grad, axis=0)),
        mixing_grad,
        regression_grad,
        gains[0],
        gains[1],
        ordered[0].T,
        ordered[1].T,
        ordered[2],
    )


def solution(mesh):
    placed = (
        P("filt", "rows", None),
        P(),
        P(),
        P("filt", None, None),
        P(),
        P(),
        P(None, "filt"),
        P(None, "filt"),
        P("filt", None),
        P("filt", "rows", None),
    )
    return jax.shard_map(
        shards,
        mesh=mesh,
        in_specs=placed,
        out_specs=(
            P("filt", "rows", None),
            P("filt", "rows", None),
            P("filt", None, None),
            P(),
            P(),
            P(),
            P(None, "filt"),
            P(None, "filt"),
            P("filt", None),
        ),
        check_vma=False,
    )
```

```python
import functools

import jax
import jax.numpy as jnp
from jax import lax
from jax.experimental import pallas as pl
from jax.experimental.pallas import tpu as pltpu
from jax.sharding import PartitionSpec as P

EPSILON = 1e-05
CHUNKS = 2
F32 = jnp.float32
BF16 = jnp.bfloat16


def dot(left, right):
    return jnp.dot(left, right, preferred_element_type=F32)


def contract_rows(left, right):
    return lax.dot_general(left, right, (((0,), (0,)), ((), ())), preferred_element_type=F32)


def times_transpose(left, right):
    return lax.dot_general(left, right, (((1,), (1,)), ((), ())), preferred_element_type=F32)


def rms_factor(values):
    return lax.rsqrt(jnp.mean(values * values, axis=-1, keepdims=True) + EPSILON)


def norm_backward(grad_out, normed, factor, gain):
    inner = grad_out * gain
    return factor * (inner - normed * jnp.mean(inner * normed, axis=-1, keepdims=True))


class Grid:
    def __init__(self, size):
        self.size = size
        self.near = size // 4
        self.mate = self.near
        self.far = 2 * self.near

    def near_bits(self):
        return [1 << n for n in range(self.near.bit_length() - 1)]

    def near_shift(self, step):
        near = self.near
        return [(f, f // near * near + (f % near + step) % near) for f in range(self.size)]

    def flag(self, bit):
        return (lax.axis_index("filt") & bit) != 0

    def swap(self, values, bit):
        return lax.ppermute(values, "filt", [(f, f ^ bit) for f in range(self.size)])

    def split(self, halves, bit):
        flag = self.flag(bit)
        return jnp.where(flag, halves[1], halves[0]), jnp.where(flag, halves[0], halves[1])

    def join(self, own, other, bit):
        return jnp.where(self.flag(bit), jnp.stack([other, own]), jnp.stack([own, other]))

    def spread_bits(self):
        return [self.far, self.mate, *self.near_bits()]


def gather_filt(grid, values):
    for bit in grid.spread_bits():
        values = grid.join(values, grid.swap(values, bit), bit)
    return values


def reduce_filt(grid, values, bits):
    for bit in bits:
        own, away = grid.split(values, bit)
        values = own.astype(F32) + grid.swap(away.astype(BF16), bit).astype(F32)
    return values


def tie(value, *others):
    return lax.optimization_barrier((value, *others))[0] if others else value


def tied(*values):
    return list(lax.optimization_barrier(values))


def tie_all(values, *others):
    count = len(values)
    return list(lax.optimization_barrier((*values, *others))[:count]) if others else list(values)


def near_swaps(grid, values):
    return [
        lax.ppermute(
            values[j] if isinstance(values, list) else values, "filt", grid.near_shift(j)
        )
        for j in range(1, grid.near)
    ]


def total_of(values):
    total = values[0].astype(F32)
    for value in values[1:]:
        total = total + value.astype(F32)
    return total


def swap_rows(values, bit):
    count = lax.axis_size("rows")
    return lax.ppermute(values, "rows", [(r, r ^ bit) for r in range(count)])


def row_bits():
    count = lax.axis_size("rows")
    return [1 << n for n in range(count.bit_length() - 1)]


def row_halves(values, bit):
    parts, height, width = values.shape
    halves = values.reshape(parts, 2, height // 2, width)
    high = (lax.axis_index("rows") & bit) != 0
    away = jnp.where(high, halves[:, 0], halves[:, 1]).astype(BF16)
    return jnp.where(high, halves[:, 1], halves[:, 0]), away


def row_step(values, bit):
    kept, away = row_halves(values, bit)
    return kept, swap_rows(away, bit)


def gather_rows(full, after=()):
    index = lax.axis_index("rows")
    for n, bit in enumerate(reversed(row_bits())):
        high = (index & bit) != 0
        other = swap_rows(full, bit)
        if n == 0:
            other = tie(other, *after)
        parts, height, width = full.shape
        full = jnp.where(
            high, jnp.stack([other, full], axis=1), jnp.stack([full, other], axis=1)
        ).reshape(parts, 2 * height, width)
    return full


def pair_sum(values, axis):
    count = lax.axis_size(axis)
    for bit in (1 << n for n in range(count.bit_length() - 1)):
        values = values + lax.ppermute(values, axis, [(r, r ^ bit) for r in range(count)])
    return values


def toeplitz_kernel(half, up_ref, t00_ref, t10_ref, u00_ref, u10_ref):
    width = up_ref.shape[-1]
    up = up_ref[0]

    def build(row, parities):
        block = pltpu.roll(
            jnp.broadcast_to(row, (half, width)), 0, axis=1, stride=1, stride_axis=0
        )
        u00, u10 = block[:, :half], block[:, half : 2 * half]
        for parity in parities:
            u00_ref[parity] = u00.astype(BF16)
            u10_ref[parity] = u10.astype(BF16)
            t00_ref[parity] = u00.T.astype(BF16)
            t10_ref[parity] = u10.T.astype(BF16)

    @pl.when(pl.program_id(0) % 2 == 0)
    def _():
        build(up, (0, 1))

    @pl.when(pl.program_id(0) % 2 == 1)
    def _():
        first = lax.broadcasted_iota(jnp.int32, up.shape, 1) == 0
        build(jnp.where(first, 0.0, pltpu.roll(up, 1, axis=1)), (0,))
        build(up, (1,))


def toeplitz_blocks(filters, firsts, each):
    count = each * len(firsts)
    length = filters.shape[1] // 2
    half = length // 2
    taps = jnp.concatenate(
        [lax.dynamic_slice_in_dim(filters, first, each, 0) for first in firsts], axis=0
    ).astype(BF16).astype(F32)
    taps = taps.reshape(count, length, 2).transpose(0, 2, 1).reshape(2 * count, 1, length)
    up = jnp.pad(taps, ((0, 0), (0, 0), (0, half)))
    by_column = pl.BlockSpec((2, half, half), lambda n: (0, 0, n))
    by_row = pl.BlockSpec((2, half, half), lambda n: (0, n, 0))
    line = pl.BlockSpec((1, 1, length + half), lambda n: (n, 0, 0))
    wide = jax.ShapeDtypeStruct((2, half, 2 * count * half), BF16)
    tall = jax.ShapeDtypeStruct((2, 2 * count * half, half), BF16)
    return pl.pallas_call(
        functools.partial(toeplitz_kernel, half),
        grid=(2 * count,),
        in_specs=[line],
        out_specs=[by_column, by_column, by_row, by_row],
        out_shape=[wide, wide, tall, tall],
        cost_estimate=pl.CostEstimate(
            flops=0, bytes_accessed=48 * count * half * half * 4, transcendentals=0
        ),
        name="toeplitz",
    )(up)


def places(near, pieces, whole_ref, sign):
    length = whole_ref.shape[0] // 2
    nears = len(pieces)
    fars, _, _, height, _ = pieces[0].shape
    for j, piece in enumerate(pieces):
        at = lax.rem(near + sign * j + nears, nears)
        for i in range(fars):
            for parity in range(2):
                start = parity * length + (i * nears + at) * height
                yield piece.at[i, 0, parity], pl.ds(pl.multiple_of(start, height), height)


def assemble(near, pieces, whole_ref):
    for piece, rows in places(near, pieces, whole_ref, -1):
        whole_ref[rows, :] = piece[...]


def scatter(near, whole_ref, pieces):
    for piece, rows in places(near, pieces, whole_ref, 1):
        piece[...] = whole_ref[rows, :].astype(piece.dtype)


def mix_kernel(parts, near_ref, *refs):
    pieces = refs[:parts]
    own_pair = refs[parts : parts + 2]
    mate_pair = refs[parts + 2 : parts + 4]
    t00_ref, t10_ref = refs[parts + 4 : parts + 6]
    outs = refs[-parts - 5 : -5]
    flip_ref, states_ref, low_ref, high_ref, sum_ref = refs[-5:]
    half = t00_ref.shape[1]
    slot = pl.program_id(1)
    slots = pl.num_programs(1)

    @pl.when(slot == 0)
    def _():
        assemble(near_ref[0], pieces, states_ref)
        sum_ref[...] = jnp.zeros_like(sum_ref)
        flip_ref[0] = states_ref[...].T

    for pm in range(2):
        mixing = jnp.where(slot < slots // 2, own_pair[pm][0], mate_pair[pm][0])
        rows = pl.ds(pm * half, half)
        value = dot(states_ref[...], mixing).astype(BF16)
        for quarter in range(4):
            part = value[quarter * half : (quarter + 1) * half]
            (low_ref, high_ref)[quarter % 2][quarter // 2 ^ pm, rows, :] = part

    for parity in range(2):
        base = 2 * parity * half
        sum_ref[pl.ds(base, half), :] += dot(t00_ref[parity], low_ref[parity])
        sum_ref[pl.ds(base + half, half), :] += dot(t10_ref[parity], low_ref[parity]) + dot(
            t00_ref[parity], high_ref[parity]
        )

    @pl.when(slot == slots - 1)
    def _():
        scatter(near_ref[0], sum_ref, outs)


def mix_back_kernel(parts, near_ref, own_ref, *refs):
    pieces = refs[:parts]
    turned = refs[parts : parts + 2]
    u00_ref, u10_ref, slab_ref = refs[parts + 2 : parts + 5]
    before = refs[parts + 5 : -parts - 4]
    outs = refs[-parts - 4 : -4]
    back_ref, lag_ref, grad_ref, sum_ref = refs[-4:]
    half = u00_ref.shape[2]
    width = grad_ref.shape[1]
    length = grad_ref.shape[0] // 2
    slot = pl.program_id(1)
    slots = pl.num_programs(1)

    @pl.when((pl.program_id(0) == 0) & (slot == 0))
    def _():
        lag_ref[...] = before[1][...] if before else jnp.zeros_like(lag_ref)

    @pl.when(slot == 0)
    def _():
        assemble(near_ref[0], pieces, grad_ref)
        sum_ref[...] = jnp.zeros_like(sum_ref)
        own = slab_ref[0].astype(F32)
        even, odd = own[:, :length], own[:, length:]
        first = lax.broadcasted_iota(jnp.int32, even.shape, 1) == 0
        even_late = jnp.where(first, 0.0, pltpu.roll(even, 1, axis=1))
        odd_late = jnp.where(first, 0.0, pltpu.roll(odd, 1, axis=1))
        for lag, (on_even, on_odd) in enumerate(
            ((even, odd), (odd_late, even), (even_late, odd_late))
        ):
            lag_ref[lag] += dot(on_even.astype(BF16), grad_ref[:length, :]) + dot(
                on_odd.astype(BF16), grad_ref[length:, :]
            )

    for parity in range(2):
        base = 2 * parity * half
        low = grad_ref[pl.ds(base, half), :]
        high = grad_ref[pl.ds(base + half, half), :]
        both = (dot(u00_ref[parity], low) + dot(u10_ref[parity], high)).astype(BF16)
        last = dot(u00_ref[parity], high).astype(BF16)
        for pm in range(2):
            columns = pl.ds(pm * width, width)
            target = 2 * half * (parity ^ pm)
            rows = slice(pm * half, (pm + 1) * half)
            back_ref[0, pl.ds(target, half), columns] = both[rows]
            back_ref[0, pl.ds(target + half, half), columns] = last[rows]

    for set_of in range(2):

        @pl.when((slot >= slots // 2) == bool(set_of))
        def _():
            sum_ref[...] += dot(back_ref[0], turned[set_of][...])

    @pl.when(slot == slots - 1)
    def _():
        scatter(near_ref[0], sum_ref, outs)


def feed_forward_kernel(
    shares, earlier, last, arrived, inputs, states, late, lag_ref, gain_ref, cot_ref, *refs
):
    weights = refs[:shares]
    saved = refs[shares : shares + 5 * earlier]
    block, grad, low, gain_out, *rest = refs[shares + 5 * earlier :]
    if last:
        sum_refs = rest
    else:
        scaled_ref, hidden_ref, gate_ref, up_ref = rest
    width = gain_ref.shape[1]
    shape = inputs.shape
    flat = (shape[0] * shape[1] * shape[2], width)

    spectral = arrived[0].astype(F32)
    for i in range(1, arrived.shape[0]):
        spectral = spectral + arrived[i].astype(F32)
    lags = (
        states[...],
        jnp.stack([late[:, 1], states[:, 0]], axis=1),
        late[...],
    )
    regress = sum(dot(lag.reshape(flat), lag_ref[n]) for n, lag in enumerate(lags))
    middle = (inputs[...].astype(F32) + spectral).reshape(flat) + regress
    factor = rms_factor(middle)
    normed = middle * factor
    gain = gain_ref[...]
    scaled = (normed * gain).astype(BF16)
    if not last:
        scaled_ref[...] = scaled
    cot = cot_ref[...].reshape(flat)
    value = middle
    mid_back = jnp.zeros(flat, F32)
    for n, weight in enumerate(weights):
        units = weight.shape[0] * weight.shape[2]
        columns = pl.ds(n * units, units)
        gate_t, up_t, down = (weight[:, m].reshape(units, width) for m in range(3))
        gate_pre = times_transpose(scaled, gate_t)
        up_values = times_transpose(scaled, up_t)
        grad_hidden = times_transpose(cot, down)
        sigmoid = 1.0 / (1.0 + jnp.exp(-gate_pre))
        silu = gate_pre * sigmoid
        hidden = (silu * up_values).astype(BF16)
        gate_back = (
            grad_hidden * up_values * (sigmoid * (1.0 + gate_pre * (1.0 - sigmoid)))
        ).astype(BF16)
        up_back = (grad_hidden * silu).astype(BF16)
        if last:
            sums = [
                contract_rows(gate_back, scaled),
                contract_rows(up_back, scaled),
                contract_rows(hidden, cot),
            ]
            for e in range(earlier):
                *parts, right, right_cot = saved[5 * e : 5 * e + 5]
                right_cot = right_cot[...].reshape(-1, width)
                for m, part in enumerate(parts):
                    sums[m] += contract_rows(
                        part[:, columns], right_cot if m == 2 else right[...]
                    )
            for m in range(3):
                split = (weight.shape[0], weight.shape[2], width)
                sum_refs[n][:, m] = sums[m].astype(sum_refs[n].dtype).reshape(split)
        else:
            hidden_ref[:, columns] = hidden
            gate_ref[:, columns] = gate_back
            up_ref[:, columns] = up_back
        value = value + dot(hidden, down)
        mid_back = mid_back + (dot(gate_back, gate_t) + dot(up_back, up_t))
    block[...] = value.astype(BF16).reshape(shape)
    gain_out[...] = jnp.sum(mid_back * normed, axis=0, keepdims=True)
    total = cot.astype(F32) + norm_backward(mid_back, normed, factor, gain)
    grad[...] = total.reshape(shape)
    rounded = total.astype(BF16).reshape(shape)
    for i in range(low.shape[0]):
        low[i] = rounded


def mixing_kernel(
    bit_ref, flip_ref, plus_ref, minus_ref, sum_ref, rest_ref, stay_ref, away_ref, gain_ref
):
    rows = stay_ref.shape[1]

    @pl.when(pl.program_id(0) == 0)
    def _():
        gain_ref[...] = jnp.zeros_like(gain_ref)

    for n, out_ref in enumerate((stay_ref, away_ref)):
        here = pl.ds(pl.multiple_of((bit_ref[0] ^ n) * rows, rows), rows)
        plus, minus = (
            sum(dot(flip_ref[s, here, :], ref[s]) for s in range(flip_ref.shape[0]))
            for ref in (plus_ref, minus_ref)
        )
        out_ref[0] = (plus + minus).astype(out_ref.dtype)
        out_ref[1] = (plus - minus).astype(out_ref.dtype)
        gain_ref[here, :] += jnp.sum(
            plus * sum_ref[0, here, :].astype(F32) + minus * rest_ref[0, here, :].astype(F32),
            axis=1,
            keepdims=True,
        )


def resident(shape):
    zeros = (0,) * len(shape)
    return pl.BlockSpec(shape, lambda *_: zeros, pipeline_mode=pl.Buffered(1))


def mix_sequences(pieces, near, pairs, t00, t10, start, total, flips):
    parts = len(pieces)
    fars, count, _, height, width = pieces[0].shape
    half = t00.shape[1]
    slots = pairs[0].shape[0] // 2
    block = pl.BlockSpec((fars, 1, 2, height, width), lambda n, *_: (0, n, 0, 0, 0))
    pair_specs = [
        pl.BlockSpec((1, width, width), lambda n, q, *_, pm=pm: (pm + jnp.minimum(q, slots - 1), 0, 0))
        for pm in (0, slots)
    ] + [
        pl.BlockSpec((1, width, width), lambda n, q, *_, pm=pm: (pm + jnp.maximum(q - slots, 0), 0, 0))
        for pm in (0, slots)
    ]
    line = pl.BlockSpec((2, half, 2 * half), lambda n, q, *_: (0, 0, q))
    flip = pl.BlockSpec((1, width, 4 * half), lambda n, *_: (start + n, 0, 0))
    return pl.pallas_call(
        functools.partial(mix_kernel, parts),
        grid_spec=pltpu.PrefetchScalarGridSpec(
            num_scalar_prefetch=1,
            grid=(count, 2 * slots),
            in_specs=[block] * parts
            + [*pair_specs, line, line]
            + [pl.BlockSpec(memory_space=pl.ANY)] * len(flips),
            out_specs=[block] * parts + [flip],
            scratch_shapes=[
                pltpu.VMEM((4 * half, width), BF16),
                pltpu.VMEM((2, 2 * half, width), BF16),
                pltpu.VMEM((2, 2 * half, width), BF16),
                pltpu.VMEM((4 * half, width), F32),
            ],
        ),
        out_shape=[jax.ShapeDtypeStruct(pieces[0].shape, BF16)] * parts
        + [jax.ShapeDtypeStruct((total, width, 4 * half), BF16)],
        input_output_aliases={parts + 7: parts} if flips else {},
        compiler_params=pltpu.CompilerParams(vmem_limit_bytes=48 << 20),
        cost_estimate=pl.CostEstimate(
            flops=count * (16 * half * pairs[0].size + 12 * half * t00.shape[2] * width),
            bytes_accessed=4 * parts * pieces[0].size + 4 * pairs[0].size + 4 * t00.size,
            transcendentals=0,
        ),
        name="mix",
    )(near, *pieces, pairs[0], pairs[0], pairs[1], pairs[1], t00, t10, *flips)


def mix_sequences_back(pieces, near, own, turned, u00, u10, lag_count, start, flips, before):
    parts = len(pieces)
    fars, count, _, height, width = pieces[0].shape
    half = u00.shape[2]
    block = pl.BlockSpec((fars, 1, 2, height, width), lambda n, *_: (0, n, 0, 0, 0))
    rows = u00.shape[1]
    slab = 2 * width // (parts * fars)
    lag_shape = (lag_count, slab, width)
    back_shape = (flips.shape[0], 4 * half, 2 * turned[0].shape[0])
    slots = turned[0].shape[0] // width // 2
    back = pl.BlockSpec((1, 4 * half, 2 * width), lambda n, q, *_: (start + n, 0, q))
    slab_spec = pl.BlockSpec((1, slab, 4 * half), lambda n, q, _, own: (start + n, own[0], 0))
    turned_specs = [
        pl.BlockSpec((2 * width, width), lambda n, q, *_: (jnp.minimum(q, slots - 1), 0)),
        pl.BlockSpec((2 * width, width), lambda n, q, *_: (jnp.maximum(q - slots, 0), 0)),
    ]
    line = pl.BlockSpec((2, 2 * half, half), lambda n, q, *_: (0, q, 0))
    return pl.pallas_call(
        functools.partial(mix_back_kernel, parts),
        grid_spec=pltpu.PrefetchScalarGridSpec(
            num_scalar_prefetch=2,
            grid=(count, 2 * slots),
            in_specs=[block] * parts
            + [*turned_specs, line, line, slab_spec]
            + ([pl.BlockSpec(memory_space=pl.ANY), resident(lag_shape)] if before else []),
            out_specs=[block] * parts + [back, resident(lag_shape)],
            scratch_shapes=[
                pltpu.VMEM((4 * half, width), BF16),
                pltpu.VMEM((4 * half, width), F32),
            ],
        ),
        out_shape=[jax.ShapeDtypeStruct(pieces[0].shape, BF16)] * parts
        + [
            jax.ShapeDtypeStruct(back_shape, BF16),
            jax.ShapeDtypeStruct(lag_shape, F32),
        ],
        input_output_aliases={parts + 7: parts} if before else {},
        compiler_params=pltpu.CompilerParams(vmem_limit_bytes=56 << 20),
        cost_estimate=pl.CostEstimate(
            flops=count * (16 * half * turned[0].size + 12 * half * rows * width),
            bytes_accessed=4 * parts * pieces[0].size + 8 * turned[0].size,
            transcendentals=0,
        ),
        name="mix_back",
    )(near, own, *pieces, *turned, u00, u10, flips, *before)


def mixing_products(flips, backs, pairs, bit, set_of):
    count, width, length = flips.shape
    slots = pairs.shape[0] // 2
    plus = pl.BlockSpec((count, length, width), lambda k, _: (0, 0, 2 * (set_of * slots + k)))
    minus = pl.BlockSpec(
        (count, length, width), lambda k, _: (0, 0, 2 * (set_of * slots + k) + 1)
    )
    pair = pl.BlockSpec((1, width, width), lambda k, _: (k, 0, 0))
    rest = pl.BlockSpec((1, width, width), lambda k, _: (slots + k, 0, 0))
    half = pl.BlockSpec((2, width // 2, width), lambda k, _: (k, 0, 0))
    return pl.pallas_call(
        mixing_kernel,
        grid_spec=pltpu.PrefetchScalarGridSpec(
            num_scalar_prefetch=1,
            grid=(slots,),
            in_specs=[resident(flips.shape), plus, minus, pair, rest],
            out_specs=[half, half, resident((width, 1))],
        ),
        out_shape=[
            jax.ShapeDtypeStruct((2 * slots, width // 2, width), F32),
            jax.ShapeDtypeStruct((2 * slots, width // 2, width), BF16),
            jax.ShapeDtypeStruct((width, 1), F32),
        ],
        compiler_params=pltpu.CompilerParams(vmem_limit_bytes=56 << 20),
        cost_estimate=pl.CostEstimate(
            flops=backs.size * width,
            bytes_accessed=2 * flips.size + backs.size + 8 * slots * width * width,
            transcendentals=0,
        ),
        name="mixing_products",
    )(bit, flips, backs, backs, pairs, pairs)


def feed_forward(arrived, inputs, states, late, lag, gain, cot, weights, saved, last):
    rows, width = inputs.size // inputs.shape[-1], inputs.shape[-1]
    shares = len(weights)
    units = weights[0].shape[0] * weights[0].shape[2]
    flat_saved = [value for values in saved for value in values] if last else []
    operands = (arrived, inputs, states, late, lag, gain, cot, *weights, *flat_saved)
    whole = pl.BlockSpec(memory_space=pltpu.VMEM)
    if last:
        extra = [
            jax.ShapeDtypeStruct(weights[0].shape, F32 if n < shares // 2 else BF16)
            for n in range(shares)
        ]
    else:
        extra = [jax.ShapeDtypeStruct((rows, width), BF16)] + [
            jax.ShapeDtypeStruct((rows, shares * units), BF16)
        ] * 3
    return pl.pallas_call(
        functools.partial(feed_forward_kernel, shares, len(flat_saved) // 5, last),
        in_specs=[whole] * len(operands),
        out_specs=[whole] * (4 + len(extra)),
        out_shape=[
            jax.ShapeDtypeStruct(inputs.shape, BF16),
            jax.ShapeDtypeStruct(inputs.shape, F32),
            jax.ShapeDtypeStruct(arrived.shape, BF16),
            jax.ShapeDtypeStruct((1, width), F32),
            *extra,
        ],
        compiler_params=pltpu.CompilerParams(vmem_limit_bytes=56 << 20),
        cost_estimate=pl.CostEstimate(
            flops=(24 if last else 12) * rows * width * shares * units,
            bytes_accessed=6 * shares * units * width + 40 * rows * width,
            transcendentals=rows * shares * units,
        ),
        name="feed_forward",
    )(*operands)


def leading(values, edge):
    early = jnp.concatenate([values[:, :, 1:], edge], axis=2)
    return values, jnp.stack([values[:, 1], early[:, 0]], axis=1), early


def shards(inputs, filters, gain_in, mixing, regression, gain_mid, w_gate, w_up, w_down, out_grad):
    shard_rows, local_seqs, width = inputs.shape
    grid = Grid(lax.axis_size("filt"))
    row_count = lax.axis_size("rows")
    row_index = lax.axis_index("rows")
    bits = row_bits()
    index = lax.axis_index("filt")
    branches = mixing.shape[0]
    lag_count = regression.shape[0]
    height = shard_rows // 2
    chunks = CHUNKS
    step = local_seqs // chunks
    own_seqs = step // 2
    block = (own_seqs, 2, height, width)

    def inward(values):
        return values.reshape(height, 2, local_seqs, width).transpose(2, 1, 0, 3)

    def outward(values):
        return values.transpose(2, 1, 0, 3).reshape(shard_rows, local_seqs, width)

    def cut(values):
        return [values[c * step : (c + 1) * step] for c in range(chunks)]

    def to_mate(part):
        keep, away = grid.split(part.reshape(2, *block), grid.mate)
        return keep, grid.swap(away, grid.mate)

    def to_far(keep, received):
        pair = grid.join(keep, received, grid.mate)
        return pair, grid.swap(pair, grid.far)

    def to_near(pair, received):
        quad = grid.join(pair, received, grid.far).reshape(4, *block)
        return quad, near_swaps(grid, quad)

    def from_near(partial, received):
        total = total_of([partial[0], *received]).reshape(2, 2, *block)
        keep, away = grid.split(total, grid.far)
        return keep, away.astype(BF16)

    def from_far(keep, received):
        return grid.split((keep + received.astype(F32)).astype(BF16), grid.mate)

    def from_mate(keep, received):
        return grid.join(keep, received, grid.mate).reshape(step, 2, height, width)

    inputs_low = inward(inputs)
    residual = inputs_low.astype(F32)
    factor_in = rms_factor(residual)
    normed_in = residual * factor_in
    states = (normed_in * gain_in).astype(BF16)
    mates = [to_mate(part) for part in cut(states)]

    slots = (branches + 1) // 2
    first_branch = index * branches
    if branches % 2:
        odd_start = first_branch % 2
        paired = lax.dynamic_update_slice_in_dim(
            jnp.zeros((2 * slots,) + mixing.shape[1:], mixing.dtype), mixing, odd_start, 0
        )
    else:
        paired = mixing
    paired = tie(paired, mates[0][0])
    first, second = (paired[n::2].astype(F32) for n in range(2))
    own_pairs = jnp.concatenate([first + second, first - second], axis=0).astype(BF16)
    part_rows = width // row_count
    start = sum(
        jnp.where((row_index & bit) != 0, width >> (n + 1), 0) for n, bit in enumerate(bits)
    )
    own_part = lax.dynamic_slice_in_dim(own_pairs, start, part_rows, 1)
    hidden_own = w_down.shape[0]
    share = hidden_own // row_count
    w_gate, w_up, w_down = tie_all([w_gate, w_up, w_down], mates[0][0])
    packed = jnp.stack([w_gate.T, w_up.T, w_down])
    *early_bits, last_bit = grid.spread_bits()
    start = sum(
        jnp.where((row_index & bit) != 0, hidden_own >> (n + 1), 0) for n, bit in enumerate(bits)
    )
    shares = lax.dynamic_slice_in_dim(packed, start, share, 1)
    shares = grid.join(shares, grid.swap(shares, early_bits[0]), early_bits[0])
    mates = [(keep, tie(received, own_part)) for keep, received in mates]
    mate_part = grid.swap(tie(own_part, *(received for _, received in mates)), grid.mate)
    fars = [to_far(*values) for values in mates]
    received = [received for _, received in fars]
    edge = lax.ppermute(
        tie(states[:, :, -1:], *(pair for pair, _ in fars)),
        "filt",
        [(f, f + 1) for f in range(grid.size - 1)],
    )
    t00, t10, u00, u10 = toeplitz_blocks(
        tie(filters, *(pair for pair, _ in fars)),
        [first_branch // 2, (index ^ grid.mate) * branches // 2],
        slots,
    )
    mate_part, edge = tie_all([mate_part, edge], t00, received[0])
    mate_part = tie(mate_part, edge)
    for bit in early_bits[1:]:
        shares = tie(shares, mate_part)
        shares = grid.join(shares, grid.swap(shares, bit), bit)
    quads = [to_near(*values) for values in fars]
    mate_pairs = gather_rows(
        mate_part, [shares, *(value for _, values in quads for value in values)]
    )
    pairs = [own_pairs, mate_pairs]
    cotangent_low = inward(tie(out_grad, *received))

    near = jnp.reshape(index % grid.near, (1,)).astype(jnp.int32)
    late = jnp.concatenate([edge, states[:, :, :-1]], axis=2)
    quads[0] = (quads[0][0], tie_all(quads[0][1], *quads[-1][1]))
    late, inputs_low, cotangent_low, shares, *pieces = tied(
        late, inputs_low, cotangent_low, shares, quads[0][0], *quads[0][1]
    )

    partials, flips, near_received = [], [], []
    received = grid.swap(shares, last_bit)
    for c in range(chunks):
        if c:
            pieces = [quads[c][0], *quads[c][1]]
        *partial, flip = mix_sequences(
            pieces, near, pairs, t00, t10, c * own_seqs, chunks * own_seqs, flips
        )
        if c == 0:
            received = tie(received, partial[0])
            shares = grid.join(shares, received, last_bit)
        else:
            near_received[-1] = tie_all(near_received[-1], partial[0])
            partial = tie_all(partial, *near_received[-1])
        partials.append(partial)
        near_received.append(near_swaps(grid, partial))
        flips = [flip]
    kept_sums, from_fars, turned = [], [], []
    for c in range(chunks):
        kept_sums.append(from_near(partials[c], near_received[c]))
        from_fars.append(grid.swap(kept_sums[c][1], grid.far))
        if c == 0:
            turned = [
                value.reshape(2, slots, width, width)
                .transpose(1, 0, 3, 2)
                .reshape(2 * slots * width, width)
                for value in tie_all(pairs, kept_sums[0][1])
            ]
            from_fars[0] = tie(from_fars[0], *turned, *near_received[1])
    weights = [shares.reshape(grid.size, 3, share, width)]
    for n, bit in enumerate(reversed(bits)):
        received = [swap_rows(weight, bit) for weight in weights]
        if n == 0:
            received = tie_all(received, from_fars[0])
        weights = weights + received

    block_out, middle_grad, lows, fars, kept = [], [], [], [], []
    gain_mid_part = jnp.zeros((1, width), F32)
    for c in range(chunks):
        part = slice(c * step, (c + 1) * step)
        keep, away = from_far(kept_sums[c][0], from_fars[c])
        arrived = from_mate(keep, grid.swap(away, grid.mate))
        if c:
            arrived = tie(arrived, fars[-1][0])
        if c + 1 < chunks:
            arrived = tie(arrived, kept_sums[c + 1][1])
        cot = cotangent_low[part]
        value, grad, low, gain_part, *rest = feed_forward(
            arrived[None], inputs_low[part], states[part], late[part], regression,
            gain_mid[None], cot, weights, kept, c + 1 == chunks,
        )
        block_out.append(value)
        middle_grad.append(grad)
        gain_mid_part = gain_mid_part + gain_part
        if c + 1 < chunks:
            from_fars[c + 1] = tie(from_fars[c + 1], grad)
            low = tie(low, from_fars[c + 1])
        if c:
            fars[-1] = (fars[-1][0], tie(fars[-1][1], grad))
            low, *rest = tie_all([low, *rest], fars[-1][1])
        lows.append(low[0])
        fars.append(to_far(*to_mate(low[0])))
        if c + 1 < chunks:
            scaled, hidden, gate_back, up_back = rest
            kept.append((gate_back, up_back, hidden, scaled, cot))
    gain_mid_part = gain_mid_part[0]

    quads = [to_near(*values) for values in fars]

    half_count = len(rest) // 2
    values = [swap_rows(away, bits[0]) for away in rest[half_count:]]
    values = tie_all(values, *quads[0][1])
    sums_of = [[stay, value] for stay, value in zip(rest[:half_count], values, strict=True)]

    group = index // grid.far * grid.near + index % grid.near
    own = jnp.reshape(group, (1,)).astype(jnp.int32)
    before = ()
    back_partials, near_received = [], []
    mix_back = jnp.concatenate(lows, axis=0)
    next_edge = lax.ppermute(
        mix_back[:, :, :1], "filt", [(f + 1, f) for f in range(grid.size - 1)]
    )
    for bit in bits[1:-1]:
        half_count = len(sums_of) // 2
        values = [swap_rows(total_of(v).astype(BF16), bit) for v in sums_of[half_count:]]
        sums_of = [[*v, value] for v, value in zip(sums_of[:half_count], values, strict=True)]
    parts, away = sums_of
    half_count = away[0].shape[0] // 2
    away = total_of(away).astype(BF16)
    away = [away[:half_count], away[half_count:]]
    from_rows = [swap_rows(away[0], bits[-1])]
    first_quad, next_edge = tie_all([quads[0][0], next_edge], *away)
    quads[0] = (first_quad, quads[0][1])
    for c in range(chunks):
        quad, received = quads[c]
        if c + 1 < chunks:
            quad = tie(quad, quads[c + 1][0])
        *partial, backs, lag_sum = mix_sequences_back(
            [quad, *received], near, own, turned, u00, u10, lag_count, c * own_seqs, flip, before
        )
        before = (backs, lag_sum)
        if c + 1 < chunks:
            later_received = tie_all(quads[c + 1][1], partial[0])
            quads[c + 1] = (quads[c + 1][0], later_received)
            from_rows = [
                tie(from_rows[0], partial[0]), swap_rows(tie(away[1], partial[0]), bits[-1])
            ]
            partial = tie_all(partial, *later_received, from_rows[0])
        if c:
            near_received[-1] = tie_all(near_received[-1], partial[0])
            from_rows[-1] = tie(from_rows[-1], partial[0])
            lag_sum, backs, *partial = tie_all(
                [lag_sum, backs, *partial], *near_received[-1], from_rows[-1]
            )
        back_partials.append(partial)
        near_received.append(near_swaps(grid, partial))
    sums = [from_near(back_partials[0], near_received[0])]
    kept, value = row_step(tie(lag_sum, sums[0][1]), bits[0])
    lag_share = kept + value.astype(F32)
    kept, value = row_step(lag_share, bits[1])
    core_bit = jnp.reshape(row_index & 1, (1,)).astype(jnp.int32)
    mate_stay, mate_away, mate_gain = mixing_products(
        flip, tie(backs, sums[0][1], kept), mate_pairs, core_bit, 1
    )
    from_fars = [tie(grid.swap(sums[0][1], grid.far), mate_gain)]
    mate_stay, mate_away, mate_gain = tie_all([mate_stay, mate_away, mate_gain], from_fars[0])
    lag_share = kept + tie(value, mate_gain).astype(F32)
    for bit in bits[2:]:
        kept, value = row_step(lag_share, bit)
        lag_share = kept + value.astype(F32)
    lag_rows = lag_share.shape[1] // 2
    lag_share, lag_away = grid.split(
        lag_share.reshape(lag_count, 2, lag_rows, width).transpose(1, 0, 2, 3), grid.mate
    )
    lag_away = lag_away.astype(BF16)
    mate_sends = [from_far(sums[0][0], from_fars[0])]
    mate_share = mate_stay + swap_rows(mate_away, bits[0]).astype(F32)
    for c in range(1, chunks):
        sums.append(from_near(back_partials[c], tie_all(near_received[c], mate_gain)))
        from_fars.append(grid.swap(sums[c][1], grid.far))
    twos = (2,) * len(grid.spread_bits())
    grads = jnp.concatenate(
        [
            total_of([*(part[n * half_count : (n + 1) * half_count] for part in parts), value])
            for n, value in enumerate(tie_all(from_rows, mate_gain))
        ]
    ).reshape(*twos, 3, share, width)
    last_bits = grid.spread_bits()[::-1]
    grads, away = grid.split(grads, last_bits[0])
    away = away.astype(BF16)
    mate_kept, mate_away = row_halves(mate_share, bits[1])
    own_stay, own_away, own_gain = mixing_products(
        flip,
        tie(backs, mate_away, mate_sends[0][1], away, lag_away, *(v for _, v in sums[1:])),
        own_pairs, core_bit, 0,
    )
    from_mates = [tie(grid.swap(mate_sends[0][1], grid.mate), own_gain)]
    value = tie(swap_rows(mate_away, bits[1]), own_gain)
    mate_share = mate_kept + value.astype(F32)
    for bit in bits[2:]:
        kept, value = row_step(mate_share, bit)
        mate_share = kept + value.astype(F32)
    from_fars[1:] = tie_all(from_fars[1:], own_gain)
    own_gain = tie(own_gain, value, *from_mates, *from_fars[1:])
    grads = grads + tie(grid.swap(away, last_bits[0]), own_gain).astype(F32)
    lag_share = lag_share + tie(grid.swap(lag_away, grid.mate), own_gain).astype(F32)
    own_stay, own_away = tie_all([own_stay, own_away], own_gain)
    own_share = own_stay + swap_rows(own_away, bits[0]).astype(F32)
    for bit in bits[1:]:
        kept, value = row_step(own_share, bit)
        own_share = kept + value.astype(F32)
    received = grid.swap(mate_share.astype(BF16), grid.mate)
    mixing_low = (own_share + received.astype(F32)).astype(BF16)
    lag_share, mix_back, next_edge, grads, *block_out = tie_all(
        [lag_share, mix_back, next_edge, grads, *block_out], mixing_low
    )
    gain_column = mate_gain + own_gain
    for c in range(1, chunks):
        mate_sends.append(from_far(sums[c][0], from_fars[c]))
    from_mates += [grid.swap(away, grid.mate) for _, away in mate_sends[1:]]
    state_back = [
        from_mate(keep, received).astype(F32)
        for (keep, _), received in zip(mate_sends, from_mates, strict=True)
    ]
    mixing_grad = gather_rows(mixing_low).astype(F32)
    if branches % 2:
        mixing_grad = lax.dynamic_slice_in_dim(mixing_grad, odd_start, branches, 0)

    slab = width // grid.size * 2
    own_regression = lax.dynamic_slice_in_dim(regression, group * slab, slab, 1)
    gain_lag = jnp.sum(own_regression.astype(F32) * lag_sum, axis=(0, 2))
    gain_in_part = gain_column[:, 0]
    gain_in_part = lax.dynamic_update_slice_in_dim(
        gain_in_part,
        lax.dynamic_slice_in_dim(gain_in_part, group * slab, slab, 0) + gain_lag,
        group * slab,
        0,
    ) / gain_in
    gains = pair_sum(
        jnp.pad(jnp.stack([gain_in_part, gain_mid_part]), ((0, 6), (0, 0))), "rows"
    )
    gains = pair_sum(tie(gains, mixing_low), "filt")

    own_grads = reduce_filt(grid, grads, last_bits[1:]).astype(BF16)

    spread = gather_filt(grid, lag_share.astype(BF16))
    spread = (
        spread.reshape(grid.near, 2, 2, lag_count, lag_rows, width)
        .transpose(2, 0, 3, 1, 4, 5)
        .reshape(2 * grid.near * lag_count, 2 * lag_rows, width)
    )
    regression_grad = (
        gather_rows(spread)
        .reshape(2 * grid.near, lag_count, slab, width)
        .transpose(1, 0, 2, 3)
        .reshape(lag_count, width, width)
        .astype(F32)
    )

    lag_back = sum(
        jnp.einsum("spae,de->spad", lead, regression[n], preferred_element_type=F32)
        for n, lead in enumerate(leading(mix_back, next_edge))
    )
    input_grad = []
    for c in range(chunks):
        part = slice(c * step, (c + 1) * step)
        back = state_back[c] + lag_back[part]
        input_grad.append(
            middle_grad[c] + norm_backward(back, normed_in[part], factor_in[part], gain_in)
        )

    ordered = gather_rows(own_grads).astype(F32)
    return (
        outward(jnp.concatenate(block_out, axis=0)),
        outward(jnp.concatenate(input_grad, axis=0)),
        mixing_grad,
        regression_grad,
        gains[0],
        gains[1],
        ordered[0].T,
        ordered[1].T,
        ordered[2],
    )


def solution(mesh):
    placed = (
        P("filt", "rows", None),
        P(),
        P(),
        P("filt", None, None),
        P(),
        P(),
        P(None, "filt"),
        P(None, "filt"),
        P("filt", None),
        P("filt", "rows", None),
    )
    return jax.shard_map(
        shards,
        mesh=mesh,
        in_specs=placed,
        out_specs=(
            P("filt", "rows", None),
            P("filt", "rows", None),
            P("filt", None, None),
            P(),
            P(),
            P(),
            P(None, "filt"),
            P(None, "filt"),
            P("filt", None),
        ),
        check_vma=False,
    )
```
